256 devices in a mesh: row: 8 (over y, core), col: 32 (over x, z).
Axes of the slice: x: 4, y: 4, z: 8, core: 2. Of those that a mesh axis runs over, the one named last changes fastest.
Arguments:
- tokens: bfloat16 [16384, 3072], P(('row', 'col')), may hold values from -6 to 6
- w_in: bfloat16 [3072, 12288], P('row', 'col'), may hold values from -0.109375 to 0.109375
- b_in: float32 [12288], P('col'), may hold values from -3 to 3
- conv_taps: float32 [27, 12288], P(None, 'col'), may hold values from -1.25 to 1.25
- conv_bias: float32 [12288], P('col'), may hold values from -3 to 3
- w_out: bfloat16 [12288, 3072], P('col', 'row'), may hold values from -0.0546875 to 0.0546875
- b_out: float32 [3072], replicated, may hold values from -3 to 3
Outputs:
- mixed: bfloat16 [16384, 3072], P(('row', 'col'))
The draws below stay inside these ranges and needn't reach their ends.
All inputs are finite; a program needn't handle non-finite values.
Results may differ from the reference program's by a relative error of at most 0.0053.
Values may be sent and summed in bfloat16 or wider, within the bound.
A program may use at most 128 MiB of HBM per device.

```python
import jax
import jax.numpy as jnp

D = 3072
FF = 12288
HH = 32
WW = 32
FRAMES = 16
TOKENS = 16384


def steps_of(rng, shape, cuts, low, largest):
    loudness, own = 1.0, jax.random.fold_in(rng, 6)
    for axis_at, shards_of in cuts:
        steps = jnp.exp(jax.random.uniform(jax.random.fold_in(own, axis_at), (shards_of,), jnp.float32, low / len(cuts), largest / len(cuts)))
        loudness = loudness * jnp.repeat(steps, shape[axis_at] // shards_of).reshape([-1 if axis == axis_at else 1 for axis in range(len(shape))])
    return loudness


def scatter_about(stream_key, extent, spread, limit, shards=(), held_as=jnp.bfloat16):
    values = spread * jax.random.normal(stream_key, extent, jnp.float32)
    if shards:
        values = values * steps_of(stream_key, extent, shards, -0.22, 0.18)
    return jnp.clip(values, -limit, limit).astype(held_as)


def setup_inputs(seed: int = 0) -> dict:
    keys = jax.random.split(jax.random.key(seed), 8)
    return {
        "tokens": scatter_about(keys[0], (TOKENS, D), 1.0, 6.0, ((0, 256),)),
        "w_in": scatter_about(keys[1], (D, FF), D ** -0.5, 0.109375, ((0, 8), (1, 32))),
        "b_in": scatter_about(keys[2], (FF,), 0.5, 3.0, ((0, 32),), jnp.float32),
        "conv_taps": scatter_about(keys[3], (27, FF), 27 ** -0.5, 1.25, ((1, 32),), jnp.float32),
        "conv_bias": scatter_about(keys[4], (FF,), 0.5, 3.0, ((0, 32),), jnp.float32),
        "w_out": scatter_about(keys[5], (FF, D), FF ** -0.5, 0.0546875, ((0, 32), (1, 8))),
        "b_out": scatter_about(keys[6], (D,), 0.5, 3.0, (), jnp.float32),
    }


def reference(tokens, w_in, b_in, conv_taps, conv_bias, w_out, b_out):
    before = jnp.dot(tokens, w_in, preferred_element_type=jnp.float32) + b_in
    hidden = before.astype(jnp.bfloat16).reshape(FRAMES, HH, WW, FF)
    padded = jnp.pad(hidden, ((1, 1), (1, 1), (1, 1), (0, 0)))
    summed = jnp.zeros((FRAMES, HH, WW, FF), jnp.float32)
    for offset in range(27):
        shift_t = offset // 9
        shift_h = (offset // 3) % 3
        shift_w = offset % 3
        window = padded[shift_t:shift_t + FRAMES, shift_h:shift_h + HH, shift_w:shift_w + WW, :]
        summed = summed + window.astype(jnp.float32) * conv_taps[offset]
    activated = jax.nn.gelu(summed + conv_bias, approximate=True).astype(jnp.bfloat16)
    activated = activated.reshape(TOKENS, FF)
    result = jnp.dot(activated, w_out, preferred_element_type=jnp.float32) + b_out
    return result.astype(jnp.bfloat16)
```

```python
import functools

import jax
import jax.numpy as jnp
from jax import lax
from jax.experimental import pallas as pl
from jax.experimental.pallas import tpu as pltpu
from jax.sharding import PartitionSpec as P

MESH = pl.DeviceIdType.MESH
NX, NY, NZ = 4, 4, 8
D = 3072
BLK = 384
HALF = BLK // 2
CH = NX * BLK
GROUP = 512
OWN = 64
WW = 32
ROWS = GROUP // WW
HALO_CHUNKS = 3
HALO_CH = CH // HALO_CHUNKS
BF16, F32 = jnp.bfloat16, jnp.float32


def place():
    row, col = lax.axis_index("row"), lax.axis_index("col")
    return row // 2, row % 2, col // NZ, col % NZ


def dev(y, c, x, z):
    return {"row": y * 2 + c, "col": x * NZ + z}


def moved_to(y, c, x):
    b = c ^ (y & 1)
    upper = x & 1
    return x >> 1, jnp.where(upper == 0, b, 3 - b)


def moved_from(y, c, x):
    b = (x ^ (x >> 1)) & 1
    return b ^ (y & 1), c * 2 + (x >> 1)


def frame_of(y, c, x):
    b = (x ^ (x >> 1)) & 1
    return 4 * y + 2 * (b ^ (y & 1)) + c


def holder(frame, upper):
    pair = frame >> 1
    y = pair >> 1
    b = (pair & 1) ^ (y & 1)
    return y, frame & 1, jnp.where(upper == 0, b, 3 - b)


class Sender:
    def __init__(self, ssem, rsem):
        self.ssem, self.rsem, self.used, self.sent = ssem, rsem, 0, []

    def key(self):
        self.used += 1
        return self.used - 1

    def make(self, src, dst, k, to):
        return pltpu.make_async_remote_copy(
            src_ref=src,
            dst_ref=dst,
            send_sem=self.ssem.at[k],
            recv_sem=self.rsem.at[k],
            device_id=to,
            device_id_type=MESH,
        )

    def send(self, src, dst, to, when=None):
        k = self.key()
        copy = self.make(src, dst, k, to)
        if when is None:
            copy.start()
        else:
            pl.when(when)(copy.start)
        self.sent.append((copy, when))
        return k

    def arrived(self, ref, k, when=None):
        copy = pltpu.make_async_copy(ref, ref, self.rsem.at[k])
        if when is None:
            copy.wait()
        else:
            pl.when(when)(copy.wait)

    def drain(self):
        for copy, when in self.sent:
            if when is None:
                copy.wait_send()
            else:
                pl.when(when)(copy.wait_send)
        self.sent = []


def greet(peers):
    barrier = pltpu.get_barrier_semaphore()
    count = 0
    for to, when in peers:
        signal = functools.partial(pl.semaphore_signal, barrier, inc=1, device_id=to, device_id_type=MESH)
        if when is None:
            signal()
            count = count + 1
        else:
            pl.when(when)(signal)
            count = count + when.astype(jnp.int32)
    pl.semaphore_wait(barrier, count)


class WeightGather:
    def __init__(self, sender, own, block, band_a, band_b):
        self.s, self.own = sender, own
        self.block, self.band_a, self.band_b = block, band_a, band_b
        self.y, self.c, self.x, self.z = place()
        self.xp, self.xm = (self.x + 1) % NX, (self.x + NX - 1) % NX
        self.yp, self.ym = (self.y + 1) % NY, (self.y + NY - 1) % NY
        self.x2, self.y2 = (self.x + 2) % NX, (self.y + 2) % NY

    def to_x(self, x):
        return dev(self.y, self.c, x, self.z)

    def to_y(self, y):
        return dev(y, self.c, self.x, self.z)

    def stage1(self):
        s, x, y, own = self.s, self.x, self.y, self.own
        a, b = pl.ds(0, HALF), pl.ds(HALF, HALF)
        self.k_axp = s.send(own.at[a], self.block(x, y, a), self.to_x(self.xp))
        self.k_axm = s.send(own.at[a], self.block(x, y, a), self.to_x(self.xm))
        self.k_byp = s.send(own.at[b], self.block(x, y, b), self.to_y(self.yp))
        self.k_bym = s.send(own.at[b], self.block(x, y, b), self.to_y(self.ym))

    def stage1_forward(self):
        s, q = self.s, HALF // 2
        lo, hi = pl.ds(0, q), pl.ds(q, q)
        s.arrived(self.block(self.xm, self.y, pl.ds(0, HALF)), self.k_axp)
        src = self.block(self.xm, self.y, lo)
        self.k_afp = s.send(src, src, self.to_x(self.xp))
        s.arrived(self.block(self.xp, self.y, pl.ds(0, HALF)), self.k_axm)
        src = self.block(self.xp, self.y, hi)
        self.k_afm = s.send(src, src, self.to_x(self.xm))
        lo, hi = pl.ds(HALF, q), pl.ds(HALF + q, q)
        s.arrived(self.block(self.x, self.ym, pl.ds(HALF, HALF)), self.k_byp)
        src = self.block(self.x, self.ym, lo)
        self.k_bfp = s.send(src, src, self.to_y(self.yp))
        s.arrived(self.block(self.x, self.yp, pl.ds(HALF, HALF)), self.k_bym)
        src = self.block(self.x, self.yp, hi)
        self.k_bfm = s.send(src, src, self.to_y(self.ym))

    def stage2(self):
        s, q = self.s, HALF // 2
        s.arrived(self.block(self.x2, self.y, pl.ds(0, q)), self.k_afp)
        s.arrived(self.block(self.x2, self.y, pl.ds(q, q)), self.k_afm)
        band = self.band_a(self.y, None)
        self.k_ayp = s.send(band, band, self.to_y(self.yp))
        self.k_aym = s.send(band, band, self.to_y(self.ym))
        s.arrived(self.block(self.x, self.y2, pl.ds(HALF, q)), self.k_bfp)
        s.arrived(self.block(self.x, self.y2, pl.ds(HALF + q, q)), self.k_bfm)
        band = self.band_b(self.x, None)
        self.k_bxp = s.send(band, band, self.to_x(self.xp))
        self.k_bxm = s.send(band, band, self.to_x(self.xm))
        self.partner(0, self.y, self.x)

    def partner(self, at, y, x):
        other = dev(self.y, 1 - self.c, self.x, self.z)
        a, b = self.band_a(y, None), self.band_b(x, None)
        ka = self.s.send(a, a, other)
        kb = self.s.send(b, b, other)
        self.from_partner = getattr(self, "from_partner", [])
        self.from_partner.append((ka, kb, y, x))

    def stage2_forward(self):
        s = self.s
        s.arrived(self.band_a(self.ym, None), self.k_ayp)
        src = self.band_a(self.ym, 0)
        self.k_a2p = s.send(src, src, self.to_y(self.yp))
        s.arrived(self.band_a(self.yp, None), self.k_aym)
        src = self.band_a(self.yp, 1)
        self.k_a2m = s.send(src, src, self.to_y(self.ym))
        s.arrived(self.band_b(self.xm, None), self.k_bxp)
        src = self.band_b(self.xm, 0)
        self.k_b2p = s.send(src, src, self.to_x(self.xp))
        s.arrived(self.band_b(self.xp, None), self.k_bxm)
        src = self.band_b(self.xp, 1)
        self.k_b2m = s.send(src, src, self.to_x(self.xm))
        self.partner(1, self.ym, self.xm)
        self.partner(2, self.yp, self.xp)

    def stage3(self):
        s = self.s
        for part, k in ((0, self.k_a2p), (1, self.k_a2m)):
            s.arrived(self.band_a(self.y2, part), k)
        for part, k in ((0, self.k_b2p), (1, self.k_b2m)):
            s.arrived(self.band_b(self.x2, part), k)
        self.partner(3, self.y2, self.x2)

    def finish(self):
        for ka, kb, y, x in self.from_partner:
            self.s.arrived(self.band_a(y, None), ka)
            self.s.arrived(self.band_b(x, None), kb)


def gather_kernel(
    tok_in, win_in, wout_in, par_in, ext_out, wout, par_out, tok, win, ext, par, lsem, ssem, rsem
):
    y, c, x, z = place()
    s = Sender(ssem, rsem)
    xs = [(x + d) % NX for d in range(NX)]
    zp, zm = (z + 1) % NZ, (z + NZ - 1) % NZ
    yp, ym = (y + 1) % NY, (y + NY - 1) % NY
    upper = x >> 1
    frame = frame_of(y, c, x)
    last = NY * 4 - 1
    tc, tx = moved_to(y, c, x)
    fc, fx = moved_from(y, c, x)
    stays = (tc == c) & (tx == x)
    moves = jnp.logical_not(stays)
    has_next, has_prev = frame < last, frame > 0
    ny, nc, nx = holder(jnp.minimum(frame + 1, last), upper)
    py, pc, px = holder(jnp.maximum(frame - 1, 0), upper)
    nxt, nxt_other = dev(ny, nc, nx, z), dev(ny, nc, 3 - nx, z)
    prv, prv_other = dev(py, pc, px, z), dev(py, pc, 3 - px, z)
    other_half = dev(y, c, 3 - x, z)

    greet(
        [(dev(y, c, xs[d], z), None) for d in (1, 2, 3)]
        + [(dev(yp, c, x, z), None), (dev(ym, c, x, z), None)]
        + [(dev(y, c, x, zp), None), (dev(y, c, x, zm), None)]
        + [(dev(y, 1 - c, x, z), None)]
        + [(dev(y, tc, tx, z), moves), (dev(y, fc, fx, z), moves)]
        + [(nxt, has_next), (nxt_other, has_next), (prv, has_prev), (prv_other, has_prev)]
        + [(other_half, None)]
    )

    home = tok.at[pl.ds(z * OWN, OWN)]
    k_move = s.send(tok_in, home, dev(y, tc, tx, z), when=moves)
    stay = pltpu.make_async_copy(tok_in, home, rsem.at[k_move])
    pl.when(stays)(stay.start)

    def par_at(x_):
        return par.at[:, pl.ds(x_ * BLK, BLK)]

    k_par = [s.send(par_in, par_at(x), dev(y, c, xs[d], z)) for d in (1, 2, 3)]
    own_par = pltpu.make_async_copy(par_in, par_at(x), lsem.at[0])
    own_par.start()

    def win_block(x_, y_, rows):
        return win.at[y_, c, rows, pl.ds(x_ * BLK, BLK)]

    def win_a(y_, part):
        cols = pl.ds(0, CH) if part is None else pl.ds(part * (CH // 2), CH // 2)
        return win.at[y_, c, pl.ds(0, HALF), cols]

    def win_b(x_, part):
        ys = pl.ds(0, NY) if part is None else pl.ds(part * 2, 2)
        return win.at[ys, c, pl.ds(HALF, HALF), pl.ds(x_ * BLK, BLK)]

    def wout_block(x_, y_, rows):
        return wout.at[x_, rows, pl.ds(c * (NY * BLK) + y_ * BLK, BLK)]

    def wout_a(y_, part):
        xs_ = pl.ds(0, NX) if part is None else pl.ds(part * 2, 2)
        return wout.at[xs_, pl.ds(0, HALF), pl.ds(c * (NY * BLK) + y_ * BLK, BLK)]

    def wout_b(x_, part):
        n = NY * BLK
        cols = pl.ds(c * n, n) if part is None else pl.ds(c * n + part * (n // 2), n // 2)
        return wout.at[x_, pl.ds(HALF, HALF), cols]

    g_in = WeightGather(s, win_in, win_block, win_a, win_b)
    g_out = WeightGather(s, wout_in, wout_block, wout_a, wout_b)
    own_in = pltpu.make_async_copy(win_in, win_block(x, y, pl.ds(0, BLK)), lsem.at[1])
    own_out = pltpu.make_async_copy(wout_in, wout_block(x, y, pl.ds(0, BLK)), lsem.at[2])
    own_in.start()
    own_out.start()
    g_in.stage1()

    @pl.when(upper == 0)
    def _():
        ext[:, 0] = jnp.zeros((3, WW, CH), BF16)

    @pl.when(upper == 1)
    def _():
        ext[:, ROWS + 1] = jnp.zeros((3, WW, CH), BF16)

    @pl.when(jnp.logical_not(has_prev))
    def _():
        @pl.loop(0, ROWS + 2)
        def _(r):
            ext[0, r] = jnp.zeros((WW, CH), BF16)

    @pl.when(jnp.logical_not(has_next))
    def _():
        @pl.loop(0, ROWS + 2)
        def _(r):
            ext[2, r] = jnp.zeros((WW, CH), BF16)

    piece = OWN // 2

    def tok_at(z_, p):
        return tok.at[pl.ds(((z_ + NZ) % NZ) * OWN + p * piece, piece)]

    k_tok = {}

    def token_step(d):
        for p in (0, 1):
            for way, to in ((1, zp), (-1, zm)):
                if d == 4 and (p == 0) != (way == 1):
                    continue
                src = tok_at(z - way * (d - 1), p)
                if d > 1:
                    s.arrived(src, k_tok[way, d - 1, p])
                k_tok[way, d, p] = s.send(src, src, dev(y, c, x, to))

    stay.wait()
    token_step(1)
    g_in.stage1_forward()
    own_in.wait()
    g_in.stage2()
    token_step(2)
    token_step(3)
    g_in.stage2_forward()
    g_out.stage1()
    own_out.wait()
    token_step(4)
    g_in.stage3()
    g_out.stage1_forward()
    own_par.wait()
    for d in (1, 2, 3):
        s.arrived(par_at((x + NX - d) % NX), k_par[d - 1])
    s.arrived(tok_at(z - 3, 1), k_tok[1, 3, 1])
    s.arrived(tok_at(z + 3, 0), k_tok[-1, 3, 0])
    s.arrived(tok_at(z - 4, 0), k_tok[1, 4, 0])
    s.arrived(tok_at(z + 4, 1), k_tok[-1, 4, 1])
    g_in.finish()

    src_row = jnp.where(upper == 0, ROWS, 1)
    dst_row = jnp.where(upper == 0, 0, ROWS + 1)
    got_row = jnp.where(upper == 0, ROWS + 1, 0)
    inner = pl.ds(1, ROWS)
    arrivals = []
    step = 256
    for j in range(HALO_CHUNKS):

        @pl.loop(0, HALO_CH // step)
        def _(i):
            cols = pl.ds(pl.multiple_of(j * HALO_CH + i * step, step), step)
            w = win[:, :, :, cols].reshape(D, step)
            before = jnp.dot(tok[...], w, preferred_element_type=F32) + par[0:1, cols]
            ext[1, inner, :, cols] = before.astype(BF16).reshape(ROWS, WW, step)

        cols = pl.ds(j * HALO_CH, HALO_CH)
        frame_src = ext.at[1, inner, :, cols]
        row_src = ext.at[1, src_row, :, cols]
        k1 = s.send(frame_src, ext.at[0, inner, :, cols], nxt, when=has_next)
        k2 = s.send(frame_src, ext.at[2, inner, :, cols], prv, when=has_prev)
        k3 = s.send(row_src, ext.at[1, dst_row, :, cols], other_half)
        k4 = s.send(row_src, ext.at[0, dst_row, :, cols], nxt_other, when=has_next)
        k5 = s.send(row_src, ext.at[2, dst_row, :, cols], prv_other, when=has_prev)
        arrivals += [
            (ext.at[0, inner, :, cols], k1, has_prev),
            (ext.at[2, inner, :, cols], k2, has_next),
            (ext.at[1, got_row, :, cols], k3, None),
            (ext.at[0, got_row, :, cols], k4, has_prev),
            (ext.at[2, got_row, :, cols], k5, has_next),
        ]
        if j == 0:
            g_out.stage2()

    par_done = pltpu.make_async_copy(par, par_out, lsem.at[3])
    par_done.start()
    for ref, k, when in arrivals:
        s.arrived(ref, k, when)
    ext_done = pltpu.make_async_copy(ext, ext_out, lsem.at[4])
    ext_done.start()
    g_out.stage2_forward()
    g_out.stage3()
    g_out.finish()
    par_done.wait()
    ext_done.wait()
    s.drain()


def gather(tokens, w_in, w_out, par):
    vmem = pl.BlockSpec(memory_space=pltpu.VMEM)
    hbm = pl.BlockSpec(memory_space=pl.ANY)
    keys = 100
    return pl.pallas_call(
        gather_kernel,
        out_shape=[
            jax.ShapeDtypeStruct((3, ROWS + 2, WW, CH), BF16),
            jax.ShapeDtypeStruct((NX, BLK, D), BF16),
            jax.ShapeDtypeStruct((32, CH), F32),
        ],
        in_specs=[vmem] * 4,
        out_specs=[hbm] * 3,
        scratch_shapes=[
            pltpu.VMEM((GROUP, D), BF16),
            pltpu.VMEM((NY, 2, BLK, CH), BF16),
            pltpu.VMEM((3, ROWS + 2, WW, CH), BF16),
            pltpu.VMEM((32, CH), F32),
            pltpu.SemaphoreType.DMA((8,)),
            pltpu.SemaphoreType.DMA((keys,)),
            pltpu.SemaphoreType.DMA((keys,)),
        ],
        compiler_params=pltpu.CompilerParams(
            collective_id=0, has_side_effects=True, vmem_limit_bytes=48 * 2**20
        ),
        name="gather",
    )(tokens, w_in, w_out, par)


CONV_CH = 256


def conv_kernel(ext, par, w, out, act):
    @pl.when(pl.program_id(0) == 0)
    def _():
        @pl.loop(0, GROUP, step=64)
        def _(r):
            out[pl.ds(r, 64), :] = jnp.zeros((64, D), F32)

    column = lax.broadcasted_iota(jnp.int32, (WW, 128), 0)
    for lc in range(CONV_CH // 128):
        lanes = pl.ds(lc * 128, 128)

        @pl.loop(0, ROWS)
        def _(r):
            sums = [None, None, None]
            for dt in range(3):
                for dh in range(3):
                    v = ext[dt, r + dh, :, lanes].astype(F32)
                    for dw in range(3):
                        t = v * par[1 + 9 * dt + 3 * dh + dw : 2 + 9 * dt + 3 * dh + dw, lanes]
                        sums[dw] = t if sums[dw] is None else sums[dw] + t
            left = jnp.where(column == 0, 0.0, pltpu.roll(sums[0], 1, 0))
            right = jnp.where(column == WW - 1, 0.0, pltpu.roll(sums[2], WW - 1, 0))
            v = sums[1] + left + right + par[28:29, lanes]
            g = 0.5 * v * (1.0 + jnp.tanh(0.7978845608028654 * (v + 0.044715 * v * v * v)))
            act[pl.ds(pl.multiple_of(r * WW, WW), WW), lanes] = g.astype(BF16)

    @pl.loop(0, D // 512)
    def _(n):
        cols = pl.ds(pl.multiple_of(n * 512, 512), 512)
        out[:, cols] += jnp.dot(act[...], w[:, cols], preferred_element_type=F32)


def conv_mlp(ext, par, w_out):
    return pl.pallas_call(
        conv_kernel,
        grid=(CH // CONV_CH,),
        out_shape=jax.ShapeDtypeStruct((GROUP, D), F32),
        in_specs=[
            pl.BlockSpec((3, ROWS + 2, WW, CONV_CH), lambda i: (0, 0, 0, i)),
            pl.BlockSpec((32, CONV_CH), lambda i: (0, i)),
            pl.BlockSpec((CONV_CH, D), lambda i: (i, 0)),
        ],
        out_specs=pl.BlockSpec((GROUP, D), lambda i: (0, 0)),
        scratch_shapes=[pltpu.VMEM((GROUP, CONV_CH), BF16)],
        compiler_params=pltpu.CompilerParams(vmem_limit_bytes=40 * 2**20),
        name="conv_mlp",
    )(ext, par, w_out)


def scatter_kernel(part, bias, out, sendbuf, recvbuf, done, lsem, ssem, rsem):
    y, c, x, z = place()
    s = Sender(ssem, rsem)
    zp, zm = (z + 1) % NZ, (z + NZ - 1) % NZ
    tc, tx = moved_to(y, c, x)
    fc, fx = moved_from(y, c, x)
    stays = (tc == c) & (tx == x)
    moves = jnp.logical_not(stays)
    greet(
        [(dev(y, c, x, zp), None), (dev(y, c, x, zm), None)]
        + [(dev(y, tc, tx, z), moves), (dev(y, fc, fx, z), moves)]
    )
    wide = D // 2
    chains = [(q, way, 4 if (q == 0) == (way == 1) else 3) for q in (0, 1) for way in (1, -1)]
    slot, n = {}, 0
    for i, (q, way, length) in enumerate(chains):
        for step in range(length):
            slot[i, step] = n
            n += 1
    k_of = {}
    for step in range(4):
        for i, (q, way, length) in enumerate(chains):
            if step >= length:
                continue
            at = (z + way * (length - step) + NZ) % NZ
            rows = pl.ds(pl.multiple_of(at * OWN, OWN), OWN)
            value = part[rows, q * wide : (q + 1) * wide]
            if step > 0:
                got = recvbuf.at[slot[i, step - 1]]
                s.arrived(got, k_of[i, step - 1])
                value = value + got[...].astype(F32)
            mine = slot[i, step]
            sendbuf[mine] = value.astype(BF16)
            to = dev(y, c, x, zp if way == 1 else zm)
            k_of[i, step] = s.send(sendbuf.at[mine], recvbuf.at[mine], to)
    rows = pl.ds(pl.multiple_of(z * OWN, OWN), OWN)
    for q in (0, 1):
        value = part[rows, q * wide : (q + 1) * wide]
        for i in (2 * q, 2 * q + 1):
            mine = slot[i, chains[i][2] - 1]
            s.arrived(recvbuf.at[mine], k_of[i, chains[i][2] - 1])
            value = value + recvbuf[mine].astype(F32)
        for y_ in range(NY):
            to = (y_ * 2 + q) * BLK
            done[:, to : to + BLK] = (
                value[:, y_ * BLK : (y_ + 1) * BLK] + bias[:, to : to + BLK]
            ).astype(BF16)
    k = s.send(done, out, dev(y, fc, fx, z), when=moves)
    stay = pltpu.make_async_copy(done, out, rsem.at[k])
    pl.when(stays)(stay.start)
    stay.wait()
    s.drain()


def scatter(part, bias):
    vmem = pl.BlockSpec(memory_space=pltpu.VMEM)
    return pl.pallas_call(
        scatter_kernel,
        out_shape=jax.ShapeDtypeStruct((OWN, D), BF16),
        in_specs=[vmem] * 2,
        out_specs=pl.BlockSpec(memory_space=pl.ANY),
        scratch_shapes=[
            pltpu.VMEM((14, OWN, D // 2), BF16),
            pltpu.VMEM((14, OWN, D // 2), BF16),
            pltpu.VMEM((OWN, D), BF16),
            pltpu.SemaphoreType.DMA((2,)),
            pltpu.SemaphoreType.DMA((16,)),
            pltpu.SemaphoreType.DMA((16,)),
        ],
        compiler_params=pltpu.CompilerParams(
            collective_id=1, has_side_effects=True, vmem_limit_bytes=32 * 2**20
        ),
        name="scatter",
    )(part, bias)


def body(tokens, w_in, b_in, conv_taps, conv_bias, w_out, b_out):
    par = jnp.concatenate([b_in[None], conv_taps, conv_bias[None], jnp.zeros((3, BLK), F32)])
    ext, wide_out, wide_par = gather(tokens, w_in, w_out, par)
    part = conv_mlp(ext, wide_par, wide_out.reshape(CH, D))
    return scatter(part, b_out[None])


def solution(mesh):
    placed = (
        P(("row", "col"), None),
        P("row", "col"),
        P("col"),
        P(None, "col"),
        P("col"),
        P("col", "row"),
        P(),
    )
    return jax.shard_map(
        body, mesh=mesh, in_specs=placed, out_specs=P(("row", "col"), None), check_vma=False
    )
```

```python
import functools

import jax
import jax.numpy as jnp
from jax import lax
from jax.experimental import pallas as pl
from jax.experimental.pallas import tpu as pltpu
from jax.sharding import PartitionSpec as P

MESH = pl.DeviceIdType.MESH
NX, NY, NZ = 4, 4, 8
D = 3072
BLK = 384
HALF = BLK // 2
CH = NX * BLK
GROUP = 512
OWN = 64
WW = 32
ROWS = GROUP // WW
HALO_CHUNKS = 3
PIECES = 4
PIECE = OWN // PIECES
UNIT = 1024
HALO_CH = CH // HALO_CHUNKS
BF16, F32 = jnp.bfloat16, jnp.float32


def place():
    row, col = lax.axis_index("row"), lax.axis_index("col")
    return row // 2, row % 2, col // NZ, col % NZ


def dev(y, c, x, z):
    return {"row": y * 2 + c, "col": x * NZ + z}


def moved_to(y, c, x):
    b = c ^ (y & 1)
    upper = x & 1
    return x >> 1, jnp.where(upper == 0, b, 3 - b)


def moved_from(y, c, x):
    b = (x ^ (x >> 1)) & 1
    return b ^ (y & 1), c * 2 + (x >> 1)


def frame_of(y, c, x):
    b = (x ^ (x >> 1)) & 1
    return 4 * y + 2 * (b ^ (y & 1)) + c


def holder(frame, upper):
    pair = frame >> 1
    y = pair >> 1
    b = (pair & 1) ^ (y & 1)
    return y, frame & 1, jnp.where(upper == 0, b, 3 - b)


class Sender:
    def __init__(self, ssem, rsem):
        self.ssem, self.rsem, self.used, self.sent = ssem, rsem, 0, []

    def key(self):
        self.used += 1
        return self.used - 1

    def make(self, src, dst, k, to):
        return pltpu.make_async_remote_copy(
            src_ref=src,
            dst_ref=dst,
            send_sem=self.ssem.at[k],
            recv_sem=self.rsem.at[k],
            device_id=to,
            device_id_type=MESH,
        )

    def send(self, src, dst, to, when=None):
        k = self.key()
        copy = self.make(src, dst, k, to)
        if when is None:
            copy.start()
        else:
            pl.when(when)(copy.start)
        self.sent.append((copy, when))
        return k

    def arrived(self, ref, k, when=None):
        copy = pltpu.make_async_copy(ref, ref, self.rsem.at[k])
        if when is None:
            copy.wait()
        else:
            pl.when(when)(copy.wait)

    def drain(self):
        for copy, when in self.sent:
            if when is None:
                copy.wait_send()
            else:
                pl.when(when)(copy.wait_send)
        self.sent = []


def greet(peers):
    barrier = pltpu.get_barrier_semaphore()
    count = 0
    for to, when in peers:
        signal = functools.partial(pl.semaphore_signal, barrier, inc=1, device_id=to, device_id_type=MESH)
        if when is None:
            signal()
            count = count + 1
        else:
            pl.when(when)(signal)
            count = count + when.astype(jnp.int32)
    pl.semaphore_wait(barrier, count)


class WeightGather:
    def __init__(self, sender, own, block, band_a, band_b):
        self.s, self.own = sender, own
        self.block, self.band_a, self.band_b = block, band_a, band_b
        self.y, self.c, self.x, self.z = place()
        self.xp, self.xm = (self.x + 1) % NX, (self.x + NX - 1) % NX
        self.yp, self.ym = (self.y + 1) % NY, (self.y + NY - 1) % NY
        self.x2, self.y2 = (self.x + 2) % NX, (self.y + 2) % NY

    def to_x(self, x):
        return dev(self.y, self.c, x, self.z)

    def to_y(self, y):
        return dev(y, self.c, self.x, self.z)

    def stage1(self):
        s, x, y, own = self.s, self.x, self.y, self.own
        a, b = pl.ds(0, HALF), pl.ds(HALF, HALF)
        self.k_axp = s.send(own.at[a], self.block(x, y, a), self.to_x(self.xp))
        self.k_axm = s.send(own.at[a], self.block(x, y, a), self.to_x(self.xm))
        self.k_byp = s.send(own.at[b], self.block(x, y, b), self.to_y(self.yp))
        self.k_bym = s.send(own.at[b], self.block(x, y, b), self.to_y(self.ym))

    def stage1_forward(self):
        s, q = self.s, HALF // 2
        lo, hi = pl.ds(0, q), pl.ds(q, q)
        s.arrived(self.block(self.xm, self.y, pl.ds(0, HALF)), self.k_axp)
        src = self.block(self.xm, self.y, lo)
        self.k_afp = s.send(src, src, self.to_x(self.xp))
        s.arrived(self.block(self.xp, self.y, pl.ds(0, HALF)), self.k_axm)
        src = self.block(self.xp, self.y, hi)
        self.k_afm = s.send(src, src, self.to_x(self.xm))
        lo, hi = pl.ds(HALF, q), pl.ds(HALF + q, q)
        s.arrived(self.block(self.x, self.ym, pl.ds(HALF, HALF)), self.k_byp)
        src = self.block(self.x, self.ym, lo)
        self.k_bfp = s.send(src, src, self.to_y(self.yp))
        s.arrived(self.block(self.x, self.yp, pl.ds(HALF, HALF)), self.k_bym)
        src = self.block(self.x, self.yp, hi)
        self.k_bfm = s.send(src, src, self.to_y(self.ym))

    def stage2(self):
        s, q = self.s, HALF // 2
        s.arrived(self.block(self.x2, self.y, pl.ds(0, q)), self.k_afp)
        s.arrived(self.block(self.x2, self.y, pl.ds(q, q)), self.k_afm)
        band = self.band_a(self.y, None)
        self.k_ayp = s.send(band, band, self.to_y(self.yp))
        self.k_aym = s.send(band, band, self.to_y(self.ym))
        s.arrived(self.block(self.x, self.y2, pl.ds(HALF, q)), self.k_bfp)
        s.arrived(self.block(self.x, self.y2, pl.ds(HALF + q, q)), self.k_bfm)
        band = self.band_b(self.x, None)
        self.k_bxp = s.send(band, band, self.to_x(self.xp))
        self.k_bxm = s.send(band, band, self.to_x(self.xm))
        self.partner(0, self.y, self.x)

    def partner(self, at, y, x):
        other = dev(self.y, 1 - self.c, self.x, self.z)
        a, b = self.band_a(y, None), self.band_b(x, None)
        ka = self.s.send(a, a, other)
        kb = self.s.send(b, b, other)
        self.from_partner = getattr(self, "from_partner", [])
        self.from_partner.append((ka, kb, y, x))

    def stage2_forward(self):
        s = self.s
        s.arrived(self.band_a(self.ym, None), self.k_ayp)
        src = self.band_a(self.ym, 0)
        self.k_a2p = s.send(src, src, self.to_y(self.yp))
        s.arrived(self.band_a(self.yp, None), self.k_aym)
        src = self.band_a(self.yp, 1)
        self.k_a2m = s.send(src, src, self.to_y(self.ym))
        s.arrived(self.band_b(self.xm, None), self.k_bxp)
        src = self.band_b(self.xm, 0)
        self.k_b2p = s.send(src, src, self.to_x(self.xp))
        s.arrived(self.band_b(self.xp, None), self.k_bxm)
        src = self.band_b(self.xp, 1)
        self.k_b2m = s.send(src, src, self.to_x(self.xm))
        self.partner(1, self.ym, self.xm)
        self.partner(2, self.yp, self.xp)

    def stage3(self):
        s = self.s
        for part, k in ((0, self.k_a2p), (1, self.k_a2m)):
            s.arrived(self.band_a(self.y2, part), k)
        for part, k in ((0, self.k_b2p), (1, self.k_b2m)):
            s.arrived(self.band_b(self.x2, part), k)
        self.partner(3, self.y2, self.x2)

    def finish(self):
        for ka, kb, y, x in self.from_partner:
            self.s.arrived(self.band_a(y, None), ka)
            self.s.arrived(self.band_b(x, None), kb)


def block_kernel(
    tok_in, win_in, bin_in, taps_in, cbias_in, wout_in, bout_in, out,
    tok, win, wout0, wout1, ext, act, part, own_par, par, tp, b1, cb1, bout, sendbuf, recvbuf, done,
    lsem, ssem, rsem,
):
    y, c, x, z = place()
    s = Sender(ssem, rsem)
    xs = [(x + d) % NX for d in range(NX)]
    zp, zm = (z + 1) % NZ, (z + NZ - 1) % NZ
    yp, ym = (y + 1) % NY, (y + NY - 1) % NY
    upper = x >> 1
    frame = frame_of(y, c, x)
    last = NY * 4 - 1
    tc, tx = moved_to(y, c, x)
    fc, fx = moved_from(y, c, x)
    stays = (tc == c) & (tx == x)
    moves = jnp.logical_not(stays)
    has_next, has_prev = frame < last, frame > 0
    ny, nc, nx = holder(jnp.minimum(frame + 1, last), upper)
    py, pc, px = holder(jnp.maximum(frame - 1, 0), upper)
    nxt, nxt_other = dev(ny, nc, nx, z), dev(ny, nc, 3 - nx, z)
    prv, prv_other = dev(py, pc, px, z), dev(py, pc, 3 - px, z)
    other_half = dev(y, c, 3 - x, z)

    locals_ = [
        pltpu.make_async_copy(taps_in, tp, lsem.at[0]),
        pltpu.make_async_copy(bin_in, b1, lsem.at[1]),
        pltpu.make_async_copy(cbias_in, cb1, lsem.at[2]),
    ]
    own_bout = pltpu.make_async_copy(bout_in, bout, lsem.at[3])
    for copy in locals_ + [own_bout]:
        copy.start()

    def win_block(x_, y_, rows):
        return win.at[y_, c, rows, pl.ds(x_ * BLK, BLK)]

    def win_a(y_, part_):
        cols = pl.ds(0, CH) if part_ is None else pl.ds(part_ * (CH // 2), CH // 2)
        return win.at[y_, c, pl.ds(0, HALF), cols]

    def win_b(x_, part_):
        ys = pl.ds(0, NY) if part_ is None else pl.ds(part_ * 2, 2)
        return win.at[ys, c, pl.ds(HALF, HALF), pl.ds(x_ * BLK, BLK)]

    g_in = WeightGather(s, win_in, win_block, win_a, win_b)
    own_in = pltpu.make_async_copy(win_in, win_block(x, y, pl.ds(0, BLK)), lsem.at[4])
    own_in.start()

    def out_gather(buf, lo, w, sem):
        def block(x_, y_, rows):
            return buf.at[x_, rows, pl.ds(c * (NY * w) + y_ * w, w)]

        def band_a(y_, part_):
            xs_ = pl.ds(0, NX) if part_ is None else pl.ds(part_ * 2, 2)
            return buf.at[xs_, pl.ds(0, HALF), pl.ds(c * (NY * w) + y_ * w, w)]

        def band_b(x_, part_):
            n = NY * w
            cols = pl.ds(c * n, n) if part_ is None else pl.ds(c * n + part_ * (n // 2), n // 2)
            return buf.at[x_, pl.ds(HALF, HALF), cols]

        own = wout_in.at[:, pl.ds(lo, w)]
        copy = pltpu.make_async_copy(own, block(x, y, pl.ds(0, BLK)), lsem.at[sem])
        copy.start()
        return WeightGather(s, own, block, band_a, band_b), copy

    g0, own0 = out_gather(wout0, 0, 256, 5)
    g1, own1 = out_gather(wout1, 256, 128, 6)

    for copy in locals_:
        copy.wait()
    own_par[0:27, :] = tp[...]
    own_par[27:28, :] = b1[...].reshape(1, BLK)
    own_par[28:29, :] = cb1[...].reshape(1, BLK)

    greet(
        [(dev(y, c, xs[d], z), None) for d in (1, 2, 3)]
        + [(dev(yp, c, x, z), None), (dev(ym, c, x, z), None)]
        + [(dev(y, c, x, zp), None), (dev(y, c, x, zm), None)]
        + [(dev(y, 1 - c, x, z), None)]
        + [(dev(y, tc, tx, z), moves), (dev(y, fc, fx, z), moves)]
        + [(nxt, has_next), (nxt_other, has_next), (prv, has_prev), (prv_other, has_prev)]
        + [(other_half, None)]
    )

    def tok_at(z_, p):
        return tok.at[pl.ds(((z_ + NZ) % NZ) * OWN + p * PIECE, PIECE)]

    home = []
    for p in range(PIECES):
        src = tok_in.at[pl.ds(p * PIECE, PIECE)]
        k = s.send(src, tok_at(z, p), dev(y, tc, tx, z), when=moves)
        stay = pltpu.make_async_copy(src, tok_at(z, p), rsem.at[k])
        pl.when(stays)(stay.start)
        home.append(stay)
    g_in.stage1()

    @pl.when(upper == 0)
    def _():
        ext[:, 0] = jnp.zeros((3, WW, CH), BF16)

    @pl.when(upper == 1)
    def _():
        ext[:, ROWS + 1] = jnp.zeros((3, WW, CH), BF16)

    @pl.when(jnp.logical_not(has_prev))
    def _():
        @pl.loop(0, ROWS + 2)
        def _(r):
            ext[0, r] = jnp.zeros((WW, CH), BF16)

    @pl.when(jnp.logical_not(has_next))
    def _():
        @pl.loop(0, ROWS + 2)
        def _(r):
            ext[2, r] = jnp.zeros((WW, CH), BF16)

    k_tok = {}

    def token_step(d):
        for p in range(PIECES):
            if d == 1:
                home[p].wait()
            for way, to in ((1, zp), (-1, zm)):
                if d == 4 and (p < PIECES // 2) != (way == 1):
                    continue
                src = tok_at(z - way * (d - 1), p)
                if d > 1:
                    s.arrived(src, k_tok[way, d - 1, p])
                k_tok[way, d, p] = s.send(src, src, dev(y, c, x, to))

    def par_at(x_):
        return par.at[:, pl.ds(x_ * BLK, BLK)]

    token_step(1)
    g_in.stage1_forward()
    own_in.wait()
    g_in.stage2()
    k_par = [s.send(own_par, par_at(x), dev(y, c, xs[d], z)) for d in (1, 2, 3)]
    own_copy = pltpu.make_async_copy(own_par, par_at(x), lsem.at[7])
    own_copy.start()
    token_step(2)
    token_step(3)
    g_in.stage2_forward()
    g0.stage1()
    own0.wait()
    g_in.stage3()
    token_step(4)
    g0.stage1_forward()
    own_copy.wait()
    for d in (1, 2, 3):
        s.arrived(par_at((x + NX - d) % NX), k_par[d - 1])
    g_in.finish()
    g0.stage2()
    for p in range(PIECES):
        way = -1 if p < PIECES // 2 else 1
        s.arrived(tok_at(z - way * 3, p), k_tok[way, 3, p])
        s.arrived(tok_at(z + 4, p), k_tok[-way, 4, p])

    src_row = jnp.where(upper == 0, ROWS, 1)
    dst_row = jnp.where(upper == 0, 0, ROWS + 1)
    got_row = jnp.where(upper == 0, ROWS + 1, 0)
    inner = pl.ds(1, ROWS)
    arrivals = []
    step = 256
    for j in range(HALO_CHUNKS):

        @pl.loop(0, HALO_CH // step)
        def _(i):
            cols = pl.ds(pl.multiple_of(j * HALO_CH + i * step, step), step)
            w = win[:, :, :, cols].reshape(D, step)
            before = jnp.dot(tok[...], w, preferred_element_type=F32) + par[27:28, cols]
            ext[1, inner, :, cols] = before.astype(BF16).reshape(ROWS, WW, step)

        cols = pl.ds(j * HALO_CH, HALO_CH)
        frame_src = ext.at[1, inner, :, cols]
        row_src = ext.at[1, src_row, :, cols]
        k1 = s.send(frame_src, ext.at[0, inner, :, cols], nxt, when=has_next)
        k2 = s.send(frame_src, ext.at[2, inner, :, cols], prv, when=has_prev)
        k3 = s.send(row_src, ext.at[1, dst_row, :, cols], other_half)
        k4 = s.send(row_src, ext.at[0, dst_row, :, cols], nxt_other, when=has_next)
        k5 = s.send(row_src, ext.at[2, dst_row, :, cols], prv_other, when=has_prev)
        arrivals.append([
            (ext.at[0, inner, :, cols], k1, has_prev),
            (ext.at[2, inner, :, cols], k2, has_next),
            (ext.at[1, got_row, :, cols], k3, None),
            (ext.at[0, got_row, :, cols], k4, has_prev),
            (ext.at[2, got_row, :, cols], k5, has_next),
        ])
    g0.stage2_forward()
    g1.stage1()
    own1.wait()

    column = lax.broadcasted_iota(jnp.int32, (WW, 128), 0)

    def conv(j):
        for copy in arrivals[j]:
            s.arrived(*copy)

        @pl.loop(0, HALO_CH // 128)
        def _(i):
            lanes = pl.ds(pl.multiple_of(j * HALO_CH + i * 128, 128), 128)

            @pl.loop(0, ROWS)
            def _(r):
                sums = [None, None, None]
                for dt in range(3):
                    for dh in range(3):
                        v = ext[dt, r + dh, :, lanes].astype(F32)
                        for dw in range(3):
                            k = 9 * dt + 3 * dh + dw
                            t = v * par[k : k + 1, lanes]
                            sums[dw] = t if sums[dw] is None else sums[dw] + t
                left = jnp.where(column == 0, 0.0, pltpu.roll(sums[0], 1, 0))
                right = jnp.where(column == WW - 1, 0.0, pltpu.roll(sums[2], WW - 1, 0))
                v = sums[1] + left + right + par[28:29, lanes]
                half = 0.5 * v
                t = jnp.tanh(v * (0.7978845608028654 + 0.035677408136300125 * (v * v)))
                act[pl.ds(pl.multiple_of(r * WW, WW), WW), lanes] = (half + half * t).astype(BF16)

    conv(0)
    g0.stage3()
    g1.stage1_forward()
    conv(1)
    g1.stage2()
    conv(2)
    g1.stage2_forward()
    g0.finish()

    chains = [(q, way, 4 if (q % 2 == 0) == (way == 1) else 3) for q in range(3) for way in (1, -1)]
    slot, n = {}, 0
    for i, (q, way, length) in enumerate(chains):
        for st in range(length):
            slot[i, st] = n
            n += 1
    k_of = {}

    def multiply(q):
        buf, lo = (wout0, q * UNIT) if q < 2 else (wout1, 0)

        @pl.loop(0, UNIT // 256)
        def _(i):
            at = pl.multiple_of(i * 256, 256)
            w = buf[:, :, pl.ds(lo + at, 256)].reshape(CH, 256)
            part[q, :, pl.ds(at, 256)] = jnp.dot(act[...], w, preferred_element_type=F32)

    def pass_on(q, st):
        for i, (q_, way, length) in enumerate(chains):
            if q_ != q or st >= length:
                continue
            at = (z + way * (length - st) + NZ) % NZ
            rows = pl.ds(pl.multiple_of(at * OWN, OWN), OWN)
            value = part[q, rows, :]
            if st > 0:
                got = recvbuf.at[slot[i, st - 1]]
                s.arrived(got, k_of[i, st - 1])
                value = value + got[...].astype(F32)
            mine = slot[i, st]
            sendbuf[mine] = value.astype(BF16)
            to = dev(y, c, x, zp if way == 1 else zm)
            k_of[i, st] = s.send(sendbuf.at[mine], recvbuf.at[mine], to)

    def collect(q):
        rows = pl.ds(pl.multiple_of(z * OWN, OWN), OWN)
        value = part[q, rows, :]
        for i in (2 * q, 2 * q + 1):
            mine = slot[i, chains[i][2] - 1]
            s.arrived(recvbuf.at[mine], k_of[i, chains[i][2] - 1])
            value = value + recvbuf[mine].astype(F32)
        w, lo = (256, 0) if q < 2 else (128, 256)
        for n_ in range(UNIT // w):
            c_, y_ = (q, n_) if q < 2 else (n_ // NY, n_ % NY)
            to = (y_ * 2 + c_) * BLK + lo
            done[:, to : to + w] = (
                value[:, n_ * w : (n_ + 1) * w] + bout[to : to + w].reshape(1, w)
            ).astype(BF16)

    own_bout.wait()
    multiply(0)
    pass_on(0, 0)
    multiply(1)
    pass_on(1, 0)
    pass_on(0, 1)
    g1.stage3()
    g1.finish()
    multiply(2)
    pass_on(2, 0)
    for st in (1, 2, 3):
        for q in range(3):
            if (q, st) != (0, 1):
                pass_on(q, st)
    for q in range(3):
        collect(q)
    k = s.send(done, out, dev(y, fc, fx, z), when=moves)
    stay = pltpu.make_async_copy(done, out, rsem.at[k])
    pl.when(stays)(stay.start)
    stay.wait()
    s.drain()


def body(tokens, w_in, b_in, conv_taps, conv_bias, w_out, b_out):
    keys = 200
    hbm = pl.BlockSpec(memory_space=pl.ANY)
    return pl.pallas_call(
        block_kernel,
        out_shape=jax.ShapeDtypeStruct((OWN, D), BF16),
        in_specs=[hbm] * 7,
        out_specs=hbm,
        scratch_shapes=[
            pltpu.VMEM((GROUP, D), BF16),
            pltpu.VMEM((NY, 2, BLK, CH), BF16),
            pltpu.VMEM((NX, BLK, 2 * NY * 256), BF16),
            pltpu.VMEM((NX, BLK, 2 * NY * 128), BF16),
            pltpu.VMEM((3, ROWS + 2, WW, CH), BF16),
            pltpu.VMEM((GROUP, CH), BF16),
            pltpu.VMEM((3, GROUP, UNIT), F32),
            pltpu.VMEM((32, BLK), F32),
            pltpu.VMEM((32, CH), F32),
            pltpu.VMEM((27, BLK), F32),
            pltpu.VMEM((BLK,), F32),
            pltpu.VMEM((BLK,), F32),
            pltpu.VMEM((D,), F32),
            pltpu.VMEM((21, OWN, UNIT), BF16),
            pltpu.VMEM((21, OWN, UNIT), BF16),
            pltpu.VMEM((OWN, D), BF16),
            pltpu.SemaphoreType.DMA((8,)),
            pltpu.SemaphoreType.DMA((keys,)),
            pltpu.SemaphoreType.DMA((keys,)),
        ],
        compiler_params=pltpu.CompilerParams(
            collective_id=0, has_side_effects=True, vmem_limit_bytes=60 * 2**20
        ),
        name="mix_ffn",
    )(tokens, w_in, b_in, conv_taps, conv_bias, w_out, b_out)


def solution(mesh):
    placed = (
        P(("row", "col"), None),
        P("row", "col"),
        P("col"),
        P(None, "col"),
        P("col"),
        P("col", "row"),
        P(),
    )
    return jax.shard_map(
        body, mesh=mesh, in_specs=placed, out_specs=P(("row", "col"), None), check_vma=False
    )
```

```python
import functools

import jax
import jax.numpy as jnp
from jax import lax
from jax.experimental import pallas as pl
from jax.experimental.pallas import tpu as pltpu
from jax.sharding import PartitionSpec as P

MESH = pl.DeviceIdType.MESH
NX, NY, NZ = 4, 4, 8
D = 3072
BLK = 384
HALF = BLK // 2
CH = NX * BLK
GROUP = 512
OWN = 64
WW = 32
ROWS = GROUP // WW
HALO_CHUNKS = 3
PIECES = 4
PIECE = OWN // PIECES
UNIT = 1024
HALO_CH = CH // HALO_CHUNKS
BF16, F32 = jnp.bfloat16, jnp.float32


def place():
    row, col = lax.axis_index("row"), lax.axis_index("col")
    return row // 2, row % 2, col // NZ, col % NZ


def dev(y, c, x, z):
    return {"row": y * 2 + c, "col": x * NZ + z}


def moved_to(y, c, x):
    b = c ^ (y & 1)
    upper = x & 1
    return x >> 1, jnp.where(upper == 0, b, 3 - b)


def moved_from(y, c, x):
    b = (x ^ (x >> 1)) & 1
    return b ^ (y & 1), c * 2 + (x >> 1)


def frame_of(y, c, x):
    b = (x ^ (x >> 1)) & 1
    return 4 * y + 2 * (b ^ (y & 1)) + c


def holder(frame, upper):
    pair = frame >> 1
    y = pair >> 1
    b = (pair & 1) ^ (y & 1)
    return y, frame & 1, jnp.where(upper == 0, b, 3 - b)


class Sender:
    def __init__(self, ssem, rsem):
        self.ssem, self.rsem, self.used, self.sent = ssem, rsem, 0, []

    def key(self):
        self.used += 1
        return self.used - 1

    def make(self, src, dst, k, to):
        return pltpu.make_async_remote_copy(
            src_ref=src,
            dst_ref=dst,
            send_sem=self.ssem.at[k],
            recv_sem=self.rsem.at[k],
            device_id=to,
            device_id_type=MESH,
        )

    def send(self, src, dst, to, when=None):
        k = self.key()
        copy = self.make(src, dst, k, to)
        if when is None:
            copy.start()
        else:
            pl.when(when)(copy.start)
        self.sent.append((copy, when))
        return k

    def arrived(self, ref, k, when=None):
        copy = pltpu.make_async_copy(ref, ref, self.rsem.at[k])
        if when is None:
            copy.wait()
        else:
            pl.when(when)(copy.wait)

    def drain(self):
        for copy, when in self.sent:
            if when is None:
                copy.wait_send()
            else:
                pl.when(when)(copy.wait_send)
        self.sent = []


def greet(peers):
    barrier = pltpu.get_barrier_semaphore()
    count = 0
    for to, when in peers:
        signal = functools.partial(pl.semaphore_signal, barrier, inc=1, device_id=to, device_id_type=MESH)
        if when is None:
            signal()
            count = count + 1
        else:
            pl.when(when)(signal)
            count = count + when.astype(jnp.int32)
    pl.semaphore_wait(barrier, count)


class WeightGather:
    def __init__(self, sender, own, block, band_a, band_b):
        self.s, self.own = sender, own
        self.block, self.band_a, self.band_b = block, band_a, band_b
        self.y, self.c, self.x, self.z = place()
        y, c, x, z = self.y, self.c, self.x, self.z
        self.xs = {"0": x, "+": (x + 1) % NX, "-": (x + NX - 1) % NX, "2": (x + 2) % NX}
        self.ys = {"0": y, "+": (y + 1) % NY, "-": (y + NY - 1) % NY, "2": (y + 2) % NY}
        self.to = {
            "x+": dev(y, c, self.xs["+"], z),
            "x-": dev(y, c, self.xs["-"], z),
            "y+": dev(self.ys["+"], c, x, z),
            "y-": dev(self.ys["-"], c, x, z),
        }
        self.keys, self.from_partner = {}, []

    def at(self, place_, lo, hi):
        return self.block(self.xs[place_[0]], self.ys[place_[1]], pl.ds(lo, hi - lo))

    def push(self, place_, lo, hi, way):
        src = self.at(place_, lo, hi)
        self.keys[place_, lo, hi, way] = self.s.send(src, src, self.to[way])

    def pull(self, here, lo, hi, way, there):
        self.s.arrived(self.at(here, lo, hi), self.keys[there, lo, hi, way])

    def p0(self):
        for way in ("y+", "y-", "x+", "x-"):
            self.keys["00", 0, BLK, way] = self.s.send(self.own, self.at("00", 0, BLK), self.to[way])

    def p1y(self):
        h, q = HALF, HALF // 2
        self.pull("0-", 0, BLK, "y+", "00")
        self.push("0-", 0, h + q, "y+")
        self.push("0-", h, BLK, "x+")
        self.push("0-", h, BLK, "x-")
        self.pull("0+", 0, BLK, "y-", "00")
        self.push("0+", h + q, BLK, "y-")
        self.push("0+", h, BLK, "x+")
        self.push("0+", h, BLK, "x-")

    def p1x(self):
        h, q = HALF, HALF // 2
        self.pull("-0", 0, BLK, "x+", "00")
        self.push("-0", q, BLK, "x+")
        self.push("-0", 0, h, "y+")
        self.push("-0", 0, h, "y-")
        self.pull("+0", 0, BLK, "x-", "00")
        self.push("+0", 0, q, "x-")
        self.push("+0", 0, h, "y+")
        self.push("+0", 0, h, "y-")

    def p2y(self):
        h, q = HALF, HALF // 2
        self.pull("02", 0, h + q, "y+", "0-")
        self.pull("02", h + q, BLK, "y-", "0+")
        self.push("02", h, BLK, "x-")
        self.push("02", h, BLK, "x+")
        self.pull("--", 0, h, "y+", "-0")
        self.push("--", 0, h, "y+")
        self.pull("++", 0, h, "y-", "+0")
        self.push("++", 0, h, "y-")

    def p2x(self):
        h, q = HALF, HALF // 2
        self.pull("20", q, BLK, "x+", "-0")
        self.pull("20", 0, q, "x-", "+0")
        self.push("20", 0, h, "y-")
        self.push("20", 0, h, "y+")
        self.pull("--", h, BLK, "x+", "0-")
        self.push("--", h, BLK, "x+")
        self.pull("++", h, BLK, "x-", "0+")
        self.push("++", h, BLK, "x-")
        self.partner("0", "0")

    def p3(self):
        h = HALF
        self.pull("2+", 0, h, "y-", "20")
        self.push("2+", 0, h, "y-")
        self.pull("+2", h, BLK, "x-", "02")
        self.push("+2", h, BLK, "x-")
        self.pull("+-", 0, h, "y+", "+0")
        self.pull("-+", 0, h, "y-", "-0")
        self.pull("-+", h, BLK, "x+", "0+")
        self.pull("+-", h, BLK, "x-", "0-")
        self.pull("2-", 0, h, "y+", "20")
        self.pull("-2", h, BLK, "x+", "02")
        self.partner("-", "-")
        self.partner("+", "+")

    def p4(self):
        h = HALF
        self.pull("-2", 0, h, "y+", "--")
        self.pull("2-", h, BLK, "x+", "--")
        self.pull("+2", 0, h, "y-", "++")
        self.pull("2+", h, BLK, "x-", "++")
        self.pull("22", 0, h, "y-", "2+")
        self.pull("22", h, BLK, "x-", "+2")
        self.partner("2", "2")

    def partner(self, x, y):
        other = dev(self.y, 1 - self.c, self.x, self.z)
        a, b = self.band_a(self.ys[y]), self.band_b(self.xs[x])
        self.from_partner.append((a, self.s.send(a, a, other)))
        self.from_partner.append((b, self.s.send(b, b, other)))

    def finish(self):
        for ref, k in self.from_partner:
            self.s.arrived(ref, k)


def block_kernel(
    tok_in, win_in, bin_in, taps_in, cbias_in, wout_in, bout_in, out,
    tok, win, wout, ext, act, part, own_par, par, tp, b1, cb1, bout, sendbuf, recvbuf, summed, moved, done,
    lsem, ssem, rsem,
):
    y, c, x, z = place()
    s = Sender(ssem, rsem)
    xs = [(x + d) % NX for d in range(NX)]
    zp, zm = (z + 1) % NZ, (z + NZ - 1) % NZ
    yp, ym = (y + 1) % NY, (y + NY - 1) % NY
    upper = x >> 1
    frame = frame_of(y, c, x)
    last = NY * 4 - 1
    tc, tx = moved_to(y, c, x)
    fc, fx = moved_from(y, c, x)
    stays = (tc == c) & (tx == x)
    moves = jnp.logical_not(stays)
    has_next, has_prev = frame < last, frame > 0
    ny, nc, nx = holder(jnp.minimum(frame + 1, last), upper)
    py, pc, px = holder(jnp.maximum(frame - 1, 0), upper)
    nxt, nxt_other = dev(ny, nc, nx, z), dev(ny, nc, 3 - nx, z)
    prv, prv_other = dev(py, pc, px, z), dev(py, pc, 3 - px, z)
    other_half = dev(y, c, 3 - x, z)

    locals_ = [
        pltpu.make_async_copy(taps_in, tp, lsem.at[0]),
        pltpu.make_async_copy(bin_in, b1, lsem.at[1]),
        pltpu.make_async_copy(cbias_in, cb1, lsem.at[2]),
    ]
    own_bout = pltpu.make_async_copy(bout_in, bout, lsem.at[3])
    for copy in locals_ + [own_bout]:
        copy.start()

    def win_block(x_, y_, rows):
        return win.at[y_, c, rows, pl.ds(x_ * BLK, BLK)]

    def win_a(y_):
        return win.at[y_, c, pl.ds(0, HALF), :]

    def win_b(x_):
        return win.at[:, c, pl.ds(HALF, HALF), pl.ds(x_ * BLK, BLK)]

    g_in = WeightGather(s, win_in, win_block, win_a, win_b)
    own_in = pltpu.make_async_copy(win_in, win_block(x, y, pl.ds(0, BLK)), lsem.at[4])
    own_in.start()

    def out_gather(q):
        w = BLK // 3
        n = NY * w

        def block(x_, y_, rows):
            return wout.at[q, x_, rows, pl.ds(c * n + y_ * w, w)]

        def band_a(y_):
            return wout.at[q, :, pl.ds(0, HALF), pl.ds(c * n + y_ * w, w)]

        def band_b(x_):
            return wout.at[q, x_, pl.ds(HALF, HALF), pl.ds(c * n, n)]

        own = wout_in.at[:, pl.ds(q * w, w)]
        copy = pltpu.make_async_copy(own, block(x, y, pl.ds(0, BLK)), lsem.at[5 + q])
        copy.start()
        return WeightGather(s, own, block, band_a, band_b), copy

    (g0, own0), (g1, own1), (g2, own2) = [out_gather(q) for q in range(3)]

    for copy in locals_:
        copy.wait()
    own_par[0:27, :] = tp[...]
    own_par[27:28, :] = b1[...].reshape(1, BLK)
    own_par[28:29, :] = cb1[...].reshape(1, BLK)

    greet(
        [(dev(y, c, xs[d], z), None) for d in (1, 2, 3)]
        + [(dev(yp, c, x, z), None), (dev(ym, c, x, z), None)]
        + [(dev(y, c, x, zp), None), (dev(y, c, x, zm), None)]
        + [(dev(y, 1 - c, x, z), None)]
        + [(dev(y, tc, tx, z), moves), (dev(y, fc, fx, z), moves)]
        + [(nxt, has_next), (nxt_other, has_next), (prv, has_prev), (prv_other, has_prev)]
        + [(other_half, None)]
    )

    def tok_at(z_, p):
        return tok.at[pl.ds(((z_ + NZ) % NZ) * OWN + p * PIECE, PIECE)]

    home = []
    for p in range(PIECES):
        src = tok_in.at[pl.ds(p * PIECE, PIECE)]
        k = s.send(src, tok_at(z, p), dev(y, tc, tx, z), when=moves)
        stay = pltpu.make_async_copy(src, tok_at(z, p), rsem.at[k])
        pl.when(stays)(stay.start)
        home.append(stay)
    g_in.p0()

    @pl.when(upper == 0)
    def _():
        ext[:, 0] = jnp.zeros((3, WW, CH), BF16)

    @pl.when(upper == 1)
    def _():
        ext[:, ROWS + 1] = jnp.zeros((3, WW, CH), BF16)

    @pl.when(jnp.logical_not(has_prev))
    def _():
        @pl.loop(0, ROWS + 2)
        def _(r):
            ext[0, r] = jnp.zeros((WW, CH), BF16)

    @pl.when(jnp.logical_not(has_next))
    def _():
        @pl.loop(0, ROWS + 2)
        def _(r):
            ext[2, r] = jnp.zeros((WW, CH), BF16)

    k_tok = {}

    def token_step(d):
        for p in range(PIECES):
            if d == 1:
                home[p].wait()
            for way, to in ((1, zp), (-1, zm)):
                if d == 4 and (p < PIECES // 2) != (way == 1):
                    continue
                src = tok_at(z - way * (d - 1), p)
                if d > 1:
                    s.arrived(src, k_tok[way, d - 1, p])
                k_tok[way, d, p] = s.send(src, src, dev(y, c, x, to))

    def par_at(x_):
        return par.at[:, pl.ds(x_ * BLK, BLK)]

    token_step(1)
    g_in.p1y()
    k_par = [s.send(own_par, par_at(x), dev(y, c, xs[d], z)) for d in (1, 2, 3)]
    own_copy = pltpu.make_async_copy(own_par, par_at(x), lsem.at[8])
    own_copy.start()
    token_step(2)
    g_in.p1x()
    own_in.wait()
    g_in.p2y()
    token_step(3)
    g_in.p2x()
    token_step(4)
    g_in.p3()
    own0.wait()
    g0.p0()
    own_copy.wait()
    for d in (1, 2, 3):
        s.arrived(par_at((x + NX - d) % NX), k_par[d - 1])
    g_in.p4()
    for p in range(PIECES):
        way = -1 if p < PIECES // 2 else 1
        s.arrived(tok_at(z - way * 3, p), k_tok[way, 3, p])
        s.arrived(tok_at(z + 4, p), k_tok[-way, 4, p])
    g0.p1y()
    g0.p1x()
    g_in.finish()

    src_row = jnp.where(upper == 0, ROWS, 1)
    dst_row = jnp.where(upper == 0, 0, ROWS + 1)
    got_row = jnp.where(upper == 0, ROWS + 1, 0)
    inner = pl.ds(1, ROWS)
    arrivals = []
    step = 256
    for j in range(HALO_CHUNKS):

        @pl.loop(0, HALO_CH // step)
        def _(i):
            cols = pl.ds(pl.multiple_of(j * HALO_CH + i * step, step), step)
            w = win[:, :, :, cols].reshape(D, step)
            before = jnp.dot(tok[...], w, preferred_element_type=F32) + par[27:28, cols]
            ext[1, inner, :, cols] = before.astype(BF16).reshape(ROWS, WW, step)

        cols = pl.ds(j * HALO_CH, HALO_CH)
        frame_src = ext.at[1, inner, :, cols]
        row_src = ext.at[1, src_row, :, cols]
        k1 = s.send(frame_src, ext.at[0, inner, :, cols], nxt, when=has_next)
        k2 = s.send(frame_src, ext.at[2, inner, :, cols], prv, when=has_prev)
        k3 = s.send(row_src, ext.at[1, dst_row, :, cols], other_half)
        k4 = s.send(row_src, ext.at[0, dst_row, :, cols], nxt_other, when=has_next)
        k5 = s.send(row_src, ext.at[2, dst_row, :, cols], prv_other, when=has_prev)
        arrivals.append([
            (ext.at[0, inner, :, cols], k1, has_prev),
            (ext.at[2, inner, :, cols], k2, has_next),
            (ext.at[1, got_row, :, cols], k3, None),
            (ext.at[0, got_row, :, cols], k4, has_prev),
            (ext.at[2, got_row, :, cols], k5, has_next),
        ])
        if j == 0:
            g0.p2y()
            g0.p2x()
        if j == 1:
            g0.p3()
    own1.wait()
    g1.p0()
    g0.p4()

    column = lax.broadcasted_iota(jnp.int32, (WW, 128), 0)

    def conv(j):
        for copy in arrivals[j]:
            s.arrived(*copy)

        @pl.loop(0, HALO_CH // 128)
        def _(i):
            lanes = pl.ds(pl.multiple_of(j * HALO_CH + i * 128, 128), 128)

            @pl.loop(0, ROWS)
            def _(r):
                sums = [None, None, None]
                for dt in range(3):
                    for dh in range(3):
                        v = ext[dt, r + dh, :, lanes].astype(F32)
                        for dw in range(3):
                            k = 9 * dt + 3 * dh + dw
                            t = v * par[k : k + 1, lanes]
                            sums[dw] = t if sums[dw] is None else sums[dw] + t
                left = jnp.where(column == 0, 0.0, pltpu.roll(sums[0], 1, 0))
                right = jnp.where(column == WW - 1, 0.0, pltpu.roll(sums[2], WW - 1, 0))
                v = sums[1] + left + right + par[28:29, lanes]
                half = 0.5 * v
                t = jnp.tanh(v * (0.7978845608028654 + 0.035677408136300125 * (v * v)))
                act[pl.ds(pl.multiple_of(r * WW, WW), WW), lanes] = (half + half * t).astype(BF16)

    conv(0)
    g1.p1y()
    g1.p1x()
    conv(1)
    g1.p2y()
    g1.p2x()
    own2.wait()
    g2.p0()
    conv(2)
    g0.finish()

    chains = [(q, way, 4 if (q % 2 == 0) == (way == 1) else 3) for q in range(3) for way in (1, -1)]
    slot, n = {}, 0
    for i, (q, way, length) in enumerate(chains):
        for st in range(length):
            slot[i, st] = n
            n += 1
    k_of = {}

    def multiply(q):
        @pl.loop(0, UNIT // 256)
        def _(i):
            cols = pl.ds(pl.multiple_of(i * 256, 256), 256)
            w = wout[q, :, :, cols].reshape(CH, 256)
            part[q, :, cols] = jnp.dot(act[...], w, preferred_element_type=F32)

    def pass_on(q, st):
        for i, (q_, way, length) in enumerate(chains):
            if q_ != q or st >= length:
                continue
            at = (z + way * (length - st) + NZ) % NZ
            rows = pl.ds(pl.multiple_of(at * OWN, OWN), OWN)
            value = part[q, rows, :]
            if st > 0:
                got = recvbuf.at[slot[i, st - 1]]
                s.arrived(got, k_of[i, st - 1])
                value = value + got[...].astype(F32)
            mine = slot[i, st]
            sendbuf[mine] = value.astype(BF16)
            to = dev(y, c, x, zp if way == 1 else zm)
            k_of[i, st] = s.send(sendbuf.at[mine], recvbuf.at[mine], to)

    back = []

    def collect(q):
        rows = pl.ds(pl.multiple_of(z * OWN, OWN), OWN)
        value = part[q, rows, :]
        for i in (2 * q, 2 * q + 1):
            mine = slot[i, chains[i][2] - 1]
            s.arrived(recvbuf.at[mine], k_of[i, chains[i][2] - 1])
            value = value + recvbuf[mine].astype(F32)
        w = BLK // 3
        for n_ in range(UNIT // w):
            lo = ((n_ % NY) * 2 + n_ // NY) * BLK + q * w
            summed[q, :, n_ * w : (n_ + 1) * w] = (
                value[:, n_ * w : (n_ + 1) * w] + bout[lo : lo + w].reshape(1, w)
            ).astype(BF16)
        k = s.send(summed.at[q], moved.at[q], dev(y, fc, fx, z), when=moves)
        stay = pltpu.make_async_copy(summed.at[q], moved.at[q], rsem.at[k])
        pl.when(stays)(stay.start)
        back.append(stay)

    def put(q):
        back[q].wait()
        w = BLK // 3
        for n_ in range(UNIT // w):
            lo = ((n_ % NY) * 2 + n_ // NY) * BLK + q * w
            done[:, lo : lo + w] = moved[q, :, n_ * w : (n_ + 1) * w]

    own_bout.wait()
    multiply(0)
    pass_on(0, 0)
    g1.p3()
    g2.p1y()
    g2.p1x()
    pass_on(0, 1)
    g1.p4()
    g2.p2y()
    g2.p2x()
    g1.finish()
    multiply(1)
    pass_on(1, 0)
    pass_on(0, 2)
    g2.p3()
    pass_on(1, 1)
    pass_on(0, 3)
    g2.p4()
    g2.finish()
    multiply(2)
    pass_on(2, 0)
    pass_on(1, 2)
    collect(0)
    pass_on(2, 1)
    pass_on(1, 3)
    pass_on(2, 2)
    collect(1)
    put(0)
    pass_on(2, 3)
    collect(2)
    put(1)
    put(2)
    stored = pltpu.make_async_copy(done, out, lsem.at[9])
    stored.start()
    stored.wait()
    s.drain()


def body(tokens, w_in, b_in, conv_taps, conv_bias, w_out, b_out):
    keys = 230
    hbm = pl.BlockSpec(memory_space=pl.ANY)
    return pl.pallas_call(
        block_kernel,
        out_shape=jax.ShapeDtypeStruct((OWN, D), BF16),
        in_specs=[hbm] * 7,
        out_specs=hbm,
        scratch_shapes=[
            pltpu.VMEM((GROUP, D), BF16),
            pltpu.VMEM((NY, 2, BLK, CH), BF16),
            pltpu.VMEM((3, NX, BLK, UNIT), BF16),
            pltpu.VMEM((3, ROWS + 2, WW, CH), BF16),
            pltpu.VMEM((GROUP, CH), BF16),
            pltpu.VMEM((3, GROUP, UNIT), F32),
            pltpu.VMEM((32, BLK), F32),
            pltpu.VMEM((32, CH), F32),
            pltpu.VMEM((27, BLK), F32),
            pltpu.VMEM((BLK,), F32),
            pltpu.VMEM((BLK,), F32),
            pltpu.VMEM((D,), F32),
            pltpu.VMEM((21, OWN, UNIT), BF16),
            pltpu.VMEM((21, OWN, UNIT), BF16),
            pltpu.VMEM((3, OWN, UNIT), BF16),
            pltpu.VMEM((3, OWN, UNIT), BF16),
            pltpu.VMEM((OWN, D), BF16),
            pltpu.SemaphoreType.DMA((10,)),
            pltpu.SemaphoreType.DMA((keys,)),
            pltpu.SemaphoreType.DMA((keys,)),
        ],
        compiler_params=pltpu.CompilerParams(
            collective_id=0, has_side_effects=True, vmem_limit_bytes=60 * 2**20
        ),
        name="mix_ffn",
    )(tokens, w_in, b_in, conv_taps, conv_bias, w_out, b_out)


def solution(mesh):
    placed = (
        P(("row", "col"), None),
        P("row", "col"),
        P("col"),
        P(None, "col"),
        P("col"),
        P("col", "row"),
        P(),
    )
    return jax.shard_map(
        body, mesh=mesh, in_specs=placed, out_specs=P(("row", "col"), None), check_vma=False
    )
```

```python
import functools

import jax
import jax.numpy as jnp
from jax import lax
from jax.experimental import pallas as pl
from jax.experimental.pallas import tpu as pltpu
from jax.sharding import PartitionSpec as P

MESH = pl.DeviceIdType.MESH
NX, NY, NZ = 4, 4, 8
D = 3072
BLK = 384
UPPER_IN = 192
UPPER_OUT = 192
CH = NX * BLK
GROUP = 512
OWN = 64
WW = 32
ROWS = GROUP // WW
HALO_CHUNKS = 3
PIECES = 4
PIECE = OWN // PIECES
UNIT = 512
HALO_CH = CH // HALO_CHUNKS
BF16, F32 = jnp.bfloat16, jnp.float32


def place():
    row, col = lax.axis_index("row"), lax.axis_index("col")
    return row // 2, row % 2, col // NZ, col % NZ


def dev(y, c, x, z):
    return {"row": y * 2 + c, "col": x * NZ + z}


def moved_to(y, c, x):
    b = c ^ (y & 1)
    upper = x & 1
    return x >> 1, jnp.where(upper == 0, b, 3 - b)


def moved_from(y, c, x):
    b = (x ^ (x >> 1)) & 1
    return b ^ (y & 1), c * 2 + (x >> 1)


def frame_of(y, c, x):
    b = (x ^ (x >> 1)) & 1
    return 4 * y + 2 * (b ^ (y & 1)) + c


def holder(frame, upper):
    pair = frame >> 1
    y = pair >> 1
    b = (pair & 1) ^ (y & 1)
    return y, frame & 1, jnp.where(upper == 0, b, 3 - b)


class Sender:
    def __init__(self, ssem, rsem):
        self.ssem, self.rsem, self.used, self.sent = ssem, rsem, 0, []

    def key(self):
        self.used += 1
        return self.used - 1

    def make(self, src, dst, k, to):
        return pltpu.make_async_remote_copy(
            src_ref=src,
            dst_ref=dst,
            send_sem=self.ssem.at[k],
            recv_sem=self.rsem.at[k],
            device_id=to,
            device_id_type=MESH,
        )

    def send(self, src, dst, to, when=None):
        k = self.key()
        copy = self.make(src, dst, k, to)
        if when is None:
            copy.start()
        else:
            pl.when(when)(copy.start)
        self.sent.append((copy, when))
        return k

    def arrived(self, ref, k, when=None):
        copy = pltpu.make_async_copy(ref, ref, self.rsem.at[k])
        if when is None:
            copy.wait()
        else:
            pl.when(when)(copy.wait)

    def drain(self):
        for copy, when in self.sent:
            if when is None:
                copy.wait_send()
            else:
                pl.when(when)(copy.wait_send)
        self.sent = []


def greet(peers):
    barrier = pltpu.get_barrier_semaphore()
    count = 0
    for to, when in peers:
        signal = functools.partial(pl.semaphore_signal, barrier, inc=1, device_id=to, device_id_type=MESH)
        if when is None:
            signal()
            count = count + 1
        else:
            pl.when(when)(signal)
            count = count + when.astype(jnp.int32)
    pl.semaphore_wait(barrier, count)


class WeightGather:
    def __init__(self, sender, own, block, band_a, band_b, upper, fine):
        self.fine = fine
        self.s, self.own = sender, own
        self.h, self.qa, self.qb = upper, upper // 2, upper + (BLK - upper) // 2
        self.block, self.band_a, self.band_b = block, band_a, band_b
        self.y, self.c, self.x, self.z = place()
        y, c, x, z = self.y, self.c, self.x, self.z
        self.xs = {"0": x, "+": (x + 1) % NX, "-": (x + NX - 1) % NX, "2": (x + 2) % NX}
        self.ys = {"0": y, "+": (y + 1) % NY, "-": (y + NY - 1) % NY, "2": (y + 2) % NY}
        self.to = {
            "x+": dev(y, c, self.xs["+"], z),
            "x-": dev(y, c, self.xs["-"], z),
            "y+": dev(self.ys["+"], c, x, z),
            "y-": dev(self.ys["-"], c, x, z),
        }
        self.keys, self.from_partner = {}, []

    def at(self, place_, lo, hi):
        return self.block(self.xs[place_[0]], self.ys[place_[1]], pl.ds(lo, hi - lo))

    def push(self, place_, lo, hi, way):
        src = self.at(place_, lo, hi)
        self.keys[place_, lo, hi, way] = self.s.send(src, src, self.to[way])

    def pull(self, here, lo, hi, way, there):
        self.s.arrived(self.at(here, lo, hi), self.keys[there, lo, hi, way])

    def p0(self):
        h = self.h
        for lo, hi, ways in ((0, BLK, ("y+", "y-")), (0, h, ("x+", "x-")), (h, BLK, ("x+", "x-"))):
            for way in ways:
                src = self.own.at[pl.ds(lo, hi - lo)]
                self.keys["00", lo, hi, way] = self.s.send(src, self.at("00", lo, hi), self.to[way])
        if self.fine:
            other = dev(self.y, 1 - self.c, self.x, self.z)
            here = self.at("00", 0, BLK)
            self.from_partner.append((here, self.s.send(self.own, here, other)))

    def p1y(self):
        h, qa, qb = self.h, self.qa, self.qb
        self.pull("0-", 0, BLK, "y+", "00")
        self.push("0-", 0, qb, "y+")
        self.push("0-", h, BLK, "x+")
        self.push("0-", h, BLK, "x-")
        self.across("0-", 0, BLK)
        self.pull("0+", 0, BLK, "y-", "00")
        self.push("0+", qb, BLK, "y-")
        self.push("0+", h, BLK, "x+")
        self.push("0+", h, BLK, "x-")
        self.across("0+", 0, BLK)

    def p1x(self):
        h, qa, qb = self.h, self.qa, self.qb
        self.pull("-0", 0, h, "x+", "00")
        self.push("-0", qa, h, "x+")
        self.push("-0", 0, h, "y+")
        self.push("-0", 0, h, "y-")
        self.across("-0", 0, h)
        self.pull("+0", 0, h, "x-", "00")
        self.push("+0", 0, qa, "x-")
        self.push("+0", 0, h, "y+")
        self.push("+0", 0, h, "y-")
        self.across("+0", 0, h)

    def p2y(self):
        h, qa, qb = self.h, self.qa, self.qb
        self.pull("02", 0, qb, "y+", "0-")
        self.pull("02", qb, BLK, "y-", "0+")
        self.push("02", h, BLK, "x-")
        self.push("02", h, BLK, "x+")
        self.across("02", 0, BLK)
        self.pull("--", 0, h, "y+", "-0")
        self.push("--", 0, h, "y+")
        self.across("--", 0, h)
        self.pull("++", 0, h, "y-", "+0")
        self.push("++", 0, h, "y-")
        self.across("++", 0, h)

    def p2x(self):
        h, qa, qb = self.h, self.qa, self.qb
        self.pull("20", qa, h, "x+", "-0")
        self.pull("20", 0, qa, "x-", "+0")
        self.push("20", 0, h, "y-")
        self.push("20", 0, h, "y+")
        self.across("20", 0, h)
        self.pull("-0", h, BLK, "x+", "00")
        self.push("-0", h, BLK, "x+")
        self.across("-0", h, BLK)
        self.pull("+0", h, BLK, "x-", "00")
        self.across("+0", h, BLK)
        self.pull("--", h, BLK, "x+", "0-")
        self.push("--", h, BLK, "x+")
        self.across("--", h, BLK)
        self.pull("++", h, BLK, "x-", "0+")
        self.push("++", h, BLK, "x-")
        self.across("++", h, BLK)
        self.partner("0", "0")

    def p3(self):
        h = self.h
        self.pull("2+", 0, h, "y-", "20")
        self.push("2+", 0, h, "y-")
        self.across("2+", 0, h)
        self.pull("+2", h, BLK, "x-", "02")
        self.push("+2", h, BLK, "x-")
        self.across("+2", h, BLK)
        for here, lo, hi, way, there in (
            ("+-", 0, h, "y+", "+0"),
            ("-+", 0, h, "y-", "-0"),
            ("-+", h, BLK, "x+", "0+"),
            ("+-", h, BLK, "x-", "0-"),
            ("2-", 0, h, "y+", "20"),
            ("-2", h, BLK, "x+", "02"),
        ):
            self.pull(here, lo, hi, way, there)
            self.across(here, lo, hi)
        self.partner("-", "-")
        self.partner("+", "+")

    def p4(self):
        h = self.h
        for here, lo, hi, way, there in (
            ("20", h, BLK, "x+", "-0"),
            ("-2", 0, h, "y+", "--"),
            ("2-", h, BLK, "x+", "--"),
            ("+2", 0, h, "y-", "++"),
            ("2+", h, BLK, "x-", "++"),
            ("22", 0, h, "y-", "2+"),
            ("22", h, BLK, "x-", "+2"),
        ):
            self.pull(here, lo, hi, way, there)
            self.across(here, lo, hi)
        self.partner("2", "2")

    def across(self, here, lo, hi):
        if not self.fine:
            return
        other = dev(self.y, 1 - self.c, self.x, self.z)
        ref = self.at(here, lo, hi)
        self.from_partner.append((ref, self.s.send(ref, ref, other)))

    def partner(self, x, y):
        if self.fine:
            return
        other = dev(self.y, 1 - self.c, self.x, self.z)
        a, b = self.band_a(self.ys[y]), self.band_b(self.xs[x])
        self.from_partner.append((a, self.s.send(a, a, other)))
        self.from_partner.append((b, self.s.send(b, b, other)))

    def finish(self):
        for ref, k in self.from_partner:
            self.s.arrived(ref, k)


def block_kernel(
    tok_in, win_in, bin_in, taps_in, cbias_in, wout_in, bout_in, out,
    tok, win, wout, ext, act, part, own_par, par, tp, b1, cb1, bout, sendbuf, recvbuf, summed, moved, done,
    lsem, ssem, rsem,
):
    y, c, x, z = place()
    s = Sender(ssem, rsem)
    xs = [(x + d) % NX for d in range(NX)]
    zp, zm = (z + 1) % NZ, (z + NZ - 1) % NZ
    yp, ym = (y + 1) % NY, (y + NY - 1) % NY
    upper = x >> 1
    frame = frame_of(y, c, x)
    last = NY * 4 - 1
    tc, tx = moved_to(y, c, x)
    fc, fx = moved_from(y, c, x)
    stays = (tc == c) & (tx == x)
    moves = jnp.logical_not(stays)
    has_next, has_prev = frame < last, frame > 0
    ny, nc, nx = holder(jnp.minimum(frame + 1, last), upper)
    py, pc, px = holder(jnp.maximum(frame - 1, 0), upper)
    nxt, nxt_other = dev(ny, nc, nx, z), dev(ny, nc, 3 - nx, z)
    prv, prv_other = dev(py, pc, px, z), dev(py, pc, 3 - px, z)
    other_half = dev(y, c, 3 - x, z)

    locals_ = [
        pltpu.make_async_copy(taps_in, tp, lsem.at[0]),
        pltpu.make_async_copy(bin_in, b1, lsem.at[1]),
        pltpu.make_async_copy(cbias_in, cb1, lsem.at[2]),
    ]
    own_bout = pltpu.make_async_copy(bout_in, bout, lsem.at[3])
    for copy in locals_ + [own_bout]:
        copy.start()

    def win_block(x_, y_, rows):
        return win.at[y_, c, rows, pl.ds(x_ * BLK, BLK)]

    def win_a(y_):
        return win.at[y_, c, pl.ds(0, UPPER_IN), :]

    def win_b(x_):
        return win.at[:, c, pl.ds(UPPER_IN, BLK - UPPER_IN), pl.ds(x_ * BLK, BLK)]

    g_in = WeightGather(s, win_in, win_block, win_a, win_b, UPPER_IN, True)
    own_in = pltpu.make_async_copy(win_in, win_block(x, y, pl.ds(0, BLK)), lsem.at[4])
    own_in.start()

    def out_gather(q):
        w = BLK // 3
        n = NY * w

        def block(x_, y_, rows):
            return wout.at[q, x_, rows, pl.ds(c * n + y_ * w, w)]

        def band_a(y_):
            return wout.at[q, :, pl.ds(0, UPPER_OUT), pl.ds(c * n + y_ * w, w)]

        def band_b(x_):
            return wout.at[q, x_, pl.ds(UPPER_OUT, BLK - UPPER_OUT), pl.ds(c * n, n)]

        own = wout_in.at[:, pl.ds(q * w, w)]
        copy = pltpu.make_async_copy(own, block(x, y, pl.ds(0, BLK)), lsem.at[5 + q])
        copy.start()
        return WeightGather(s, own, block, band_a, band_b, UPPER_OUT, False), copy

    (g0, own0), (g1, own1), (g2, own2) = [out_gather(q) for q in range(3)]

    for copy in locals_:
        copy.wait()
    own_par[0:27, :] = tp[...]
    own_par[27:28, :] = b1[...].reshape(1, BLK)
    own_par[28:29, :] = cb1[...].reshape(1, BLK)

    greet(
        [(dev(y, c, xs[d], z), None) for d in (1, 2, 3)]
        + [(dev(yp, c, x, z), None), (dev(ym, c, x, z), None)]
        + [(dev(y, c, x, zp), None), (dev(y, c, x, zm), None)]
        + [(dev(y, 1 - c, x, z), None)]
        + [(dev(y, tc, tx, z), moves), (dev(y, fc, fx, z), moves)]
        + [(nxt, has_next), (nxt_other, has_next), (prv, has_prev), (prv_other, has_prev)]
        + [(other_half, None)]
    )

    def tok_at(z_, p):
        return tok.at[pl.ds(((z_ + NZ) % NZ) * OWN + p * PIECE, PIECE)]

    home = []
    for p in range(PIECES):
        src = tok_in.at[pl.ds(p * PIECE, PIECE)]
        k = s.send(src, tok_at(z, p), dev(y, tc, tx, z), when=moves)
        stay = pltpu.make_async_copy(src, tok_at(z, p), rsem.at[k])
        pl.when(stays)(stay.start)
        home.append(stay)
    g_in.p0()

    @pl.when(upper == 0)
    def _():
        ext[:, 0] = jnp.zeros((3, WW, CH), BF16)

    @pl.when(upper == 1)
    def _():
        ext[:, ROWS + 1] = jnp.zeros((3, WW, CH), BF16)

    @pl.when(jnp.logical_not(has_prev))
    def _():
        @pl.loop(0, ROWS + 2)
        def _(r):
            ext[0, r] = jnp.zeros((WW, CH), BF16)

    @pl.when(jnp.logical_not(has_next))
    def _():
        @pl.loop(0, ROWS + 2)
        def _(r):
            ext[2, r] = jnp.zeros((WW, CH), BF16)

    k_tok = {}

    def token_step(d):
        for p in range(PIECES):
            if d == 1:
                home[p].wait()
            for way, to in ((1, zp), (-1, zm)):
                if d == 4 and (p < PIECES // 2) != (way == 1):
                    continue
                src = tok_at(z - way * (d - 1), p)
                if d > 1:
                    s.arrived(src, k_tok[way, d - 1, p])
                k_tok[way, d, p] = s.send(src, src, dev(y, c, x, to))

    def par_at(x_):
        return par.at[:, pl.ds(x_ * BLK, BLK)]

    token_step(1)
    g_in.p1y()
    k_par = [s.send(own_par, par_at(x), dev(y, c, xs[d], z)) for d in (1, 2, 3)]
    own_copy = pltpu.make_async_copy(own_par, par_at(x), lsem.at[8])
    own_copy.start()
    token_step(2)
    g_in.p1x()
    own_in.wait()
    g_in.p2y()
    token_step(3)
    g_in.p2x()
    token_step(4)
    g_in.p3()
    own0.wait()
    own1.wait()
    own2.wait()
    g0.p0()
    g1.p0()
    g2.p0()
    own_copy.wait()
    for d in (1, 2, 3):
        s.arrived(par_at((x + NX - d) % NX), k_par[d - 1])
    g_in.p4()
    for p in range(PIECES):
        way = -1 if p < PIECES // 2 else 1
        s.arrived(tok_at(z - way * 3, p), k_tok[way, 3, p])
        s.arrived(tok_at(z + 4, p), k_tok[-way, 4, p])
    g0.p1y()
    g0.p1x()
    g_in.finish()

    src_row = jnp.where(upper == 0, ROWS, 1)
    dst_row = jnp.where(upper == 0, 0, ROWS + 1)
    got_row = jnp.where(upper == 0, ROWS + 1, 0)
    inner = pl.ds(1, ROWS)
    arrivals = []
    step = 256
    for j in range(HALO_CHUNKS):

        @pl.loop(0, HALO_CH // step)
        def _(i):
            cols = pl.ds(pl.multiple_of(j * HALO_CH + i * step, step), step)
            w = win[:, :, :, cols].reshape(D, step)
            before = jnp.dot(tok[...], w, preferred_element_type=F32) + par[27:28, cols]
            ext[1, inner, :, cols] = before.astype(BF16).reshape(ROWS, WW, step)

        cols = pl.ds(j * HALO_CH, HALO_CH)
        frame_src = ext.at[1, inner, :, cols]
        row_src = ext.at[1, src_row, :, cols]
        k1 = s.send(frame_src, ext.at[0, inner, :, cols], nxt, when=has_next)
        k2 = s.send(frame_src, ext.at[2, inner, :, cols], prv, when=has_prev)
        k3 = s.send(row_src, ext.at[1, dst_row, :, cols], other_half)
        k4 = s.send(row_src, ext.at[0, dst_row, :, cols], nxt_other, when=has_next)
        k5 = s.send(row_src, ext.at[2, dst_row, :, cols], prv_other, when=has_prev)
        arrivals.append([
            (ext.at[0, inner, :, cols], k1, has_prev),
            (ext.at[2, inner, :, cols], k2, has_next),
            (ext.at[1, got_row, :, cols], k3, None),
            (ext.at[0, got_row, :, cols], k4, has_prev),
            (ext.at[2, got_row, :, cols], k5, has_next),
        ])
        if j == 0:
            g0.p2y()
            g0.p2x()

    column = lax.broadcasted_iota(jnp.int32, (WW, 128), 0)

    def conv(j):
        for copy in arrivals[j]:
            s.arrived(*copy)

        @pl.loop(0, HALO_CH // 128)
        def _(i):
            lanes = pl.ds(pl.multiple_of(j * HALO_CH + i * 128, 128), 128)

            @pl.loop(0, ROWS)
            def _(r):
                sums = [None, None, None]
                for dt in range(3):
                    for dh in range(3):
                        v = ext[dt, r + dh, :, lanes].astype(F32)
                        for dw in range(3):
                            k = 9 * dt + 3 * dh + dw
                            t = v * par[k : k + 1, lanes]
                            sums[dw] = t if sums[dw] is None else sums[dw] + t
                left = jnp.where(column == 0, 0.0, pltpu.roll(sums[0], 1, 0))
                right = jnp.where(column == WW - 1, 0.0, pltpu.roll(sums[2], WW - 1, 0))
                v = sums[1] + left + right + par[28:29, lanes]
                half = 0.5 * v
                t = jnp.tanh(v * (0.7978845608028654 + 0.035677408136300125 * (v * v)))
                act[pl.ds(pl.multiple_of(r * WW, WW), WW), lanes] = (half + half * t).astype(BF16)

    conv(0)
    g0.p3()
    g1.p1y()
    g1.p1x()
    conv(1)
    g0.p4()
    g2.p1y()
    g2.p1x()
    g1.p2y()
    g1.p2x()
    conv(2)
    g0.finish()

    units = D // UNIT
    chains = [
        (u, way, 4 if (u % 2 == 0) == (way == 1) else 3) for u in range(units) for way in (1, -1)
    ]
    slot, n = {}, 0
    for i, (u, way, length) in enumerate(chains):
        for st in range(length):
            slot[i, st] = n
            n += 1
    k_of = {}

    def multiply(q):
        @pl.loop(0, 1024 // 256)
        def _(i):
            cols = pl.ds(pl.multiple_of(i * 256, 256), 256)
            w = wout[q, :, :, cols].reshape(CH, 256)
            part[2 * q + i // 2, :, pl.ds(pl.multiple_of(i % 2 * 256, 256), 256)] = jnp.dot(act[...], w, preferred_element_type=F32)

    def pass_on(u, st):
        for i, (u_, way, length) in enumerate(chains):
            if u_ != u or st >= length:
                continue
            at = (z + way * (length - st) + NZ) % NZ
            rows = pl.ds(pl.multiple_of(at * OWN, OWN), OWN)
            value = part[u, rows, :]
            if st > 0:
                got = recvbuf.at[slot[i, st - 1]]
                s.arrived(got, k_of[i, st - 1])
                value = value + got[...].astype(F32)
            mine = slot[i, st]
            sendbuf[mine] = value.astype(BF16)
            to = dev(y, c, x, zp if way == 1 else zm)
            k_of[i, st] = s.send(sendbuf.at[mine], recvbuf.at[mine], to)

    back = []

    w = BLK // 3

    def collect(u):
        rows = pl.ds(pl.multiple_of(z * OWN, OWN), OWN)
        value = part[u, rows, :]
        for i in (2 * u, 2 * u + 1):
            mine = slot[i, chains[i][2] - 1]
            s.arrived(recvbuf.at[mine], k_of[i, chains[i][2] - 1])
            value = value + recvbuf[mine].astype(F32)
        for n_ in range(NY):
            lo = (n_ * 2 + u % 2) * BLK + u // 2 * w
            summed[u, :, n_ * w : (n_ + 1) * w] = (
                value[:, n_ * w : (n_ + 1) * w] + bout[lo : lo + w].reshape(1, w)
            ).astype(BF16)
        k = s.send(summed.at[u], moved.at[u], dev(y, fc, fx, z), when=moves)
        stay = pltpu.make_async_copy(summed.at[u], moved.at[u], rsem.at[k])
        pl.when(stays)(stay.start)
        back.append(stay)

    def put(u):
        back[u].wait()
        for n_ in range(NY):
            lo = (n_ * 2 + u % 2) * BLK + u // 2 * w
            done[:, lo : lo + w] = moved[u, :, n_ * w : (n_ + 1) * w]

    def hop(q, st):
        pass_on(2 * q, st)
        pass_on(2 * q + 1, st)

    own_bout.wait()
    multiply(0)
    hop(0, 0)
    g1.p3()
    g2.p2y()
    g2.p2x()
    g1.p4()
    hop(0, 1)
    g1.finish()
    multiply(1)
    hop(1, 0)
    g2.p3()
    hop(0, 2)
    g2.p4()
    hop(1, 1)
    g2.finish()
    multiply(2)
    hop(2, 0)
    hop(0, 3)
    hop(2, 1)
    hop(1, 2)
    collect(0)
    collect(1)
    hop(2, 2)
    hop(1, 3)
    put(0)
    put(1)
    hop(2, 3)
    collect(2)
    collect(3)
    collect(4)
    collect(5)
    put(2)
    put(3)
    put(4)
    put(5)
    stored = pltpu.make_async_copy(done, out, lsem.at[9])
    stored.start()
    stored.wait()
    s.drain()


def body(tokens, w_in, b_in, conv_taps, conv_bias, w_out, b_out):
    keys = 300
    hbm = pl.BlockSpec(memory_space=pl.ANY)
    return pl.pallas_call(
        block_kernel,
        out_shape=jax.ShapeDtypeStruct((OWN, D), BF16),
        in_specs=[hbm] * 7,
        out_specs=hbm,
        scratch_shapes=[
            pltpu.VMEM((GROUP, D), BF16),
            pltpu.VMEM((NY, 2, BLK, CH), BF16),
            pltpu.VMEM((3, NX, BLK, 2 * UNIT), BF16),
            pltpu.VMEM((3, ROWS + 2, WW, CH), BF16),
            pltpu.VMEM((GROUP, CH), BF16),
            pltpu.VMEM((6, GROUP, UNIT), F32),
            pltpu.VMEM((32, BLK), F32),
            pltpu.VMEM((32, CH), F32),
            pltpu.VMEM((27, BLK), F32),
            pltpu.VMEM((BLK,), F32),
            pltpu.VMEM((BLK,), F32),
            pltpu.VMEM((D,), F32),
            pltpu.VMEM((42, OWN, UNIT), BF16),
            pltpu.VMEM((42, OWN, UNIT), BF16),
            pltpu.VMEM((6, OWN, UNIT), BF16),
            pltpu.VMEM((6, OWN, UNIT), BF16),
            pltpu.VMEM((OWN, D), BF16),
            pltpu.SemaphoreType.DMA((10,)),
            pltpu.SemaphoreType.DMA((keys,)),
            pltpu.SemaphoreType.DMA((keys,)),
        ],
        compiler_params=pltpu.CompilerParams(
            collective_id=0, has_side_effects=True, vmem_limit_bytes=60 * 2**20
        ),
        name="mix_ffn",
    )(tokens, w_in, b_in, conv_taps, conv_bias, w_out, b_out)


def solution(mesh):
    placed = (
        P(("row", "col"), None),
        P("row", "col"),
        P("col"),
        P(None, "col"),
        P("col"),
        P("col", "row"),
        P(),
    )
    return jax.shard_map(
        body, mesh=mesh, in_specs=placed, out_specs=P(("row", "col"), None), check_vma=False
    )
```

```python
import functools

import jax
import jax.numpy as jnp
from jax import lax
from jax.experimental import pallas as pl
from jax.experimental.pallas import tpu as pltpu
from jax.sharding import PartitionSpec as P

MESH = pl.DeviceIdType.MESH
NX, NY, NZ = 4, 4, 8
D = 3072
BLK = 384
UPPER_IN = 192
UPPER_OUT = 192
CH = NX * BLK
GROUP = 512
OWN = 64
WW = 32
ROWS = GROUP // WW
HALO_CHUNKS = 3
PIECES = 4
PIECE = OWN // PIECES
UNIT = 512
HALO_CH = CH // HALO_CHUNKS
BF16, F32 = jnp.bfloat16, jnp.float32


def place():
    row, col = lax.axis_index("row"), lax.axis_index("col")
    return row // 2, row % 2, col // NZ, col % NZ


def dev(y, c, x, z):
    return {"row": y * 2 + c, "col": x * NZ + z}


def moved_to(y, c, x):
    b = c ^ (y & 1)
    upper = x & 1
    return x >> 1, jnp.where(upper == 0, b, 3 - b)


def moved_from(y, c, x):
    b = (x ^ (x >> 1)) & 1
    return b ^ (y & 1), c * 2 + (x >> 1)


def frame_of(y, c, x):
    b = (x ^ (x >> 1)) & 1
    return 4 * y + 2 * (b ^ (y & 1)) + c


def holder(frame, upper):
    pair = frame >> 1
    y = pair >> 1
    b = (pair & 1) ^ (y & 1)
    return y, frame & 1, jnp.where(upper == 0, b, 3 - b)


class Sender:
    def __init__(self, ssem, rsem):
        self.ssem, self.rsem, self.used, self.sent = ssem, rsem, 0, []

    def key(self):
        self.used += 1
        return self.used - 1

    def make(self, src, dst, k, to):
        return pltpu.make_async_remote_copy(
            src_ref=src,
            dst_ref=dst,
            send_sem=self.ssem.at[k],
            recv_sem=self.rsem.at[k],
            device_id=to,
            device_id_type=MESH,
        )

    def send(self, src, dst, to, when=None):
        k = self.key()
        copy = self.make(src, dst, k, to)
        if when is None:
            copy.start()
        else:
            pl.when(when)(copy.start)
        self.sent.append((copy, when))
        return k

    def arrived(self, ref, k, when=None):
        copy = pltpu.make_async_copy(ref, ref, self.rsem.at[k])
        if when is None:
            copy.wait()
        else:
            pl.when(when)(copy.wait)

    def drain(self):
        for copy, when in self.sent:
            if when is None:
                copy.wait_send()
            else:
                pl.when(when)(copy.wait_send)
        self.sent = []


def greet(peers):
    barrier = pltpu.get_barrier_semaphore()
    count = 0
    for to, when in peers:
        signal = functools.partial(pl.semaphore_signal, barrier, inc=1, device_id=to, device_id_type=MESH)
        if when is None:
            signal()
            count = count + 1
        else:
            pl.when(when)(signal)
            count = count + when.astype(jnp.int32)
    pl.semaphore_wait(barrier, count)


class WeightGather:
    def __init__(self, sender, own, block, band_a, band_b, upper, fine):
        self.fine = fine
        self.s, self.own = sender, own
        self.h, self.qa, self.qb = upper, upper // 2, upper + (BLK - upper) // 2
        self.block, self.band_a, self.band_b = block, band_a, band_b
        self.y, self.c, self.x, self.z = place()
        y, c, x, z = self.y, self.c, self.x, self.z
        self.xs = {"0": x, "+": (x + 1) % NX, "-": (x + NX - 1) % NX, "2": (x + 2) % NX}
        self.ys = {"0": y, "+": (y + 1) % NY, "-": (y + NY - 1) % NY, "2": (y + 2) % NY}
        self.to = {
            "x+": dev(y, c, self.xs["+"], z),
            "x-": dev(y, c, self.xs["-"], z),
            "y+": dev(self.ys["+"], c, x, z),
            "y-": dev(self.ys["-"], c, x, z),
        }
        self.keys, self.from_partner = {}, []

    def at(self, place_, lo, hi):
        return self.block(self.xs[place_[0]], self.ys[place_[1]], pl.ds(lo, hi - lo))

    def push(self, place_, lo, hi, way):
        src = self.at(place_, lo, hi)
        self.keys[place_, lo, hi, way] = self.s.send(src, src, self.to[way])

    def pull(self, here, lo, hi, way, there):
        self.s.arrived(self.at(here, lo, hi), self.keys[there, lo, hi, way])

    def p0(self):
        h = self.h
        for lo, hi, ways in ((0, BLK, ("y+", "y-")), (0, h, ("x+", "x-")), (h, BLK, ("x+", "x-"))):
            for way in ways:
                src = self.own.at[pl.ds(lo, hi - lo)]
                self.keys["00", lo, hi, way] = self.s.send(src, self.at("00", lo, hi), self.to[way])
        if self.fine:
            other = dev(self.y, 1 - self.c, self.x, self.z)
            here = self.at("00", 0, BLK)
            self.from_partner.append((here, self.s.send(self.own, here, other)))

    def p1y(self):
        h, qa, qb = self.h, self.qa, self.qb
        self.pull("0-", 0, BLK, "y+", "00")
        self.push("0-", 0, qb, "y+")
        self.push("0-", h, BLK, "x+")
        self.push("0-", h, BLK, "x-")
        self.across("0-", 0, BLK)
        self.pull("0+", 0, BLK, "y-", "00")
        self.push("0+", qb, BLK, "y-")
        self.push("0+", h, BLK, "x+")
        self.push("0+", h, BLK, "x-")
        self.across("0+", 0, BLK)

    def p1x(self):
        h, qa, qb = self.h, self.qa, self.qb
        self.pull("-0", 0, h, "x+", "00")
        self.push("-0", qa, h, "x+")
        self.push("-0", 0, h, "y+")
        self.push("-0", 0, h, "y-")
        self.across("-0", 0, h)
        self.pull("+0", 0, h, "x-", "00")
        self.push("+0", 0, qa, "x-")
        self.push("+0", 0, h, "y+")
        self.push("+0", 0, h, "y-")
        self.across("+0", 0, h)

    def p2y(self):
        h, qa, qb = self.h, self.qa, self.qb
        self.pull("02", 0, qb, "y+", "0-")
        self.pull("02", qb, BLK, "y-", "0+")
        self.push("02", h, BLK, "x-")
        self.push("02", h, BLK, "x+")
        self.across("02", 0, BLK)
        self.pull("--", 0, h, "y+", "-0")
        self.push("--", 0, h, "y+")
        self.across("--", 0, h)
        self.pull("++", 0, h, "y-", "+0")
        self.push("++", 0, h, "y-")
        self.across("++", 0, h)

    def p2x(self):
        h, qa, qb = self.h, self.qa, self.qb
        self.pull("20", qa, h, "x+", "-0")
        self.pull("20", 0, qa, "x-", "+0")
        self.push("20", 0, h, "y-")
        self.push("20", 0, h, "y+")
        self.across("20", 0, h)
        self.pull("-0", h, BLK, "x+", "00")
        self.push("-0", h, BLK, "x+")
        self.across("-0", h, BLK)
        self.pull("+0", h, BLK, "x-", "00")
        self.across("+0", h, BLK)
        self.pull("--", h, BLK, "x+", "0-")
        self.push("--", h, BLK, "x+")
        self.across("--", h, BLK)
        self.pull("++", h, BLK, "x-", "0+")
        self.push("++", h, BLK, "x-")
        self.across("++", h, BLK)
        self.partner("0", "0")

    def p3(self):
        h = self.h
        self.pull("2+", 0, h, "y-", "20")
        self.push("2+", 0, h, "y-")
        self.across("2+", 0, h)
        self.pull("+2", h, BLK, "x-", "02")
        self.push("+2", h, BLK, "x-")
        self.across("+2", h, BLK)
        for here, lo, hi, way, there in (
            ("+-", 0, h, "y+", "+0"),
            ("-+", 0, h, "y-", "-0"),
            ("-+", h, BLK, "x+", "0+"),
            ("+-", h, BLK, "x-", "0-"),
            ("2-", 0, h, "y+", "20"),
            ("-2", h, BLK, "x+", "02"),
        ):
            self.pull(here, lo, hi, way, there)
            self.across(here, lo, hi)
        self.partner("-", "-")
        self.partner("+", "+")

    def p4(self):
        h = self.h
        for here, lo, hi, way, there in (
            ("20", h, BLK, "x+", "-0"),
            ("-2", 0, h, "y+", "--"),
            ("2-", h, BLK, "x+", "--"),
            ("+2", 0, h, "y-", "++"),
            ("2+", h, BLK, "x-", "++"),
            ("22", 0, h, "y-", "2+"),
            ("22", h, BLK, "x-", "+2"),
        ):
            self.pull(here, lo, hi, way, there)
            self.across(here, lo, hi)
        self.partner("2", "2")

    def across(self, here, lo, hi):
        if not self.fine:
            return
        other = dev(self.y, 1 - self.c, self.x, self.z)
        ref = self.at(here, lo, hi)
        self.from_partner.append((ref, self.s.send(ref, ref, other)))

    def partner(self, x, y):
        if self.fine:
            return
        other = dev(self.y, 1 - self.c, self.x, self.z)
        a, b = self.band_a(self.ys[y]), self.band_b(self.xs[x])
        self.from_partner.append((a, self.s.send(a, a, other)))
        self.from_partner.append((b, self.s.send(b, b, other)))

    def finish(self):
        for ref, k in self.from_partner:
            self.s.arrived(ref, k)


class SkewGather(WeightGather):
    def __init__(self, *rest):
        super().__init__(*rest)
        y, c, x, z = self.y, self.c, self.x, self.z
        to_next = ((x ^ (x >> 1)) ^ y) & 1
        even = 1 - (x & 1)
        step_x, step_y = 2 * even - 1, 2 * to_next - 1
        self.xs["L"], self.xs["U"] = (x + NX + step_x) % NX, (x + NX - step_x) % NX
        self.ys["L"], self.ys["U"] = (y + NY + step_y) % NY, (y + NY - step_y) % NY
        self.to = {
            "xL": dev(y, c, self.xs["L"], z),
            "xU": dev(y, c, self.xs["U"], z),
            "yL": dev(self.ys["L"], c, x, z),
            "yU": dev(self.ys["U"], c, x, z),
        }

    def p0(self):
        for way in ("yL", "yU", "xL", "xU"):
            self.keys["00", 0, BLK, way] = self.s.send(self.own, self.at("00", 0, BLK), self.to[way])

    def p1y(self):
        h = self.h
        self.pull("0L", 0, BLK, "yL", "00")
        self.push("0L", 0, BLK, "yU")
        self.pull("0U", 0, BLK, "yU", "00")
        for block in ("0+", "0-"):
            self.push(block, h, BLK, "xL")
            self.push(block, h, BLK, "xU")

    def p1x(self):
        h = self.h
        self.pull("L0", 0, BLK, "xL", "00")
        self.push("L0", 0, BLK, "xU")
        self.push("L0", 0, h, "yL")
        self.push("L0", 0, h, "yU")
        self.pull("U0", 0, BLK, "xU", "00")
        self.push("U0", 0, h, "yL")
        self.push("U0", 0, h, "yU")

    def p2y(self):
        h = self.h
        self.pull("02", 0, BLK, "yU", "0L")
        self.push("02", h, BLK, "xL")
        self.push("02", h, BLK, "xU")
        self.pull("LL", 0, h, "yL", "L0")
        self.push("LL", 0, h, "yU")
        self.pull("UL", 0, h, "yL", "U0")
        self.push("UL", 0, h, "yU")

    def p2x(self):
        h = self.h
        self.pull("20", 0, BLK, "xU", "L0")
        self.push("20", 0, h, "yL")
        self.push("20", 0, h, "yU")
        self.pull("L+", h, BLK, "xL", "0+")
        self.push("L+", h, BLK, "xU")
        self.pull("L-", h, BLK, "xL", "0-")
        self.push("L-", h, BLK, "xU")
        self.partner("0", "0")

    def p3(self):
        h = self.h
        self.pull("2L", 0, h, "yL", "20")
        self.push("2L", 0, h, "yU")
        self.pull("L2", h, BLK, "xL", "02")
        self.push("L2", h, BLK, "xU")
        self.pull("LU", 0, h, "yU", "L0")
        self.pull("UU", 0, h, "yU", "U0")
        self.pull("2U", 0, h, "yU", "20")
        self.pull("U+", h, BLK, "xU", "0+")
        self.pull("U-", h, BLK, "xU", "0-")
        self.pull("U2", h, BLK, "xU", "02")
        self.partner("L", "L")
        self.partner("U", "U")

    def p4(self):
        h = self.h
        self.pull("L2", 0, h, "yU", "LL")
        self.pull("2+", h, BLK, "xU", "L+")
        self.pull("U2", 0, h, "yU", "UL")
        self.pull("2-", h, BLK, "xU", "L-")
        self.pull("22", 0, h, "yU", "2L")
        self.pull("22", h, BLK, "xU", "L2")
        self.partner("2", "2")


def block_kernel(
    tok_in, win_in, bin_in, taps_in, cbias_in, wout_in, bout_in, out,
    tok, win, wout, ext, act, part, own_par, par, tp, b1, cb1, bout, sendbuf, recvbuf, summed, moved, done,
    lsem, ssem, rsem,
):
    y, c, x, z = place()
    s = Sender(ssem, rsem)
    xs = [(x + d) % NX for d in range(NX)]
    zp, zm = (z + 1) % NZ, (z + NZ - 1) % NZ
    yp, ym = (y + 1) % NY, (y + NY - 1) % NY
    upper = x >> 1
    frame = frame_of(y, c, x)
    last = NY * 4 - 1
    tc, tx = moved_to(y, c, x)
    fc, fx = moved_from(y, c, x)
    stays = (tc == c) & (tx == x)
    moves = jnp.logical_not(stays)
    has_next, has_prev = frame < last, frame > 0
    ny, nc, nx = holder(jnp.minimum(frame + 1, last), upper)
    py, pc, px = holder(jnp.maximum(frame - 1, 0), upper)
    nxt, nxt_other = dev(ny, nc, nx, z), dev(ny, nc, 3 - nx, z)
    prv, prv_other = dev(py, pc, px, z), dev(py, pc, 3 - px, z)
    other_half = dev(y, c, 3 - x, z)

    locals_ = [
        pltpu.make_async_copy(taps_in, tp, lsem.at[0]),
        pltpu.make_async_copy(bin_in, b1, lsem.at[1]),
        pltpu.make_async_copy(cbias_in, cb1, lsem.at[2]),
    ]
    own_bout = pltpu.make_async_copy(bout_in, bout, lsem.at[3])
    for copy in locals_ + [own_bout]:
        copy.start()

    def win_block(x_, y_, rows):
        return win.at[y_, c, rows, pl.ds(x_ * BLK, BLK)]

    def win_a(y_):
        return win.at[y_, c, pl.ds(0, UPPER_IN), :]

    def win_b(x_):
        return win.at[:, c, pl.ds(UPPER_IN, BLK - UPPER_IN), pl.ds(x_ * BLK, BLK)]

    g_in = WeightGather(s, win_in, win_block, win_a, win_b, UPPER_IN, True)
    own_in = pltpu.make_async_copy(win_in, win_block(x, y, pl.ds(0, BLK)), lsem.at[4])
    own_in.start()

    def out_gather(q):
        w = BLK // 3
        n = NY * w

        def block(x_, y_, rows):
            return wout.at[q, x_, rows, pl.ds(c * n + y_ * w, w)]

        def band_a(y_):
            return wout.at[q, :, pl.ds(0, UPPER_OUT), pl.ds(c * n + y_ * w, w)]

        def band_b(x_):
            return wout.at[q, x_, pl.ds(UPPER_OUT, BLK - UPPER_OUT), pl.ds(c * n, n)]

        own = wout_in.at[:, pl.ds(q * w, w)]
        copy = pltpu.make_async_copy(own, block(x, y, pl.ds(0, BLK)), lsem.at[5 + q])
        copy.start()
        return SkewGather(s, own, block, band_a, band_b, UPPER_OUT, False), copy

    (g0, own0), (g1, own1), (g2, own2) = [out_gather(q) for q in range(3)]

    for copy in locals_:
        copy.wait()
    own_par[0:27, :] = tp[...]
    own_par[27:28, :] = b1[...].reshape(1, BLK)
    own_par[28:29, :] = cb1[...].reshape(1, BLK)

    greet(
        [(dev(y, c, xs[d], z), None) for d in (1, 2, 3)]
        + [(dev(yp, c, x, z), None), (dev(ym, c, x, z), None)]
        + [(dev(y, c, x, zp), None), (dev(y, c, x, zm), None)]
        + [(dev(y, 1 - c, x, z), None)]
        + [(dev(y, tc, tx, z), moves), (dev(y, fc, fx, z), moves)]
        + [(nxt, has_next), (nxt_other, has_next), (prv, has_prev), (prv_other, has_prev)]
        + [(other_half, None)]
    )

    def tok_at(z_, p):
        return tok.at[pl.ds(((z_ + NZ) % NZ) * OWN + p * PIECE, PIECE)]

    home = []
    for p in range(PIECES):
        src = tok_in.at[pl.ds(p * PIECE, PIECE)]
        k = s.send(src, tok_at(z, p), dev(y, tc, tx, z), when=moves)
        stay = pltpu.make_async_copy(src, tok_at(z, p), rsem.at[k])
        pl.when(stays)(stay.start)
        home.append(stay)
    g_in.p0()

    @pl.when(upper == 0)
    def _():
        ext[:, 0] = jnp.zeros((3, WW, CH), BF16)

    @pl.when(upper == 1)
    def _():
        ext[:, ROWS + 1] = jnp.zeros((3, WW, CH), BF16)

    @pl.when(jnp.logical_not(has_prev))
    def _():
        @pl.loop(0, ROWS + 2)
        def _(r):
            ext[0, r] = jnp.zeros((WW, CH), BF16)

    @pl.when(jnp.logical_not(has_next))
    def _():
        @pl.loop(0, ROWS + 2)
        def _(r):
            ext[2, r] = jnp.zeros((WW, CH), BF16)

    k_tok = {}

    def token_step(d):
        for p in range(PIECES):
            if d == 1:
                home[p].wait()
            for way, to in ((1, zp), (-1, zm)):
                if d == 4 and (p < PIECES // 2) != (way == 1):
                    continue
                src = tok_at(z - way * (d - 1), p)
                if d > 1:
                    s.arrived(src, k_tok[way, d - 1, p])
                k_tok[way, d, p] = s.send(src, src, dev(y, c, x, to))

    def par_at(x_):
        return par.at[:, pl.ds(x_ * BLK, BLK)]

    token_step(1)
    g_in.p1y()
    k_par = [s.send(own_par, par_at(x), dev(y, c, xs[d], z)) for d in (1, 2, 3)]
    own_copy = pltpu.make_async_copy(own_par, par_at(x), lsem.at[8])
    own_copy.start()
    token_step(2)
    g_in.p1x()
    own_in.wait()
    g_in.p2y()
    token_step(3)
    g_in.p2x()
    token_step(4)
    g_in.p3()
    own0.wait()
    own1.wait()
    own2.wait()
    g0.p0()
    g1.p0()
    g2.p0()
    own_copy.wait()
    for d in (1, 2, 3):
        s.arrived(par_at((x + NX - d) % NX), k_par[d - 1])
    g_in.p4()
    for p in range(PIECES):
        way = -1 if p < PIECES // 2 else 1
        s.arrived(tok_at(z - way * 3, p), k_tok[way, 3, p])
        s.arrived(tok_at(z + 4, p), k_tok[-way, 4, p])
    g0.p1y()
    g0.p1x()
    g_in.finish()

    src_row = jnp.where(upper == 0, ROWS, 1)
    dst_row = jnp.where(upper == 0, 0, ROWS + 1)
    got_row = jnp.where(upper == 0, ROWS + 1, 0)
    inner = pl.ds(1, ROWS)
    arrivals = []
    step = 256
    for j in range(HALO_CHUNKS):

        @pl.loop(0, HALO_CH // step)
        def _(i):
            cols = pl.ds(pl.multiple_of(j * HALO_CH + i * step, step), step)
            w = win[:, :, :, cols].reshape(D, step)
            before = jnp.dot(tok[...], w, preferred_element_type=F32) + par[27:28, cols]
            ext[1, inner, :, cols] = before.astype(BF16).reshape(ROWS, WW, step)

        cols = pl.ds(j * HALO_CH, HALO_CH)
        frame_src = ext.at[1, inner, :, cols]
        row_src = ext.at[1, src_row, :, cols]
        k1 = s.send(frame_src, ext.at[0, inner, :, cols], nxt, when=has_next)
        k2 = s.send(frame_src, ext.at[2, inner, :, cols], prv, when=has_prev)
        k3 = s.send(row_src, ext.at[1, dst_row, :, cols], other_half)
        k4 = s.send(row_src, ext.at[0, dst_row, :, cols], nxt_other, when=has_next)
        k5 = s.send(row_src, ext.at[2, dst_row, :, cols], prv_other, when=has_prev)
        arrivals.append([
            (ext.at[0, inner, :, cols], k1, has_prev),
            (ext.at[2, inner, :, cols], k2, has_next),
            (ext.at[1, got_row, :, cols], k3, None),
            (ext.at[0, got_row, :, cols], k4, has_prev),
            (ext.at[2, got_row, :, cols], k5, has_next),
        ])
        if j == 0:
            g0.p2y()
            g0.p2x()

    column = lax.broadcasted_iota(jnp.int32, (WW, 128), 0)

    def conv(j):
        for copy in arrivals[j]:
            s.arrived(*copy)

        @pl.loop(0, HALO_CH // 128)
        def _(i):
            lanes = pl.ds(pl.multiple_of(j * HALO_CH + i * 128, 128), 128)

            @pl.loop(0, ROWS, step=2)
            def _(r):
                sums = [[None] * 3 for _ in range(2)]
                for dt in range(3):
                    for dr in range(2 + 2):
                        v = ext[dt, r + dr, :, lanes].astype(F32)
                        for row in range(2):
                            dh = dr - row
                            if not 0 <= dh < 3:
                                continue
                            for dw in range(3):
                                k = 9 * dt + 3 * dh + dw
                                t = v * par[k : k + 1, lanes]
                                old = sums[row][dw]
                                sums[row][dw] = t if old is None else old + t
                for row in range(2):
                    left = jnp.where(column == 0, 0.0, pltpu.roll(sums[row][0], 1, 0))
                    right = jnp.where(column == WW - 1, 0.0, pltpu.roll(sums[row][2], WW - 1, 0))
                    v = sums[row][1] + left + right + par[28:29, lanes]
                    half = 0.5 * v
                    t = jnp.tanh(v * (0.7978845608028654 + 0.035677408136300125 * (v * v)))
                    to = pl.ds(pl.multiple_of((r + row) * WW, WW), WW)
                    act[to, lanes] = (half + half * t).astype(BF16)

    conv(0)
    g0.p3()
    g1.p1y()
    g1.p1x()
    conv(1)
    g0.p4()
    g2.p1y()
    g2.p1x()
    conv(2)
    g1.p2y()
    g1.p2x()
    g0.finish()

    units = D // UNIT
    chains = [
        (u, way, 4 if (u % 2 == 0) == (way == 1) else 3) for u in range(units) for way in (1, -1)
    ]
    slot, n = {}, 0
    for i, (u, way, length) in enumerate(chains):
        for st in range(length):
            slot[i, st] = n
            n += 1
    k_of = {}

    def multiply(q):
        @pl.loop(0, 1024 // 256)
        def _(i):
            cols = pl.ds(pl.multiple_of(i * 256, 256), 256)
            w = wout[q, :, :, cols].reshape(CH, 256)
            part[2 * q + i // 2, :, pl.ds(pl.multiple_of(i % 2 * 256, 256), 256)] = jnp.dot(act[...], w, preferred_element_type=F32)

    def pass_on(u, st):
        for i, (u_, way, length) in enumerate(chains):
            if u_ != u or st >= length:
                continue
            at = (z + way * (length - st) + NZ) % NZ
            rows = pl.ds(pl.multiple_of(at * OWN, OWN), OWN)
            value = part[u, rows, :]
            if st > 0:
                got = recvbuf.at[slot[i, st - 1]]
                s.arrived(got, k_of[i, st - 1])
                value = value + got[...].astype(F32)
            mine = slot[i, st]
            sendbuf[mine] = value.astype(BF16)
            to = dev(y, c, x, zp if way == 1 else zm)
            k_of[i, st] = s.send(sendbuf.at[mine], recvbuf.at[mine], to)

    back = []

    w = BLK // 3

    def collect(u):
        rows = pl.ds(pl.multiple_of(z * OWN, OWN), OWN)
        value = part[u, rows, :]
        for i in (2 * u, 2 * u + 1):
            mine = slot[i, chains[i][2] - 1]
            s.arrived(recvbuf.at[mine], k_of[i, chains[i][2] - 1])
            value = value + recvbuf[mine].astype(F32)
        for n_ in range(NY):
            lo = (n_ * 2 + u % 2) * BLK + u // 2 * w
            summed[u, :, n_ * w : (n_ + 1) * w] = (
                value[:, n_ * w : (n_ + 1) * w] + bout[lo : lo + w].reshape(1, w)
            ).astype(BF16)
        k = s.send(summed.at[u], moved.at[u], dev(y, fc, fx, z), when=moves)
        stay = pltpu.make_async_copy(summed.at[u], moved.at[u], rsem.at[k])
        pl.when(stays)(stay.start)
        back.append(stay)

    def put(u):
        back[u].wait()
        for n_ in range(NY):
            lo = (n_ * 2 + u % 2) * BLK + u // 2 * w
            done[:, lo : lo + w] = moved[u, :, n_ * w : (n_ + 1) * w]

    def hop(q, st):
        pass_on(2 * q, st)
        pass_on(2 * q + 1, st)

    own_bout.wait()
    multiply(0)
    hop(0, 0)
    g1.p3()
    g2.p2y()
    g2.p2x()
    g1.p4()
    hop(0, 1)
    g1.finish()
    multiply(1)
    hop(1, 0)
    g2.p3()
    hop(0, 2)
    g2.p4()
    hop(1, 1)
    g2.finish()
    multiply(2)
    hop(2, 0)
    hop(0, 3)
    hop(2, 1)
    hop(1, 2)
    collect(0)
    collect(1)
    hop(2, 2)
    hop(1, 3)
    put(0)
    put(1)
    hop(2, 3)
    collect(2)
    collect(3)
    collect(4)
    collect(5)
    put(2)
    put(3)
    put(4)
    put(5)
    stored = pltpu.make_async_copy(done, out, lsem.at[9])
    stored.start()
    stored.wait()
    s.drain()


def body(tokens, w_in, b_in, conv_taps, conv_bias, w_out, b_out):
    keys = 300
    hbm = pl.BlockSpec(memory_space=pl.ANY)
    return pl.pallas_call(
        block_kernel,
        out_shape=jax.ShapeDtypeStruct((OWN, D), BF16),
        in_specs=[hbm] * 7,
        out_specs=hbm,
        scratch_shapes=[
            pltpu.VMEM((GROUP, D), BF16),
            pltpu.VMEM((NY, 2, BLK, CH), BF16),
            pltpu.VMEM((3, NX, BLK, 2 * UNIT), BF16),
            pltpu.VMEM((3, ROWS + 2, WW, CH), BF16),
            pltpu.VMEM((GROUP, CH), BF16),
            pltpu.VMEM((6, GROUP, UNIT), F32),
            pltpu.VMEM((32, BLK), F32),
            pltpu.VMEM((32, CH), F32),
            pltpu.VMEM((27, BLK), F32),
            pltpu.VMEM((BLK,), F32),
            pltpu.VMEM((BLK,), F32),
            pltpu.VMEM((D,), F32),
            pltpu.VMEM((42, OWN, UNIT), BF16),
            pltpu.VMEM((42, OWN, UNIT), BF16),
            pltpu.VMEM((6, OWN, UNIT), BF16),
            pltpu.VMEM((6, OWN, UNIT), BF16),
            pltpu.VMEM((OWN, D), BF16),
            pltpu.SemaphoreType.DMA((10,)),
            pltpu.SemaphoreType.DMA((keys,)),
            pltpu.SemaphoreType.DMA((keys,)),
        ],
        compiler_params=pltpu.CompilerParams(
            collective_id=0, has_side_effects=True, vmem_limit_bytes=60 * 2**20
        ),
        name="mix_ffn",
    )(tokens, w_in, b_in, conv_taps, conv_bias, w_out, b_out)


def solution(mesh):
    placed = (
        P(("row", "col"), None),
        P("row", "col"),
        P("col"),
        P(None, "col"),
        P("col"),
        P("col", "row"),
        P(),
    )
    return jax.shard_map(
        body, mesh=mesh, in_specs=placed, out_specs=P(("row", "col"), None), check_vma=False
    )
```

```python
import functools

import jax
import jax.numpy as jnp
from jax import lax
from jax.experimental import pallas as pl
from jax.experimental.pallas import tpu as pltpu
from jax.sharding import PartitionSpec as P

MESH = pl.DeviceIdType.MESH
NX, NY, NZ = 4, 4, 8
D = 3072
BLK = 384
UPPER_IN = 192
UPPER_OUT = 192
CH = NX * BLK
GROUP = 512
OWN = 64
WW = 32
ROWS = GROUP // WW
CHUNKS = ((0, 512), (512, 512), (1024, 256), (1280, 256))
PIECES = 4
PIECE = OWN // PIECES
UNIT = 512
BF16, F32 = jnp.bfloat16, jnp.float32


def place():
    row, col = lax.axis_index("row"), lax.axis_index("col")
    return row // 2, row % 2, col // NZ, col % NZ


def dev(y, c, x, z):
    return {"row": y * 2 + c, "col": x * NZ + z}


def moved_to(y, c, x):
    b = c ^ (y & 1)
    upper = x & 1
    return x >> 1, jnp.where(upper == 0, b, 3 - b)


def moved_from(y, c, x):
    b = (x ^ (x >> 1)) & 1
    return b ^ (y & 1), c * 2 + (x >> 1)


def frame_of(y, c, x):
    b = (x ^ (x >> 1)) & 1
    return 4 * y + 2 * (b ^ (y & 1)) + c


def holder(frame, upper):
    pair = frame >> 1
    y = pair >> 1
    b = (pair & 1) ^ (y & 1)
    return y, frame & 1, jnp.where(upper == 0, b, 3 - b)


class Sender:
    def __init__(self, ssem, rsem):
        self.ssem, self.rsem, self.used, self.sent = ssem, rsem, 0, []

    def key(self):
        self.used += 1
        return self.used - 1

    def make(self, src, dst, k, to):
        return pltpu.make_async_remote_copy(
            src_ref=src,
            dst_ref=dst,
            send_sem=self.ssem.at[k],
            recv_sem=self.rsem.at[k],
            device_id=to,
            device_id_type=MESH,
        )

    def send(self, src, dst, to, when=None):
        k = self.key()
        copy = self.make(src, dst, k, to)
        if when is None:
            copy.start()
        else:
            pl.when(when)(copy.start)
        self.sent.append((copy, when))
        return k

    def arrived(self, ref, k, when=None):
        copy = pltpu.make_async_copy(ref, ref, self.rsem.at[k])
        if when is None:
            copy.wait()
        else:
            pl.when(when)(copy.wait)

    def drain(self):
        for copy, when in self.sent:
            if when is None:
                copy.wait_send()
            else:
                pl.when(when)(copy.wait_send)
        self.sent = []


def greet(peers):
    barrier = pltpu.get_barrier_semaphore()
    count = 0
    for to, when in peers:
        signal = functools.partial(pl.semaphore_signal, barrier, inc=1, device_id=to, device_id_type=MESH)
        if when is None:
            signal()
            count = count + 1
        else:
            pl.when(when)(signal)
            count = count + when.astype(jnp.int32)
    pl.semaphore_wait(barrier, count)


class WeightGather:
    def __init__(self, sender, own, block, band_a, band_b, upper, fine):
        self.fine = fine
        self.s, self.own = sender, own
        self.h, self.qa, self.qb = upper, upper // 2, upper + (BLK - upper) // 2
        self.block, self.band_a, self.band_b = block, band_a, band_b
        self.y, self.c, self.x, self.z = place()
        y, c, x, z = self.y, self.c, self.x, self.z
        self.xs = {"0": x, "+": (x + 1) % NX, "-": (x + NX - 1) % NX, "2": (x + 2) % NX}
        self.ys = {"0": y, "+": (y + 1) % NY, "-": (y + NY - 1) % NY, "2": (y + 2) % NY}
        self.to = {
            "x+": dev(y, c, self.xs["+"], z),
            "x-": dev(y, c, self.xs["-"], z),
            "y+": dev(self.ys["+"], c, x, z),
            "y-": dev(self.ys["-"], c, x, z),
        }
        self.keys, self.from_partner = {}, []

    def at(self, place_, lo, hi):
        return self.block(self.xs[place_[0]], self.ys[place_[1]], pl.ds(lo, hi - lo))

    def push(self, place_, lo, hi, way):
        src = self.at(place_, lo, hi)
        self.keys[place_, lo, hi, way] = self.s.send(src, src, self.to[way])

    def pull(self, here, lo, hi, way, there):
        self.s.arrived(self.at(here, lo, hi), self.keys[there, lo, hi, way])

    def p0(self):
        self.p0x(((0, BLK, ("y+", "y-")),))
        if self.fine:
            other = dev(self.y, 1 - self.c, self.x, self.z)
            here = self.at("00", 0, BLK)
            self.from_partner.append((here, self.s.send(self.own, here, other)))

    def p0x(self, parts=None):
        h = self.h
        for lo, hi, ways in parts or ((0, h, ("x+", "x-")), (h, BLK, ("x+", "x-"))):
            for way in ways:
                src = self.own.at[pl.ds(lo, hi - lo)]
                self.keys["00", lo, hi, way] = self.s.send(src, self.at("00", lo, hi), self.to[way])

    def p1y(self):
        h, qa, qb = self.h, self.qa, self.qb
        self.pull("0-", 0, BLK, "y+", "00")
        self.push("0-", 0, qb, "y+")
        self.push("0-", h, BLK, "x+")
        self.push("0-", h, BLK, "x-")
        self.across("0-", 0, BLK)
        self.pull("0+", 0, BLK, "y-", "00")
        self.push("0+", qb, BLK, "y-")
        self.push("0+", h, BLK, "x+")
        self.push("0+", h, BLK, "x-")
        self.across("0+", 0, BLK)

    def p1x(self):
        h, qa, qb = self.h, self.qa, self.qb
        self.pull("-0", 0, h, "x+", "00")
        self.push("-0", qa, h, "x+")
        self.push("-0", 0, h, "y+")
        self.push("-0", 0, h, "y-")
        self.across("-0", 0, h)
        self.pull("+0", 0, h, "x-", "00")
        self.push("+0", 0, qa, "x-")
        self.push("+0", 0, h, "y+")
        self.push("+0", 0, h, "y-")
        self.across("+0", 0, h)

    def p2y(self):
        h, qa, qb = self.h, self.qa, self.qb
        self.pull("02", 0, qb, "y+", "0-")
        self.pull("02", qb, BLK, "y-", "0+")
        self.push("02", h, BLK, "x-")
        self.push("02", h, BLK, "x+")
        self.across("02", 0, BLK)
        self.pull("--", 0, h, "y+", "-0")
        self.push("--", 0, h, "y+")
        self.across("--", 0, h)
        self.pull("++", 0, h, "y-", "+0")
        self.push("++", 0, h, "y-")
        self.across("++", 0, h)

    def p2x(self):
        h, qa, qb = self.h, self.qa, self.qb
        self.pull("20", qa, h, "x+", "-0")
        self.pull("20", 0, qa, "x-", "+0")
        self.push("20", 0, h, "y-")
        self.push("20", 0, h, "y+")
        self.across("20", 0, h)
        self.pull("-0", h, BLK, "x+", "00")
        self.push("-0", h, BLK, "x+")
        self.across("-0", h, BLK)
        self.pull("+0", h, BLK, "x-", "00")
        self.across("+0", h, BLK)
        self.pull("--", h, BLK, "x+", "0-")
        self.push("--", h, BLK, "x+")
        self.across("--", h, BLK)
        self.pull("++", h, BLK, "x-", "0+")
        self.push("++", h, BLK, "x-")
        self.across("++", h, BLK)
        self.partner("0", "0")

    def p3(self):
        h = self.h
        self.pull("2+", 0, h, "y-", "20")
        self.push("2+", 0, h, "y-")
        self.across("2+", 0, h)
        self.pull("+2", h, BLK, "x-", "02")
        self.push("+2", h, BLK, "x-")
        self.across("+2", h, BLK)
        for here, lo, hi, way, there in (
            ("+-", 0, h, "y+", "+0"),
            ("-+", 0, h, "y-", "-0"),
            ("-+", h, BLK, "x+", "0+"),
            ("+-", h, BLK, "x-", "0-"),
            ("2-", 0, h, "y+", "20"),
            ("-2", h, BLK, "x+", "02"),
        ):
            self.pull(here, lo, hi, way, there)
            self.across(here, lo, hi)
        self.partner("-", "-")
        self.partner("+", "+")

    def p4(self):
        h = self.h
        for here, lo, hi, way, there in (
            ("20", h, BLK, "x+", "-0"),
            ("-2", 0, h, "y+", "--"),
            ("2-", h, BLK, "x+", "--"),
            ("+2", 0, h, "y-", "++"),
            ("2+", h, BLK, "x-", "++"),
            ("22", 0, h, "y-", "2+"),
            ("22", h, BLK, "x-", "+2"),
        ):
            self.pull(here, lo, hi, way, there)
            self.across(here, lo, hi)
        self.partner("2", "2")

    def across(self, here, lo, hi):
        if not self.fine:
            return
        other = dev(self.y, 1 - self.c, self.x, self.z)
        ref = self.at(here, lo, hi)
        self.from_partner.append((ref, self.s.send(ref, ref, other)))

    def partner(self, x, y):
        if self.fine:
            return
        other = dev(self.y, 1 - self.c, self.x, self.z)
        a, b = self.band_a(self.ys[y]), self.band_b(self.xs[x])
        self.from_partner.append((a, self.s.send(a, a, other)))
        self.from_partner.append((b, self.s.send(b, b, other)))

    def finish(self):
        for ref, k in self.from_partner:
            self.s.arrived(ref, k)


class SkewGather(WeightGather):
    def __init__(self, *rest):
        super().__init__(*rest)
        y, c, x, z = self.y, self.c, self.x, self.z
        to_next = ((x ^ (x >> 1)) ^ y) & 1
        even = 1 - (x & 1)
        step_x, step_y = 2 * even - 1, 2 * to_next - 1
        self.xs["L"], self.xs["U"] = (x + NX + step_x) % NX, (x + NX - step_x) % NX
        self.ys["L"], self.ys["U"] = (y + NY + step_y) % NY, (y + NY - step_y) % NY
        self.to = {
            "xL": dev(y, c, self.xs["L"], z),
            "xU": dev(y, c, self.xs["U"], z),
            "yL": dev(self.ys["L"], c, x, z),
            "yU": dev(self.ys["U"], c, x, z),
        }

    def p0(self):
        for way in ("yL", "yU", "xL", "xU"):
            self.keys["00", 0, BLK, way] = self.s.send(self.own, self.at("00", 0, BLK), self.to[way])

    def p1y(self):
        h = self.h
        self.pull("0L", 0, BLK, "yL", "00")
        self.push("0L", 0, BLK, "yU")
        self.pull("0U", 0, BLK, "yU", "00")
        for block in ("0+", "0-"):
            self.push(block, h, BLK, "xL")
            self.push(block, h, BLK, "xU")

    def p1x(self):
        h = self.h
        self.pull("L0", 0, BLK, "xL", "00")
        self.push("L0", 0, BLK, "xU")
        self.push("L0", 0, h, "yL")
        self.push("L0", 0, h, "yU")
        self.pull("U0", 0, BLK, "xU", "00")
        self.push("U0", 0, h, "yL")
        self.push("U0", 0, h, "yU")

    def p2y(self):
        h = self.h
        self.pull("02", 0, BLK, "yU", "0L")
        self.push("02", h, BLK, "xL")
        self.push("02", h, BLK, "xU")
        self.pull("LL", 0, h, "yL", "L0")
        self.push("LL", 0, h, "yU")
        self.pull("UL", 0, h, "yL", "U0")
        self.push("UL", 0, h, "yU")

    def p2x(self):
        h = self.h
        self.pull("20", 0, BLK, "xU", "L0")
        self.push("20", 0, h, "yL")
        self.push("20", 0, h, "yU")
        self.pull("L+", h, BLK, "xL", "0+")
        self.push("L+", h, BLK, "xU")
        self.pull("L-", h, BLK, "xL", "0-")
        self.push("L-", h, BLK, "xU")
        self.partner("0", "0")

    def p3(self):
        h = self.h
        self.pull("2L", 0, h, "yL", "20")
        self.push("2L", 0, h, "yU")
        self.pull("L2", h, BLK, "xL", "02")
        self.push("L2", h, BLK, "xU")
        self.pull("LU", 0, h, "yU", "L0")
        self.pull("UU", 0, h, "yU", "U0")
        self.pull("2U", 0, h, "yU", "20")
        self.pull("U+", h, BLK, "xU", "0+")
        self.pull("U-", h, BLK, "xU", "0-")
        self.pull("U2", h, BLK, "xU", "02")
        self.partner("L", "L")
        self.partner("U", "U")

    def p4(self):
        h = self.h
        self.pull("L2", 0, h, "yU", "LL")
        self.pull("2+", h, BLK, "xU", "L+")
        self.pull("U2", 0, h, "yU", "UL")
        self.pull("2-", h, BLK, "xU", "L-")
        self.pull("22", 0, h, "yU", "2L")
        self.pull("22", h, BLK, "xU", "L2")
        self.partner("2", "2")


def block_kernel(
    tok_in, win_in, bin_in, taps_in, cbias_in, wout_in, bout_in, out,
    tok, win, wout, ext, act, part, own_par, par, tp, b1, cb1, bout, sendbuf, recvbuf, summed, moved, done, relay,
    lsem, ssem, rsem,
):
    y, c, x, z = place()
    s = Sender(ssem, rsem)
    xs = [(x + d) % NX for d in range(NX)]
    zp, zm = (z + 1) % NZ, (z + NZ - 1) % NZ
    yp, ym = (y + 1) % NY, (y + NY - 1) % NY
    upper = x >> 1
    frame = frame_of(y, c, x)
    last = NY * 4 - 1
    tc, tx = moved_to(y, c, x)
    fc, fx = moved_from(y, c, x)
    stays = (tc == c) & (tx == x)
    moves = jnp.logical_not(stays)
    far = ((x == 1) | (x == 2)) & (c == (y & 1))
    near = jnp.logical_and(moves, jnp.logical_not(far))
    between = ((x == 0) & (c == 0)) | ((x == NX - 1) & (c == 1))
    has_next, has_prev = frame < last, frame > 0
    ny, nc, nx = holder(jnp.minimum(frame + 1, last), upper)
    py, pc, px = holder(jnp.maximum(frame - 1, 0), upper)
    nxt, nxt_other = dev(ny, nc, nx, z), dev(ny, nc, 3 - nx, z)
    prv, prv_other = dev(py, pc, px, z), dev(py, pc, 3 - px, z)
    other_half = dev(y, c, 3 - x, z)

    locals_ = [
        pltpu.make_async_copy(taps_in, tp, lsem.at[0]),
        pltpu.make_async_copy(bin_in, b1, lsem.at[1]),
        pltpu.make_async_copy(cbias_in, cb1, lsem.at[2]),
    ]
    own_bout = pltpu.make_async_copy(bout_in, bout, lsem.at[3])
    for copy in locals_ + [own_bout]:
        copy.start()

    def win_block(x_, y_, rows):
        return win.at[y_, c, rows, pl.ds(x_ * BLK, BLK)]

    def win_a(y_):
        return win.at[y_, c, pl.ds(0, UPPER_IN), :]

    def win_b(x_):
        return win.at[:, c, pl.ds(UPPER_IN, BLK - UPPER_IN), pl.ds(x_ * BLK, BLK)]

    g_in = WeightGather(s, win_in, win_block, win_a, win_b, UPPER_IN, True)
    own_in = pltpu.make_async_copy(win_in, win_block(x, y, pl.ds(0, BLK)), lsem.at[4])
    own_in.start()

    def out_gather(q):
        w = BLK // 3
        n = NY * w

        def block(x_, y_, rows):
            return wout.at[q, x_, rows, pl.ds(c * n + y_ * w, w)]

        def band_a(y_):
            return wout.at[q, :, pl.ds(0, UPPER_OUT), pl.ds(c * n + y_ * w, w)]

        def band_b(x_):
            return wout.at[q, x_, pl.ds(UPPER_OUT, BLK - UPPER_OUT), pl.ds(c * n, n)]

        own = wout_in.at[:, pl.ds(q * w, w)]
        copy = pltpu.make_async_copy(own, block(x, y, pl.ds(0, BLK)), lsem.at[5 + q])
        copy.start()
        return SkewGather(s, own, block, band_a, band_b, UPPER_OUT, False), copy

    (g0, own0), (g1, own1), (g2, own2) = [out_gather(q) for q in range(3)]

    for copy in locals_:
        copy.wait()
    own_par[0:27, :] = tp[...]
    own_par[27:28, :] = b1[...].reshape(1, BLK)
    own_par[28:29, :] = cb1[...].reshape(1, BLK)

    greet(
        [(dev(y, c, xs[d], z), None) for d in (1, 2, 3)]
        + [(dev(yp, c, x, z), None), (dev(ym, c, x, z), None)]
        + [(dev(y, c, x, zp), None), (dev(y, c, x, zm), None)]
        + [(dev(y, 1 - c, x, z), None)]
        + [(dev(y, tc, tx, z), moves), (dev(y, fc, fx, z), moves)]
        + [(nxt, has_next), (nxt_other, has_next), (prv, has_prev), (prv_other, has_prev)]
        + [(other_half, None)]
        + [(dev(y, tc, jnp.where(x == 1, 0, NX - 1), z), far)]
        + [(dev(y, y & 1, jnp.where(x == 0, 1, 2), z), between)]
    )

    def tok_at(z_, p):
        return tok.at[pl.ds(((z_ + NZ) % NZ) * OWN + p * PIECE, PIECE)]

    home, relays = [], []
    for p in range(PIECES):
        src = tok_in.at[pl.ds(p * PIECE, PIECE)]
        stop = relay.at[pl.ds(p * PIECE, PIECE)]
        k = s.send(src, tok_at(z, p), dev(y, tc, tx, z), when=near)
        k_stop = s.send(src, stop, dev(y, tc, jnp.where(x == 1, 0, NX - 1), z), when=far)
        relays.append((stop, k_stop, k))
        stay = pltpu.make_async_copy(src, tok_at(z, p), rsem.at[k])
        pl.when(stays)(stay.start)
        home.append(stay)
    g_in.p0()

    @pl.when(upper == 0)
    def _():
        ext[:, 0] = jnp.zeros((3, WW, CH), BF16)

    @pl.when(upper == 1)
    def _():
        ext[:, ROWS + 1] = jnp.zeros((3, WW, CH), BF16)

    @pl.when(jnp.logical_not(has_prev))
    def _():
        @pl.loop(0, ROWS + 2)
        def _(r):
            ext[0, r] = jnp.zeros((WW, CH), BF16)

    @pl.when(jnp.logical_not(has_next))
    def _():
        @pl.loop(0, ROWS + 2)
        def _(r):
            ext[2, r] = jnp.zeros((WW, CH), BF16)

    k_tok = {}

    def pass_relay(p):
        stop, k_stop, k = relays[p]
        s.arrived(stop, k_stop, between)
        onward = pltpu.make_async_remote_copy(
            src_ref=stop,
            dst_ref=tok_at(z, p),
            send_sem=s.ssem.at[s.key()],
            recv_sem=s.rsem.at[k],
            device_id=other_half,
            device_id_type=MESH,
        )
        pl.when(between)(onward.start)
        s.sent.append((onward, between))

    def token_step(d, first=0, last=PIECES):
        for p in range(first, last):
            if d == 1:
                if p > 0:
                    pass_relay(p - 1)
                home[p].wait()
            for way, to in ((1, zp), (-1, zm)):
                if d == 4 and (p < PIECES // 2) != (way == 1):
                    continue
                src = tok_at(z - way * (d - 1), p)
                if d > 1:
                    s.arrived(src, k_tok[way, d - 1, p])
                k_tok[way, d, p] = s.send(src, src, dev(y, c, x, to))

    def par_at(x_):
        return par.at[:, pl.ds(x_ * BLK, BLK)]

    token_step(1)
    pass_relay(PIECES - 1)
    g_in.p0x()
    g_in.p1y()
    token_step(2, 0, 2)
    g_in.p1x()
    token_step(2, 2)
    own_in.wait()
    token_step(3, 0, 1)
    g_in.p2y()
    token_step(3, 1)
    g_in.p2x()
    token_step(4, 0, 2)
    g_in.p3()
    k_par = [s.send(own_par, par_at(x), dev(y, c, xs[d], z)) for d in (1, 2, 3)]
    own_copy = pltpu.make_async_copy(own_par, par_at(x), lsem.at[8])
    own_copy.start()
    own0.wait()
    own1.wait()
    own2.wait()
    g0.p0()
    g1.p0()
    g2.p0()
    token_step(4, 2)
    g_in.p4()
    own_copy.wait()
    for d in (1, 2, 3):
        s.arrived(par_at((x + NX - d) % NX), k_par[d - 1])
    for p in range(PIECES):
        way = -1 if p < PIECES // 2 else 1
        s.arrived(tok_at(z - way * 3, p), k_tok[way, 3, p])
        s.arrived(tok_at(z + 4, p), k_tok[-way, 4, p])
    g0.p1y()
    g0.p1x()
    g_in.finish()

    src_row = jnp.where(upper == 0, ROWS, 1)
    dst_row = jnp.where(upper == 0, 0, ROWS + 1)
    got_row = jnp.where(upper == 0, ROWS + 1, 0)
    inner = pl.ds(1, ROWS)
    arrivals = []
    step = 256
    for j, (first, many) in enumerate(CHUNKS):

        @pl.loop(0, many // step)
        def _(i):
            cols = pl.ds(pl.multiple_of(first + i * step, step), step)
            w = win[:, :, :, cols].reshape(D, step)
            before = jnp.dot(tok[...], w, preferred_element_type=F32) + par[27:28, cols]
            ext[1, inner, :, cols] = before.astype(BF16).reshape(ROWS, WW, step)

        cols = pl.ds(first, many)
        frame_src = ext.at[1, inner, :, cols]
        row_src = ext.at[1, src_row, :, cols]
        k1 = s.send(frame_src, ext.at[0, inner, :, cols], nxt, when=has_next)
        k2 = s.send(frame_src, ext.at[2, inner, :, cols], prv, when=has_prev)
        k3 = s.send(row_src, ext.at[1, dst_row, :, cols], other_half)
        k4 = s.send(row_src, ext.at[0, dst_row, :, cols], nxt_other, when=has_next)
        k5 = s.send(row_src, ext.at[2, dst_row, :, cols], prv_other, when=has_prev)
        arrivals.append([
            (ext.at[0, inner, :, cols], k1, has_prev),
            (ext.at[2, inner, :, cols], k2, has_next),
            (ext.at[1, got_row, :, cols], k3, None),
            (ext.at[0, got_row, :, cols], k4, has_prev),
            (ext.at[2, got_row, :, cols], k5, has_next),
        ])
        if j == 0:
            g0.p2y()
            g0.p2x()

    column = lax.broadcasted_iota(jnp.int32, (WW, 128), 0)

    def conv(j):
        first, many = CHUNKS[j]
        for copy in arrivals[j]:
            s.arrived(*copy)

        @pl.loop(0, many // 128)
        def _(i):
            lanes = pl.ds(pl.multiple_of(first + i * 128, 128), 128)

            @pl.loop(0, ROWS, step=2)
            def _(r):
                sums = [[None] * 3 for _ in range(2)]
                for dt in range(3):
                    for dr in range(2 + 2):
                        v = ext[dt, r + dr, :, lanes].astype(F32)
                        for row in range(2):
                            dh = dr - row
                            if not 0 <= dh < 3:
                                continue
                            for dw in range(3):
                                k = 9 * dt + 3 * dh + dw
                                t = v * par[k : k + 1, lanes]
                                old = sums[row][dw]
                                sums[row][dw] = t if old is None else old + t
                for row in range(2):
                    left = jnp.where(column == 0, 0.0, pltpu.roll(sums[row][0], 1, 0))
                    right = jnp.where(column == WW - 1, 0.0, pltpu.roll(sums[row][2], WW - 1, 0))
                    v = sums[row][1] + left + right + par[28:29, lanes]
                    half = 0.5 * v
                    t = jnp.tanh(v * (0.7978845608028654 + 0.035677408136300125 * (v * v)))
                    to = pl.ds(pl.multiple_of((r + row) * WW, WW), WW)
                    act[to, lanes] = (half + half * t).astype(BF16)

    conv(0)
    g0.p3()
    g1.p1y()
    g1.p1x()
    conv(1)
    g0.p4()
    g2.p1y()
    g2.p1x()
    conv(2)
    conv(3)
    g1.p2y()
    g1.p2x()
    g0.finish()

    units = D // UNIT
    chains = [
        (u, way, 4 if (u % 2 == 0) == (way == 1) else 3) for u in range(units) for way in (1, -1)
    ]
    slot, n = {}, 0
    for i, (u, way, length) in enumerate(chains):
        for st in range(length):
            slot[i, st] = n
            n += 1
    k_of = {}

    def multiply(q, first=0, many=CH):
        @pl.loop(0, 1024 // 256)
        def _(i):
            cols = pl.ds(pl.multiple_of(i * 256, 256), 256)
            w = wout[q, :, :, cols].reshape(CH, 256)[first : first + many]
            to = (2 * q + i // 2, slice(None), pl.ds(pl.multiple_of(i % 2 * 256, 256), 256))
            more = jnp.dot(act[:, first : first + many], w, preferred_element_type=F32)
            part[to] = more if first == 0 else part[to] + more

    def pass_on(u, st):
        for i, (u_, way, length) in enumerate(chains):
            if u_ != u or st >= length:
                continue
            at = (z + way * (length - st) + NZ) % NZ
            rows = pl.ds(pl.multiple_of(at * OWN, OWN), OWN)
            value = part[u, rows, :]
            if st > 0:
                got = recvbuf.at[slot[i, st - 1]]
                s.arrived(got, k_of[i, st - 1])
                value = value + got[...].astype(F32)
            mine = slot[i, st]
            sendbuf[mine] = value.astype(BF16)
            to = dev(y, c, x, zp if way == 1 else zm)
            k_of[i, st] = s.send(sendbuf.at[mine], recvbuf.at[mine], to)

    back = []

    w = BLK // 3

    def collect(u):
        rows = pl.ds(pl.multiple_of(z * OWN, OWN), OWN)
        value = part[u, rows, :]
        for i in (2 * u, 2 * u + 1):
            mine = slot[i, chains[i][2] - 1]
            s.arrived(recvbuf.at[mine], k_of[i, chains[i][2] - 1])
            value = value + recvbuf[mine].astype(F32)
        for n_ in range(NY):
            lo = (n_ * 2 + u % 2) * BLK + u // 2 * w
            summed[u, :, n_ * w : (n_ + 1) * w] = (
                value[:, n_ * w : (n_ + 1) * w] + bout[lo : lo + w].reshape(1, w)
            ).astype(BF16)
        k = s.send(summed.at[u], moved.at[u], dev(y, fc, fx, z), when=moves)
        stay = pltpu.make_async_copy(summed.at[u], moved.at[u], rsem.at[k])
        pl.when(stays)(stay.start)
        back.append(stay)

    def put(u):
        back[u].wait()
        for n_ in range(NY):
            lo = (n_ * 2 + u % 2) * BLK + u // 2 * w
            done[:, lo : lo + w] = moved[u, :, n_ * w : (n_ + 1) * w]

    def hop(q, st):
        pass_on(2 * q, st)
        pass_on(2 * q + 1, st)

    own_bout.wait()
    multiply(0)
    hop(0, 0)
    g1.p3()
    g2.p2y()
    g2.p2x()
    g1.p4()
    hop(0, 1)
    g1.finish()
    multiply(1)
    hop(1, 0)
    g2.p3()
    hop(0, 2)
    g2.p4()
    hop(1, 1)
    g2.finish()
    multiply(2)
    hop(2, 0)
    hop(0, 3)
    hop(2, 1)
    hop(1, 2)
    collect(0)
    collect(1)
    hop(2, 2)
    hop(1, 3)
    put(0)
    put(1)
    hop(2, 3)
    collect(2)
    collect(3)
    collect(4)
    collect(5)
    put(2)
    put(3)
    put(4)
    put(5)
    stored = pltpu.make_async_copy(done, out, lsem.at[9])
    stored.start()
    stored.wait()
    s.drain()


def body(tokens, w_in, b_in, conv_taps, conv_bias, w_out, b_out):
    keys = 300
    hbm = pl.BlockSpec(memory_space=pl.ANY)
    return pl.pallas_call(
        block_kernel,
        out_shape=jax.ShapeDtypeStruct((OWN, D), BF16),
        in_specs=[hbm] * 7,
        out_specs=hbm,
        scratch_shapes=[
            pltpu.VMEM((GROUP, D), BF16),
            pltpu.VMEM((NY, 2, BLK, CH), BF16),
            pltpu.VMEM((3, NX, BLK, 2 * UNIT), BF16),
            pltpu.VMEM((3, ROWS + 2, WW, CH), BF16),
            pltpu.VMEM((GROUP, CH), BF16),
            pltpu.VMEM((6, GROUP, UNIT), F32),
            pltpu.VMEM((32, BLK), F32),
            pltpu.VMEM((32, CH), F32),
            pltpu.VMEM((27, BLK), F32),
            pltpu.VMEM((BLK,), F32),
            pltpu.VMEM((BLK,), F32),
            pltpu.VMEM((D,), F32),
            pltpu.VMEM((42, OWN, UNIT), BF16),
            pltpu.VMEM((42, OWN, UNIT), BF16),
            pltpu.VMEM((6, OWN, UNIT), BF16),
            pltpu.VMEM((6, OWN, UNIT), BF16),
            pltpu.VMEM((OWN, D), BF16),
            pltpu.VMEM((OWN, D), BF16),
            pltpu.SemaphoreType.DMA((10,)),
            pltpu.SemaphoreType.DMA((keys,)),
            pltpu.SemaphoreType.DMA((keys,)),
        ],
        compiler_params=pltpu.CompilerParams(
            collective_id=0, has_side_effects=True, vmem_limit_bytes=60 * 2**20
        ),
        name="mix_ffn",
    )(tokens, w_in, b_in, conv_taps, conv_bias, w_out, b_out)


def solution(mesh):
    placed = (
        P(("row", "col"), None),
        P("row", "col"),
        P("col"),
        P(None, "col"),
        P("col"),
        P("col", "row"),
        P(),
    )
    return jax.shard_map(
        body, mesh=mesh, in_specs=placed, out_specs=P(("row", "col"), None), check_vma=False
    )
```

```python
import functools

import jax
import jax.numpy as jnp
from jax import lax
from jax.experimental import pallas as pl
from jax.experimental.pallas import tpu as pltpu
from jax.sharding import PartitionSpec as P

MESH = pl.DeviceIdType.MESH
NX, NY, NZ = 4, 4, 8
D = 3072
BLK = 384
UPPER_IN = 192
UPPER_OUT = 192
CH = NX * BLK
GROUP = 512
OWN = 64
WW = 32
ROWS = GROUP // WW
CHUNKS = ((0, 512), (512, 512), (1024, 256), (1280, 256))
PIECES = 4
PIECE = OWN // PIECES
UNIT = 512
BF16, F32 = jnp.bfloat16, jnp.float32


def place():
    row, col = lax.axis_index("row"), lax.axis_index("col")
    return row // 2, row % 2, col // NZ, col % NZ


def dev(y, c, x, z):
    return {"row": y * 2 + c, "col": x * NZ + z}


def moved_to(y, c, x):
    b = c ^ (y & 1)
    upper = x & 1
    return x >> 1, jnp.where(upper == 0, b, 3 - b)


def moved_from(y, c, x):
    b = (x ^ (x >> 1)) & 1
    return b ^ (y & 1), c * 2 + (x >> 1)


def frame_of(y, c, x):
    b = (x ^ (x >> 1)) & 1
    return 4 * y + 2 * (b ^ (y & 1)) + c


def holder(frame, upper):
    pair = frame >> 1
    y = pair >> 1
    b = (pair & 1) ^ (y & 1)
    return y, frame & 1, jnp.where(upper == 0, b, 3 - b)


class Sender:
    def __init__(self, ssem, rsem):
        self.ssem, self.rsem, self.used, self.sent = ssem, rsem, 0, []

    def key(self):
        self.used += 1
        return self.used - 1

    def make(self, src, dst, k, to):
        return pltpu.make_async_remote_copy(
            src_ref=src,
            dst_ref=dst,
            send_sem=self.ssem.at[k],
            recv_sem=self.rsem.at[k],
            device_id=to,
            device_id_type=MESH,
        )

    def send(self, src, dst, to, when=None):
        k = self.key()
        copy = self.make(src, dst, k, to)
        if when is None:
            copy.start()
        else:
            pl.when(when)(copy.start)
        self.sent.append((copy, when))
        return k

    def arrived(self, ref, k, when=None):
        copy = pltpu.make_async_copy(ref, ref, self.rsem.at[k])
        if when is None:
            copy.wait()
        else:
            pl.when(when)(copy.wait)

    def drain(self):
        for copy, when in self.sent:
            if when is None:
                copy.wait_send()
            else:
                pl.when(when)(copy.wait_send)
        self.sent = []


def greet(peers):
    barrier = pltpu.get_barrier_semaphore()
    count = 0
    for to, when in peers:
        signal = functools.partial(pl.semaphore_signal, barrier, inc=1, device_id=to, device_id_type=MESH)
        if when is None:
            signal()
            count = count + 1
        else:
            pl.when(when)(signal)
            count = count + when.astype(jnp.int32)
    pl.semaphore_wait(barrier, count)


class WeightGather:
    def __init__(self, sender, own, block, band_a, band_b, upper, fine):
        self.fine = fine
        self.s, self.own = sender, own
        self.h, self.qa, self.qb = upper, upper // 2, upper + (BLK - upper) // 2
        self.block, self.band_a, self.band_b = block, band_a, band_b
        self.y, self.c, self.x, self.z = place()
        y, c, x, z = self.y, self.c, self.x, self.z
        self.xs = {"0": x, "+": (x + 1) % NX, "-": (x + NX - 1) % NX, "2": (x + 2) % NX}
        self.ys = {"0": y, "+": (y + 1) % NY, "-": (y + NY - 1) % NY, "2": (y + 2) % NY}
        self.to = {
            "x+": dev(y, c, self.xs["+"], z),
            "x-": dev(y, c, self.xs["-"], z),
            "y+": dev(self.ys["+"], c, x, z),
            "y-": dev(self.ys["-"], c, x, z),
        }
        self.keys, self.from_partner = {}, []

    def at(self, place_, lo, hi):
        return self.block(self.xs[place_[0]], self.ys[place_[1]], pl.ds(lo, hi - lo))

    def push(self, place_, lo, hi, way):
        src = self.at(place_, lo, hi)
        self.keys[place_, lo, hi, way] = self.s.send(src, src, self.to[way])

    def pull(self, here, lo, hi, way, there):
        self.s.arrived(self.at(here, lo, hi), self.keys[there, lo, hi, way])

    def p0(self):
        self.p0x(((0, BLK, ("y+", "y-")),))
        if self.fine:
            other = dev(self.y, 1 - self.c, self.x, self.z)
            here = self.at("00", 0, BLK)
            self.from_partner.append((here, self.s.send(self.own, here, other)))

    def p0x(self, parts=None):
        h = self.h
        for lo, hi, ways in parts or ((0, h, ("x+", "x-")), (h, BLK, ("x+", "x-"))):
            for way in ways:
                src = self.own.at[pl.ds(lo, hi - lo)]
                self.keys["00", lo, hi, way] = self.s.send(src, self.at("00", lo, hi), self.to[way])

    def p1y(self):
        h, qa, qb = self.h, self.qa, self.qb
        self.pull("0-", 0, BLK, "y+", "00")
        self.push("0-", 0, qb, "y+")
        self.push("0-", h, BLK, "x+")
        self.push("0-", h, BLK, "x-")
        self.across("0-", 0, BLK)
        self.pull("0+", 0, BLK, "y-", "00")
        self.push("0+", qb, BLK, "y-")
        self.push("0+", h, BLK, "x+")
        self.push("0+", h, BLK, "x-")
        self.across("0+", 0, BLK)

    def p1x(self):
        h, qa, qb = self.h, self.qa, self.qb
        self.pull("-0", 0, h, "x+", "00")
        self.push("-0", qa, h, "x+")
        self.push("-0", 0, h, "y+")
        self.push("-0", 0, h, "y-")
        self.across("-0", 0, h)
        self.pull("+0", 0, h, "x-", "00")
        self.push("+0", 0, qa, "x-")
        self.push("+0", 0, h, "y+")
        self.push("+0", 0, h, "y-")
        self.across("+0", 0, h)

    def p2y(self):
        h, qa, qb = self.h, self.qa, self.qb
        self.pull("02", 0, qb, "y+", "0-")
        self.pull("02", qb, BLK, "y-", "0+")
        self.push("02", h, BLK, "x-")
        self.push("02", h, BLK, "x+")
        self.across("02", 0, BLK)
        self.pull("--", 0, h, "y+", "-0")
        self.push("--", 0, h, "y+")
        self.across("--", 0, h)
        self.pull("++", 0, h, "y-", "+0")
        self.push("++", 0, h, "y-")
        self.across("++", 0, h)

    def p2x(self):
        h, qa, qb = self.h, self.qa, self.qb
        self.pull("20", qa, h, "x+", "-0")
        self.pull("20", 0, qa, "x-", "+0")
        self.push("20", 0, h, "y-")
        self.push("20", 0, h, "y+")
        self.across("20", 0, h)
        self.pull("-0", h, BLK, "x+", "00")
        self.push("-0", h, BLK, "x+")
        self.across("-0", h, BLK)
        self.pull("+0", h, BLK, "x-", "00")
        self.across("+0", h, BLK)
        self.pull("--", h, BLK, "x+", "0-")
        self.push("--", h, BLK, "x+")
        self.across("--", h, BLK)
        self.pull("++", h, BLK, "x-", "0+")
        self.push("++", h, BLK, "x-")
        self.across("++", h, BLK)
        self.partner("0", "0")

    def p3(self):
        h = self.h
        self.pull("2+", 0, h, "y-", "20")
        self.push("2+", 0, h, "y-")
        self.across("2+", 0, h)
        self.pull("+2", h, BLK, "x-", "02")
        self.push("+2", h, BLK, "x-")
        self.across("+2", h, BLK)
        for here, lo, hi, way, there in (
            ("+-", 0, h, "y+", "+0"),
            ("-+", 0, h, "y-", "-0"),
            ("-+", h, BLK, "x+", "0+"),
            ("+-", h, BLK, "x-", "0-"),
            ("2-", 0, h, "y+", "20"),
            ("-2", h, BLK, "x+", "02"),
        ):
            self.pull(here, lo, hi, way, there)
            self.across(here, lo, hi)
        self.partner("-", "-")
        self.partner("+", "+")

    def p4(self):
        h = self.h
        for here, lo, hi, way, there in (
            ("20", h, BLK, "x+", "-0"),
            ("-2", 0, h, "y+", "--"),
            ("2-", h, BLK, "x+", "--"),
            ("+2", 0, h, "y-", "++"),
            ("2+", h, BLK, "x-", "++"),
            ("22", 0, h, "y-", "2+"),
            ("22", h, BLK, "x-", "+2"),
        ):
            self.pull(here, lo, hi, way, there)
            self.across(here, lo, hi)
        self.partner("2", "2")

    def across(self, here, lo, hi):
        if not self.fine:
            return
        other = dev(self.y, 1 - self.c, self.x, self.z)
        ref = self.at(here, lo, hi)
        self.from_partner.append((ref, self.s.send(ref, ref, other)))

    def partner(self, x, y):
        if self.fine:
            return
        other = dev(self.y, 1 - self.c, self.x, self.z)
        a, b = self.band_a(self.ys[y]), self.band_b(self.xs[x])
        self.from_partner.append((a, self.s.send(a, a, other)))
        self.from_partner.append((b, self.s.send(b, b, other)))

    def finish(self):
        for ref, k in self.from_partner:
            self.s.arrived(ref, k)


class SkewGather(WeightGather):
    def __init__(self, *rest):
        super().__init__(*rest)
        y, c, x, z = self.y, self.c, self.x, self.z
        to_next = ((x ^ (x >> 1)) ^ y) & 1
        even = 1 - (x & 1)
        step_x, step_y = 2 * even - 1, 2 * to_next - 1
        self.xs["L"], self.xs["U"] = (x + NX + step_x) % NX, (x + NX - step_x) % NX
        self.ys["L"], self.ys["U"] = (y + NY + step_y) % NY, (y + NY - step_y) % NY
        self.to = {
            "xL": dev(y, c, self.xs["L"], z),
            "xU": dev(y, c, self.xs["U"], z),
            "yL": dev(self.ys["L"], c, x, z),
            "yU": dev(self.ys["U"], c, x, z),
        }

    def p0(self):
        for way in ("yL", "yU", "xL", "xU"):
            self.keys["00", 0, BLK, way] = self.s.send(self.own, self.at("00", 0, BLK), self.to[way])

    def p1y(self):
        h = self.h
        self.pull("0L", 0, BLK, "yL", "00")
        self.push("0L", 0, BLK, "yU")
        self.pull("0U", 0, BLK, "yU", "00")
        for block in ("0+", "0-"):
            self.push(block, h, BLK, "xL")
            self.push(block, h, BLK, "xU")

    def p1x(self):
        h = self.h
        self.pull("L0", 0, BLK, "xL", "00")
        self.push("L0", 0, BLK, "xU")
        self.push("L0", 0, h, "yL")
        self.push("L0", 0, h, "yU")
        self.pull("U0", 0, BLK, "xU", "00")
        self.push("U0", 0, h, "yL")
        self.push("U0", 0, h, "yU")

    def p2y(self):
        h = self.h
        self.pull("02", 0, BLK, "yU", "0L")
        self.push("02", h, BLK, "xL")
        self.push("02", h, BLK, "xU")
        self.pull("LL", 0, h, "yL", "L0")
        self.push("LL", 0, h, "yU")
        self.pull("UL", 0, h, "yL", "U0")
        self.push("UL", 0, h, "yU")

    def p2x(self):
        h = self.h
        self.pull("20", 0, BLK, "xU", "L0")
        self.push("20", 0, h, "yL")
        self.push("20", 0, h, "yU")
        self.pull("L+", h, BLK, "xL", "0+")
        self.push("L+", h, BLK, "xU")
        self.pull("L-", h, BLK, "xL", "0-")
        self.push("L-", h, BLK, "xU")
        self.partner("0", "0")

    def p3(self):
        h = self.h
        self.pull("2L", 0, h, "yL", "20")
        self.push("2L", 0, h, "yU")
        self.pull("L2", h, BLK, "xL", "02")
        self.push("L2", h, BLK, "xU")
        self.pull("LU", 0, h, "yU", "L0")
        self.pull("UU", 0, h, "yU", "U0")
        self.pull("2U", 0, h, "yU", "20")
        self.pull("U+", h, BLK, "xU", "0+")
        self.pull("U-", h, BLK, "xU", "0-")
        self.pull("U2", h, BLK, "xU", "02")
        self.partner("L", "L")
        self.partner("U", "U")

    def p4(self):
        h = self.h
        self.pull("L2", 0, h, "yU", "LL")
        self.pull("2+", h, BLK, "xU", "L+")
        self.pull("U2", 0, h, "yU", "UL")
        self.pull("2-", h, BLK, "xU", "L-")
        self.pull("22", 0, h, "yU", "2L")
        self.pull("22", h, BLK, "xU", "L2")
        self.partner("2", "2")


def block_kernel(
    tok_in, win_in, bin_in, taps_in, cbias_in, wout_in, bout_in, out,
    tok, win, wout, ext, act, part, own_par, par, tp, b1, cb1, bout, sendbuf, recvbuf, summed, moved, done, relay,
    lsem, ssem, rsem,
):
    y, c, x, z = place()
    s = Sender(ssem, rsem)
    xs = [(x + d) % NX for d in range(NX)]
    zp, zm = (z + 1) % NZ, (z + NZ - 1) % NZ
    yp, ym = (y + 1) % NY, (y + NY - 1) % NY
    upper = x >> 1
    frame = frame_of(y, c, x)
    last = NY * 4 - 1
    tc, tx = moved_to(y, c, x)
    fc, fx = moved_from(y, c, x)
    stays = (tc == c) & (tx == x)
    moves = jnp.logical_not(stays)
    far = ((x == 1) | (x == 2)) & (c == (y & 1))
    near = jnp.logical_and(moves, jnp.logical_not(far))
    between = ((x == 0) & (c == 0)) | ((x == NX - 1) & (c == 1))
    has_next, has_prev = frame < last, frame > 0
    ny, nc, nx = holder(jnp.minimum(frame + 1, last), upper)
    py, pc, px = holder(jnp.maximum(frame - 1, 0), upper)
    nxt, nxt_other = dev(ny, nc, nx, z), dev(ny, nc, 3 - nx, z)
    prv, prv_other = dev(py, pc, px, z), dev(py, pc, 3 - px, z)
    other_half = dev(y, c, 3 - x, z)

    locals_ = [
        pltpu.make_async_copy(taps_in, tp, lsem.at[0]),
        pltpu.make_async_copy(bin_in, b1, lsem.at[1]),
        pltpu.make_async_copy(cbias_in, cb1, lsem.at[2]),
    ]
    own_bout = pltpu.make_async_copy(bout_in, bout, lsem.at[3])
    for copy in locals_ + [own_bout]:
        copy.start()

    def win_block(x_, y_, rows):
        return win.at[y_, c, rows, pl.ds(x_ * BLK, BLK)]

    def win_a(y_):
        return win.at[y_, c, pl.ds(0, UPPER_IN), :]

    def win_b(x_):
        return win.at[:, c, pl.ds(UPPER_IN, BLK - UPPER_IN), pl.ds(x_ * BLK, BLK)]

    g_in = WeightGather(s, win_in, win_block, win_a, win_b, UPPER_IN, True)
    own_in = pltpu.make_async_copy(win_in, win_block(x, y, pl.ds(0, BLK)), lsem.at[4])
    own_in.start()

    def out_gather(q):
        w = BLK // 3
        n = NY * w

        def block(x_, y_, rows):
            return wout.at[q, x_, rows, pl.ds(c * n + y_ * w, w)]

        def band_a(y_):
            return wout.at[q, :, pl.ds(0, UPPER_OUT), pl.ds(c * n + y_ * w, w)]

        def band_b(x_):
            return wout.at[q, x_, pl.ds(UPPER_OUT, BLK - UPPER_OUT), pl.ds(c * n, n)]

        own = wout_in.at[:, pl.ds(q * w, w)]
        copy = pltpu.make_async_copy(own, block(x, y, pl.ds(0, BLK)), lsem.at[5 + q])
        copy.start()
        return SkewGather(s, own, block, band_a, band_b, UPPER_OUT, False), copy

    (g0, own0), (g1, own1), (g2, own2) = [out_gather(q) for q in range(3)]

    greet(
        [(dev(y, c, xs[d], z), None) for d in (1, 2, 3)]
        + [(dev(yp, c, x, z), None), (dev(ym, c, x, z), None)]
        + [(dev(y, c, x, zp), None), (dev(y, c, x, zm), None)]
        + [(dev(y, 1 - c, x, z), None)]
        + [(dev(y, tc, tx, z), moves), (dev(y, fc, fx, z), moves)]
        + [(nxt, has_next), (nxt_other, has_next), (prv, has_prev), (prv_other, has_prev)]
        + [(other_half, None)]
        + [(dev(y, tc, jnp.where(x == 1, 0, NX - 1), z), far)]
        + [(dev(y, y & 1, jnp.where(x == 0, 1, 2), z), between)]
    )

    def tok_at(z_, p):
        return tok.at[pl.ds(((z_ + NZ) % NZ) * OWN + p * PIECE, PIECE)]

    home, relays = [], []
    for p in range(PIECES):
        src = tok_in.at[pl.ds(p * PIECE, PIECE)]
        stop = relay.at[pl.ds(p * PIECE, PIECE)]
        k = s.send(src, tok_at(z, p), dev(y, tc, tx, z), when=near)
        k_stop = s.send(src, stop, dev(y, tc, jnp.where(x == 1, 0, NX - 1), z), when=far)
        relays.append((stop, k_stop, k))
        stay = pltpu.make_async_copy(src, tok_at(z, p), rsem.at[k])
        pl.when(stays)(stay.start)
        home.append(stay)
    g_in.p0()

    @pl.when(upper == 0)
    def _():
        ext[:, 0] = jnp.zeros((3, WW, CH), BF16)

    @pl.when(upper == 1)
    def _():
        ext[:, ROWS + 1] = jnp.zeros((3, WW, CH), BF16)

    @pl.when(jnp.logical_not(has_prev))
    def _():
        @pl.loop(0, ROWS + 2)
        def _(r):
            ext[0, r] = jnp.zeros((WW, CH), BF16)

    @pl.when(jnp.logical_not(has_next))
    def _():
        @pl.loop(0, ROWS + 2)
        def _(r):
            ext[2, r] = jnp.zeros((WW, CH), BF16)

    k_tok = {}

    def pass_relay(p):
        stop, k_stop, k = relays[p]
        s.arrived(stop, k_stop, between)
        onward = pltpu.make_async_remote_copy(
            src_ref=stop,
            dst_ref=tok_at(z, p),
            send_sem=s.ssem.at[s.key()],
            recv_sem=s.rsem.at[k],
            device_id=other_half,
            device_id_type=MESH,
        )
        pl.when(between)(onward.start)
        s.sent.append((onward, between))

    def token_step(d, first=0, last=PIECES):
        for p in range(first, last):
            if d == 1:
                if p > 0:
                    pass_relay(p - 1)
                home[p].wait()
            for way, to in ((1, zp), (-1, zm)):
                if d == 4 and (p < PIECES // 2) != (way == 1):
                    continue
                src = tok_at(z - way * (d - 1), p)
                if d > 1:
                    s.arrived(src, k_tok[way, d - 1, p])
                k_tok[way, d, p] = s.send(src, src, dev(y, c, x, to))

    def par_at(x_):
        return par.at[:, pl.ds(x_ * BLK, BLK)]

    token_step(1)
    pass_relay(PIECES - 1)
    g_in.p0x()
    g_in.p1y()
    token_step(2, 0, 2)
    g_in.p1x()
    token_step(2, 2)
    own_in.wait()
    token_step(3, 0, 1)
    g_in.p2y()
    token_step(3, 1)
    g_in.p2x()
    token_step(4, 0, 2)
    g_in.p3()
    for copy in locals_:
        copy.wait()
    own_par[0:27, :] = tp[...]
    own_par[27:28, :] = b1[...].reshape(1, BLK)
    own_par[28:29, :] = cb1[...].reshape(1, BLK)
    k_par = [s.send(own_par, par_at(x), dev(y, c, xs[d], z)) for d in (1, 2, 3)]
    own_copy = pltpu.make_async_copy(own_par, par_at(x), lsem.at[8])
    own_copy.start()
    own0.wait()
    own1.wait()
    own2.wait()
    g0.p0()
    g1.p0()
    g2.p0()
    token_step(4, 2)
    g_in.p4()
    own_copy.wait()
    for d in (1, 2, 3):
        s.arrived(par_at((x + NX - d) % NX), k_par[d - 1])
    for p in range(PIECES):
        way = -1 if p < PIECES // 2 else 1
        s.arrived(tok_at(z - way * 3, p), k_tok[way, 3, p])
        s.arrived(tok_at(z + 4, p), k_tok[-way, 4, p])
    g0.p1y()
    g0.p1x()
    g_in.finish()

    src_row = jnp.where(upper == 0, ROWS, 1)
    dst_row = jnp.where(upper == 0, 0, ROWS + 1)
    got_row = jnp.where(upper == 0, ROWS + 1, 0)
    inner = pl.ds(1, ROWS)
    arrivals = []
    step = 256
    for j, (first, many) in enumerate(CHUNKS):

        @pl.loop(0, many // step)
        def _(i):
            cols = pl.ds(pl.multiple_of(first + i * step, step), step)
            w = win[:, :, :, cols].reshape(D, step)
            before = jnp.dot(tok[...], w, preferred_element_type=F32) + par[27:28, cols]
            ext[1, inner, :, cols] = before.astype(BF16).reshape(ROWS, WW, step)

        cols = pl.ds(first, many)
        frame_src = ext.at[1, inner, :, cols]
        row_src = ext.at[1, src_row, :, cols]
        k1 = s.send(frame_src, ext.at[0, inner, :, cols], nxt, when=has_next)
        k2 = s.send(frame_src, ext.at[2, inner, :, cols], prv, when=has_prev)
        k3 = s.send(row_src, ext.at[1, dst_row, :, cols], other_half)
        k4 = s.send(row_src, ext.at[0, dst_row, :, cols], nxt_other, when=has_next)
        k5 = s.send(row_src, ext.at[2, dst_row, :, cols], prv_other, when=has_prev)
        arrivals.append([
            (ext.at[0, inner, :, cols], k1, has_prev),
            (ext.at[2, inner, :, cols], k2, has_next),
            (ext.at[1, got_row, :, cols], k3, None),
            (ext.at[0, got_row, :, cols], k4, has_prev),
            (ext.at[2, got_row, :, cols], k5, has_next),
        ])
        if j == 0:
            g0.p2y()
            g0.p2x()

    column = lax.broadcasted_iota(jnp.int32, (WW, 128), 0)

    def conv(j):
        first, many = CHUNKS[j]
        for copy in arrivals[j]:
            s.arrived(*copy)

        @pl.loop(0, many // 128)
        def _(i):
            lanes = pl.ds(pl.multiple_of(first + i * 128, 128), 128)

            @pl.loop(0, ROWS, step=2)
            def _(r):
                sums = [[None] * 3 for _ in range(2)]
                for dt in range(3):
                    for dr in range(2 + 2):
                        v = ext[dt, r + dr, :, lanes].astype(F32)
                        for row in range(2):
                            dh = dr - row
                            if not 0 <= dh < 3:
                                continue
                            for dw in range(3):
                                k = 9 * dt + 3 * dh + dw
                                t = v * par[k : k + 1, lanes]
                                old = sums[row][dw]
                                sums[row][dw] = t if old is None else old + t
                for row in range(2):
                    left = jnp.where(column == 0, 0.0, pltpu.roll(sums[row][0], 1, 0))
                    right = jnp.where(column == WW - 1, 0.0, pltpu.roll(sums[row][2], WW - 1, 0))
                    v = sums[row][1] + left + right + par[28:29, lanes]
                    half = 0.5 * v
                    t = jnp.tanh(v * (0.7978845608028654 + 0.035677408136300125 * (v * v)))
                    to = pl.ds(pl.multiple_of((r + row) * WW, WW), WW)
                    act[to, lanes] = (half + half * t).astype(BF16)

    conv(0)
    g0.p3()
    g1.p1y()
    g1.p1x()
    conv(1)
    g0.p4()
    g2.p1y()
    g2.p1x()
    conv(2)
    g1.p2y()
    g1.p2x()
    conv(3)
    g0.finish()

    units = D // UNIT
    chains = [
        (u, way, 4 if (u % 2 == 0) == (way == 1) else 3) for u in range(units) for way in (1, -1)
    ]
    slot, n = {}, 0
    for i, (u, way, length) in enumerate(chains):
        for st in range(length):
            slot[i, st] = n
            n += 1
    k_of = {}

    def multiply(u):
        @pl.loop(0, UNIT // 256)
        def _(i):
            at = pl.multiple_of(i * 256, 256)
            w = wout[u // 2, :, :, pl.ds(u % 2 * UNIT + at, 256)].reshape(CH, 256)
            part[u, :, pl.ds(at, 256)] = jnp.dot(act[...], w, preferred_element_type=F32)

    def pass_on(u, st):
        for i, (u_, way, length) in enumerate(chains):
            if u_ != u or st >= length:
                continue
            at = (z + way * (length - st) + NZ) % NZ
            rows = pl.ds(pl.multiple_of(at * OWN, OWN), OWN)
            value = part[u, rows, :]
            if st > 0:
                got = recvbuf.at[slot[i, st - 1]]
                s.arrived(got, k_of[i, st - 1])
                value = value + got[...].astype(F32)
            mine = slot[i, st]
            sendbuf[mine] = value.astype(BF16)
            to = dev(y, c, x, zp if way == 1 else zm)
            k_of[i, st] = s.send(sendbuf.at[mine], recvbuf.at[mine], to)

    back = []

    w = BLK // 3

    def collect(u):
        rows = pl.ds(pl.multiple_of(z * OWN, OWN), OWN)
        value = part[u, rows, :]
        for i in (2 * u, 2 * u + 1):
            mine = slot[i, chains[i][2] - 1]
            s.arrived(recvbuf.at[mine], k_of[i, chains[i][2] - 1])
            value = value + recvbuf[mine].astype(F32)
        for n_ in range(NY):
            lo = (n_ * 2 + u % 2) * BLK + u // 2 * w
            summed[u, :, n_ * w : (n_ + 1) * w] = (
                value[:, n_ * w : (n_ + 1) * w] + bout[lo : lo + w].reshape(1, w)
            ).astype(BF16)
        k = s.send(summed.at[u], moved.at[u], dev(y, fc, fx, z), when=moves)
        stay = pltpu.make_async_copy(summed.at[u], moved.at[u], rsem.at[k])
        pl.when(stays)(stay.start)
        back.append(stay)

    def put(u):
        back[u].wait()
        for n_ in range(NY):
            lo = (n_ * 2 + u % 2) * BLK + u // 2 * w
            done[:, lo : lo + w] = moved[u, :, n_ * w : (n_ + 1) * w]

    def hop(q, st):
        pass_on(2 * q, st)
        pass_on(2 * q + 1, st)

    own_bout.wait()
    multiply(0)
    pass_on(0, 0)
    multiply(1)
    pass_on(1, 0)
    g1.p3()
    g2.p2y()
    g2.p2x()
    g1.p4()
    hop(0, 1)
    g1.finish()
    multiply(2)
    pass_on(2, 0)
    multiply(3)
    pass_on(3, 0)
    g2.p3()
    hop(0, 2)
    g2.p4()
    hop(1, 1)
    g2.finish()
    multiply(4)
    pass_on(4, 0)
    multiply(5)
    pass_on(5, 0)
    hop(0, 3)
    hop(2, 1)
    hop(1, 2)
    collect(0)
    collect(1)
    hop(2, 2)
    hop(1, 3)
    put(0)
    put(1)
    hop(2, 3)
    collect(2)
    collect(3)
    collect(4)
    collect(5)
    put(2)
    put(3)
    put(4)
    put(5)
    stored = pltpu.make_async_copy(done, out, lsem.at[9])
    stored.start()
    stored.wait()
    s.drain()


def body(tokens, w_in, b_in, conv_taps, conv_bias, w_out, b_out):
    keys = 300
    hbm = pl.BlockSpec(memory_space=pl.ANY)
    return pl.pallas_call(
        block_kernel,
        out_shape=jax.ShapeDtypeStruct((OWN, D), BF16),
        in_specs=[hbm] * 7,
        out_specs=hbm,
        scratch_shapes=[
            pltpu.VMEM((GROUP, D), BF16),
            pltpu.VMEM((NY, 2, BLK, CH), BF16),
            pltpu.VMEM((3, NX, BLK, 2 * UNIT), BF16),
            pltpu.VMEM((3, ROWS + 2, WW, CH), BF16),
            pltpu.VMEM((GROUP, CH), BF16),
            pltpu.VMEM((6, GROUP, UNIT), F32),
            pltpu.VMEM((32, BLK), F32),
            pltpu.VMEM((32, CH), F32),
            pltpu.VMEM((27, BLK), F32),
            pltpu.VMEM((BLK,), F32),
            pltpu.VMEM((BLK,), F32),
            pltpu.VMEM((D,), F32),
            pltpu.VMEM((42, OWN, UNIT), BF16),
            pltpu.VMEM((42, OWN, UNIT), BF16),
            pltpu.VMEM((6, OWN, UNIT), BF16),
            pltpu.VMEM((6, OWN, UNIT), BF16),
            pltpu.VMEM((OWN, D), BF16),
            pltpu.VMEM((OWN, D), BF16),
            pltpu.SemaphoreType.DMA((10,)),
            pltpu.SemaphoreType.DMA((keys,)),
            pltpu.SemaphoreType.DMA((keys,)),
        ],
        compiler_params=pltpu.CompilerParams(
            collective_id=0, has_side_effects=True, vmem_limit_bytes=60 * 2**20
        ),
        name="mix_ffn",
    )(tokens, w_in, b_in, conv_taps, conv_bias, w_out, b_out)


def solution(mesh):
    placed = (
        P(("row", "col"), None),
        P("row", "col"),
        P("col"),
        P(None, "col"),
        P("col"),
        P("col", "row"),
        P(),
    )
    return jax.shard_map(
        body, mesh=mesh, in_specs=placed, out_specs=P(("row", "col"), None), check_vma=False
    )
```

```python
import functools

import jax
import jax.numpy as jnp
from jax import lax
from jax.experimental import pallas as pl
from jax.experimental.pallas import tpu as pltpu
from jax.sharding import PartitionSpec as P

MESH = pl.DeviceIdType.MESH
NX, NY, NZ = 4, 4, 8
D = 3072
BLK = 384
UPPER_IN = 192
UPPER_OUT = 224
CH = NX * BLK
GROUP = 512
OWN = 64
WW = 32
ROWS = GROUP // WW
CHUNKS = ((0, 512), (512, 512), (1024, 256), (1280, 256))
PIECES = 4
PIECE = OWN // PIECES
UNIT = 512
BF16, F32 = jnp.bfloat16, jnp.float32


def place():
    row, col = lax.axis_index("row"), lax.axis_index("col")
    return row // 2, row % 2, col // NZ, col % NZ


def dev(y, c, x, z):
    return {"row": y * 2 + c, "col": x * NZ + z}


def moved_to(y, c, x):
    b = c ^ (y & 1)
    upper = x & 1
    return x >> 1, jnp.where(upper == 0, b, 3 - b)


def moved_from(y, c, x):
    b = (x ^ (x >> 1)) & 1
    return b ^ (y & 1), c * 2 + (x >> 1)


def frame_of(y, c, x):
    b = (x ^ (x >> 1)) & 1
    return 4 * y + 2 * (b ^ (y & 1)) + c


def holder(frame, upper):
    pair = frame >> 1
    y = pair >> 1
    b = (pair & 1) ^ (y & 1)
    return y, frame & 1, jnp.where(upper == 0, b, 3 - b)


class Sender:
    def __init__(self, ssem, rsem):
        self.ssem, self.rsem, self.used, self.sent = ssem, rsem, 0, []

    def key(self):
        self.used += 1
        return self.used - 1

    def make(self, src, dst, k, to):
        return pltpu.make_async_remote_copy(
            src_ref=src,
            dst_ref=dst,
            send_sem=self.ssem.at[k],
            recv_sem=self.rsem.at[k],
            device_id=to,
            device_id_type=MESH,
        )

    def send(self, src, dst, to, when=None):
        k = self.key()
        copy = self.make(src, dst, k, to)
        if when is None:
            copy.start()
        else:
            pl.when(when)(copy.start)
        self.sent.append((copy, when))
        return k

    def arrived(self, ref, k, when=None):
        copy = pltpu.make_async_copy(ref, ref, self.rsem.at[k])
        if when is None:
            copy.wait()
        else:
            pl.when(when)(copy.wait)

    def drain(self):
        for copy, when in self.sent:
            if when is None:
                copy.wait_send()
            else:
                pl.when(when)(copy.wait_send)
        self.sent = []


def greet(peers):
    barrier = pltpu.get_barrier_semaphore()
    count = 0
    for to, when in peers:
        signal = functools.partial(pl.semaphore_signal, barrier, inc=1, device_id=to, device_id_type=MESH)
        if when is None:
            signal()
            count = count + 1
        else:
            pl.when(when)(signal)
            count = count + when.astype(jnp.int32)
    pl.semaphore_wait(barrier, count)


class WeightGather:
    def __init__(self, sender, own, block, band_a, band_b, upper, fine):
        self.fine = fine
        self.s, self.own = sender, own
        self.h, self.qa, self.qb = upper, upper // 2, upper + (BLK - upper) // 2
        self.block, self.band_a, self.band_b = block, band_a, band_b
        self.y, self.c, self.x, self.z = place()
        y, c, x, z = self.y, self.c, self.x, self.z
        self.xs = {"0": x, "+": (x + 1) % NX, "-": (x + NX - 1) % NX, "2": (x + 2) % NX}
        self.ys = {"0": y, "+": (y + 1) % NY, "-": (y + NY - 1) % NY, "2": (y + 2) % NY}
        self.to = {
            "x+": dev(y, c, self.xs["+"], z),
            "x-": dev(y, c, self.xs["-"], z),
            "y+": dev(self.ys["+"], c, x, z),
            "y-": dev(self.ys["-"], c, x, z),
        }
        self.keys, self.from_partner = {}, []

    def at(self, place_, lo, hi):
        return self.block(self.xs[place_[0]], self.ys[place_[1]], pl.ds(lo, hi - lo))

    def push(self, place_, lo, hi, way):
        src = self.at(place_, lo, hi)
        self.keys[place_, lo, hi, way] = self.s.send(src, src, self.to[way])

    def pull(self, here, lo, hi, way, there):
        self.s.arrived(self.at(here, lo, hi), self.keys[there, lo, hi, way])

    def p0(self):
        self.p0x(((0, BLK, ("y+", "y-")),))
        if self.fine:
            other = dev(self.y, 1 - self.c, self.x, self.z)
            here = self.at("00", 0, BLK)
            self.from_partner.append((here, self.s.send(self.own, here, other)))

    def p0x(self, parts=None):
        h = self.h
        for lo, hi, ways in parts or ((0, h, ("x+", "x-")), (h, BLK, ("x+", "x-"))):
            for way in ways:
                src = self.own.at[pl.ds(lo, hi - lo)]
                self.keys["00", lo, hi, way] = self.s.send(src, self.at("00", lo, hi), self.to[way])

    def p1y(self):
        h, qa, qb = self.h, self.qa, self.qb
        self.pull("0-", 0, BLK, "y+", "00")
        self.push("0-", 0, qb, "y+")
        self.push("0-", h, BLK, "x+")
        self.push("0-", h, BLK, "x-")
        self.across("0-", 0, BLK)
        self.pull("0+", 0, BLK, "y-", "00")
        self.push("0+", qb, BLK, "y-")
        self.push("0+", h, BLK, "x+")
        self.push("0+", h, BLK, "x-")
        self.across("0+", 0, BLK)

    def p1x(self):
        h, qa, qb = self.h, self.qa, self.qb
        self.pull("-0", 0, h, "x+", "00")
        self.push("-0", qa, h, "x+")
        self.push("-0", 0, h, "y+")
        self.push("-0", 0, h, "y-")
        self.across("-0", 0, h)
        self.pull("+0", 0, h, "x-", "00")
        self.push("+0", 0, qa, "x-")
        self.push("+0", 0, h, "y+")
        self.push("+0", 0, h, "y-")
        self.across("+0", 0, h)

    def p2y(self):
        h, qa, qb = self.h, self.qa, self.qb
        self.pull("02", 0, qb, "y+", "0-")
        self.pull("02", qb, BLK, "y-", "0+")
        self.push("02", h, BLK, "x-")
        self.push("02", h, BLK, "x+")
        self.across("02", 0, BLK)
        self.pull("--", 0, h, "y+", "-0")
        self.push("--", 0, h, "y+")
        self.across("--", 0, h)
        self.pull("++", 0, h, "y-", "+0")
        self.push("++", 0, h, "y-")
        self.across("++", 0, h)

    def p2x(self):
        h, qa, qb = self.h, self.qa, self.qb
        self.pull("20", qa, h, "x+", "-0")
        self.pull("20", 0, qa, "x-", "+0")
        self.push("20", 0, h, "y-")
        self.push("20", 0, h, "y+")
        self.across("20", 0, h)
        self.pull("-0", h, BLK, "x+", "00")
        self.push("-0", h, BLK, "x+")
        self.across("-0", h, BLK)
        self.pull("+0", h, BLK, "x-", "00")
        self.across("+0", h, BLK)
        self.pull("--", h, BLK, "x+", "0-")
        self.push("--", h, BLK, "x+")
        self.across("--", h, BLK)
        self.pull("++", h, BLK, "x-", "0+")
        self.push("++", h, BLK, "x-")
        self.across("++", h, BLK)
        self.partner("0", "0")

    def p3(self):
        h = self.h
        self.pull("2+", 0, h, "y-", "20")
        self.push("2+", 0, h, "y-")
        self.across("2+", 0, h)
        self.pull("+2", h, BLK, "x-", "02")
        self.push("+2", h, BLK, "x-")
        self.across("+2", h, BLK)
        for here, lo, hi, way, there in (
            ("+-", 0, h, "y+", "+0"),
            ("-+", 0, h, "y-", "-0"),
            ("-+", h, BLK, "x+", "0+"),
            ("+-", h, BLK, "x-", "0-"),
            ("2-", 0, h, "y+", "20"),
            ("-2", h, BLK, "x+", "02"),
        ):
            self.pull(here, lo, hi, way, there)
            self.across(here, lo, hi)
        self.partner("-", "-")
        self.partner("+", "+")

    def p4(self):
        h = self.h
        for here, lo, hi, way, there in (
            ("20", h, BLK, "x+", "-0"),
            ("-2", 0, h, "y+", "--"),
            ("2-", h, BLK, "x+", "--"),
            ("+2", 0, h, "y-", "++"),
            ("2+", h, BLK, "x-", "++"),
            ("22", 0, h, "y-", "2+"),
            ("22", h, BLK, "x-", "+2"),
        ):
            self.pull(here, lo, hi, way, there)
            self.across(here, lo, hi)
        self.partner("2", "2")

    def across(self, here, lo, hi):
        if not self.fine:
            return
        other = dev(self.y, 1 - self.c, self.x, self.z)
        ref = self.at(here, lo, hi)
        self.from_partner.append((ref, self.s.send(ref, ref, other)))

    def partner(self, x, y):
        if self.fine:
            return
        other = dev(self.y, 1 - self.c, self.x, self.z)
        a, b = self.band_a(self.ys[y]), self.band_b(self.xs[x])
        self.from_partner.append((a, self.s.send(a, a, other)))
        self.from_partner.append((b, self.s.send(b, b, other)))

    def finish(self):
        for ref, k in self.from_partner:
            self.s.arrived(ref, k)


class SkewGather(WeightGather):
    def __init__(self, *rest):
        super().__init__(*rest)
        y, c, x, z = self.y, self.c, self.x, self.z
        to_next = ((x ^ (x >> 1)) ^ y) & 1
        even = 1 - (x & 1)
        step_x, step_y = 2 * even - 1, 2 * to_next - 1
        self.xs["L"], self.xs["U"] = (x + NX + step_x) % NX, (x + NX - step_x) % NX
        self.ys["L"], self.ys["U"] = (y + NY + step_y) % NY, (y + NY - step_y) % NY
        self.to = {
            "xL": dev(y, c, self.xs["L"], z),
            "xU": dev(y, c, self.xs["U"], z),
            "yL": dev(self.ys["L"], c, x, z),
            "yU": dev(self.ys["U"], c, x, z),
        }

    def p0(self):
        for way in ("yL", "yU", "xL", "xU"):
            self.keys["00", 0, BLK, way] = self.s.send(self.own, self.at("00", 0, BLK), self.to[way])

    def p1y(self):
        h = self.h
        self.pull("0L", 0, BLK, "yL", "00")
        self.push("0L", 0, BLK, "yU")
        self.pull("0U", 0, BLK, "yU", "00")
        for block in ("0+", "0-"):
            self.push(block, h, BLK, "xL")
            self.push(block, h, BLK, "xU")

    def p1x(self):
        h = self.h
        self.pull("L0", 0, BLK, "xL", "00")
        self.push("L0", 0, BLK, "xU")
        self.push("L0", 0, h, "yL")
        self.push("L0", 0, h, "yU")
        self.pull("U0", 0, BLK, "xU", "00")
        self.push("U0", 0, h, "yL")
        self.push("U0", 0, h, "yU")

    def p2y(self):
        h = self.h
        self.pull("02", 0, BLK, "yU", "0L")
        self.push("02", h, BLK, "xL")
        self.push("02", h, BLK, "xU")
        self.pull("LL", 0, h, "yL", "L0")
        self.push("LL", 0, h, "yU")
        self.pull("UL", 0, h, "yL", "U0")
        self.push("UL", 0, h, "yU")

    def p2x(self):
        h = self.h
        self.pull("20", 0, BLK, "xU", "L0")
        self.push("20", 0, h, "yL")
        self.push("20", 0, h, "yU")
        self.pull("L+", h, BLK, "xL", "0+")
        self.push("L+", h, BLK, "xU")
        self.pull("L-", h, BLK, "xL", "0-")
        self.push("L-", h, BLK, "xU")
        self.partner("0", "0")

    def p3(self):
        h = self.h
        self.pull("2L", 0, h, "yL", "20")
        self.push("2L", 0, h, "yU")
        self.pull("L2", h, BLK, "xL", "02")
        self.push("L2", h, BLK, "xU")
        self.pull("LU", 0, h, "yU", "L0")
        self.pull("UU", 0, h, "yU", "U0")
        self.pull("2U", 0, h, "yU", "20")
        self.pull("U+", h, BLK, "xU", "0+")
        self.pull("U-", h, BLK, "xU", "0-")
        self.pull("U2", h, BLK, "xU", "02")
        self.partner("L", "L")
        self.partner("U", "U")

    def p4(self):
        h = self.h
        self.pull("L2", 0, h, "yU", "LL")
        self.pull("2+", h, BLK, "xU", "L+")
        self.pull("U2", 0, h, "yU", "UL")
        self.pull("2-", h, BLK, "xU", "L-")
        self.pull("22", 0, h, "yU", "2L")
        self.pull("22", h, BLK, "xU", "L2")
        self.partner("2", "2")


def block_kernel(
    tok_in, win_in, bin_in, taps_in, cbias_in, wout_in, bout_in, out,
    tok, win, wout, ext, act, part, own_par, par, tp, b1, cb1, bout, sendbuf, recvbuf, summed, moved, done, relay,
    lsem, ssem, rsem,
):
    y, c, x, z = place()
    s = Sender(ssem, rsem)
    xs = [(x + d) % NX for d in range(NX)]
    zp, zm = (z + 1) % NZ, (z + NZ - 1) % NZ
    yp, ym = (y + 1) % NY, (y + NY - 1) % NY
    upper = x >> 1
    frame = frame_of(y, c, x)
    last = NY * 4 - 1
    tc, tx = moved_to(y, c, x)
    fc, fx = moved_from(y, c, x)
    stays = (tc == c) & (tx == x)
    moves = jnp.logical_not(stays)
    far = ((x == 1) | (x == 2)) & (c == (y & 1))
    near = jnp.logical_and(moves, jnp.logical_not(far))
    between = ((x == 0) & (c == 0)) | ((x == NX - 1) & (c == 1))
    has_next, has_prev = frame < last, frame > 0
    ny, nc, nx = holder(jnp.minimum(frame + 1, last), upper)
    py, pc, px = holder(jnp.maximum(frame - 1, 0), upper)
    nxt, nxt_other = dev(ny, nc, nx, z), dev(ny, nc, 3 - nx, z)
    prv, prv_other = dev(py, pc, px, z), dev(py, pc, 3 - px, z)
    other_half = dev(y, c, 3 - x, z)

    locals_ = [
        pltpu.make_async_copy(taps_in, tp, lsem.at[0]),
        pltpu.make_async_copy(bin_in, b1, lsem.at[1]),
        pltpu.make_async_copy(cbias_in, cb1, lsem.at[2]),
    ]
    own_bout = pltpu.make_async_copy(bout_in, bout, lsem.at[3])
    for copy in locals_ + [own_bout]:
        copy.start()

    def win_block(x_, y_, rows):
        return win.at[y_, c, rows, pl.ds(x_ * BLK, BLK)]

    def win_a(y_):
        return win.at[y_, c, pl.ds(0, UPPER_IN), :]

    def win_b(x_):
        return win.at[:, c, pl.ds(UPPER_IN, BLK - UPPER_IN), pl.ds(x_ * BLK, BLK)]

    g_in = WeightGather(s, win_in, win_block, win_a, win_b, UPPER_IN, True)
    own_in = pltpu.make_async_copy(win_in, win_block(x, y, pl.ds(0, BLK)), lsem.at[4])
    own_in.start()

    def out_gather(q):
        w = BLK // 3
        n = NY * w

        def block(x_, y_, rows):
            return wout.at[q, x_, rows, pl.ds(c * n + y_ * w, w)]

        def band_a(y_):
            return wout.at[q, :, pl.ds(0, UPPER_OUT), pl.ds(c * n + y_ * w, w)]

        def band_b(x_):
            return wout.at[q, x_, pl.ds(UPPER_OUT, BLK - UPPER_OUT), pl.ds(c * n, n)]

        own = wout_in.at[:, pl.ds(q * w, w)]
        copy = pltpu.make_async_copy(own, block(x, y, pl.ds(0, BLK)), lsem.at[5 + q])
        copy.start()
        return SkewGather(s, own, block, band_a, band_b, UPPER_OUT, False), copy

    (g0, own0), (g1, own1), (g2, own2) = [out_gather(q) for q in range(3)]

    greet(
        [(dev(y, c, xs[d], z), None) for d in (1, 2, 3)]
        + [(dev(yp, c, x, z), None), (dev(ym, c, x, z), None)]
        + [(dev(y, c, x, zp), None), (dev(y, c, x, zm), None)]
        + [(dev(y, 1 - c, x, z), None)]
        + [(dev(y, tc, tx, z), moves), (dev(y, fc, fx, z), moves)]
        + [(nxt, has_next), (nxt_other, has_next), (prv, has_prev), (prv_other, has_prev)]
        + [(other_half, None)]
        + [(dev(y, tc, jnp.where(x == 1, 0, NX - 1), z), far)]
        + [(dev(y, y & 1, jnp.where(x == 0, 1, 2), z), between)]
    )

    def tok_at(z_, p):
        return tok.at[pl.ds(((z_ + NZ) % NZ) * OWN + p * PIECE, PIECE)]

    home, relays = [], []
    for p in range(PIECES):
        src = tok_in.at[pl.ds(p * PIECE, PIECE)]
        stop = relay.at[pl.ds(p * PIECE, PIECE)]
        k = s.send(src, tok_at(z, p), dev(y, tc, tx, z), when=near)
        k_stop = s.send(src, stop, dev(y, tc, jnp.where(x == 1, 0, NX - 1), z), when=far)
        relays.append((stop, k_stop, k))
        stay = pltpu.make_async_copy(src, tok_at(z, p), rsem.at[k])
        pl.when(stays)(stay.start)
        home.append(stay)
    g_in.p0()

    @pl.when(upper == 0)
    def _():
        ext[:, 0] = jnp.zeros((3, WW, CH), BF16)

    @pl.when(upper == 1)
    def _():
        ext[:, ROWS + 1] = jnp.zeros((3, WW, CH), BF16)

    @pl.when(jnp.logical_not(has_prev))
    def _():
        @pl.loop(0, ROWS + 2)
        def _(r):
            ext[0, r] = jnp.zeros((WW, CH), BF16)

    @pl.when(jnp.logical_not(has_next))
    def _():
        @pl.loop(0, ROWS + 2)
        def _(r):
            ext[2, r] = jnp.zeros((WW, CH), BF16)

    k_tok = {}

    def pass_relay(p):
        stop, k_stop, k = relays[p]
        s.arrived(stop, k_stop, between)
        onward = pltpu.make_async_remote_copy(
            src_ref=stop,
            dst_ref=tok_at(z, p),
            send_sem=s.ssem.at[s.key()],
            recv_sem=s.rsem.at[k],
            device_id=other_half,
            device_id_type=MESH,
        )
        pl.when(between)(onward.start)
        s.sent.append((onward, between))

    def token_step(d, first=0, last=PIECES):
        for p in range(first, last):
            if d == 1:
                if p > 0:
                    pass_relay(p - 1)
                home[p].wait()
            for way, to in ((1, zp), (-1, zm)):
                if d == 4 and (p < PIECES // 2) != (way == 1):
                    continue
                src = tok_at(z - way * (d - 1), p)
                if d > 1:
                    s.arrived(src, k_tok[way, d - 1, p])
                k_tok[way, d, p] = s.send(src, src, dev(y, c, x, to))

    def par_at(x_):
        return par.at[:, pl.ds(x_ * BLK, BLK)]

    token_step(1)
    pass_relay(PIECES - 1)
    g_in.p0x()
    g_in.p1y()
    token_step(2, 0, 2)
    g_in.p1x()
    token_step(2, 2)
    own_in.wait()
    token_step(3, 0, 1)
    g_in.p2y()
    token_step(3, 1)
    g_in.p2x()
    token_step(4, 0, 2)
    g_in.p3()
    for copy in locals_:
        copy.wait()
    own_par[0:27, :] = tp[...]
    own_par[27:28, :] = b1[...].reshape(1, BLK)
    own_par[28:29, :] = cb1[...].reshape(1, BLK)
    k_par = [s.send(own_par, par_at(x), dev(y, c, xs[d], z)) for d in (1, 2, 3)]
    own_copy = pltpu.make_async_copy(own_par, par_at(x), lsem.at[8])
    own_copy.start()
    own0.wait()
    own1.wait()
    own2.wait()
    g0.p0()
    g1.p0()
    g2.p0()
    token_step(4, 2)
    g_in.p4()
    own_copy.wait()
    for d in (1, 2, 3):
        s.arrived(par_at((x + NX - d) % NX), k_par[d - 1])
    for p in range(PIECES):
        way = -1 if p < PIECES // 2 else 1
        s.arrived(tok_at(z - way * 3, p), k_tok[way, 3, p])
        s.arrived(tok_at(z + 4, p), k_tok[-way, 4, p])
    g0.p1y()
    g0.p1x()
    g_in.finish()

    src_row = jnp.where(upper == 0, ROWS, 1)
    dst_row = jnp.where(upper == 0, 0, ROWS + 1)
    got_row = jnp.where(upper == 0, ROWS + 1, 0)
    inner = pl.ds(1, ROWS)
    arrivals = []
    step = 256
    for j, (first, many) in enumerate(CHUNKS):

        @pl.loop(0, many // step)
        def _(i):
            cols = pl.ds(pl.multiple_of(first + i * step, step), step)
            w = win[:, :, :, cols].reshape(D, step)
            before = jnp.dot(tok[...], w, preferred_element_type=F32) + par[27:28, cols]
            ext[1, inner, :, cols] = before.astype(BF16).reshape(ROWS, WW, step)

        cols = pl.ds(first, many)
        frame_src = ext.at[1, inner, :, cols]
        row_src = ext.at[1, src_row, :, cols]
        k1 = s.send(frame_src, ext.at[0, inner, :, cols], nxt, when=has_next)
        k2 = s.send(frame_src, ext.at[2, inner, :, cols], prv, when=has_prev)
        k3 = s.send(row_src, ext.at[1, dst_row, :, cols], other_half)
        k4 = s.send(row_src, ext.at[0, dst_row, :, cols], nxt_other, when=has_next)
        k5 = s.send(row_src, ext.at[2, dst_row, :, cols], prv_other, when=has_prev)
        arrivals.append([
            (ext.at[0, inner, :, cols], k1, has_prev),
            (ext.at[2, inner, :, cols], k2, has_next),
            (ext.at[1, got_row, :, cols], k3, None),
            (ext.at[0, got_row, :, cols], k4, has_prev),
            (ext.at[2, got_row, :, cols], k5, has_next),
        ])
        if j == 0:
            g0.p2y()
            g0.p2x()

    column = lax.broadcasted_iota(jnp.int32, (WW, 128), 0)

    def conv(j):
        first, many = CHUNKS[j]
        for copy in arrivals[j]:
            s.arrived(*copy)

        @pl.loop(0, many // 128)
        def _(i):
            lanes = pl.ds(pl.multiple_of(first + i * 128, 128), 128)

            @pl.loop(0, ROWS, step=2)
            def _(r):
                sums = [[None] * 3 for _ in range(2)]
                for dt in range(3):
                    for dr in range(2 + 2):
                        v = ext[dt, r + dr, :, lanes].astype(F32)
                        for row in range(2):
                            dh = dr - row
                            if not 0 <= dh < 3:
                                continue
                            for dw in range(3):
                                k = 9 * dt + 3 * dh + dw
                                t = v * par[k : k + 1, lanes]
                                old = sums[row][dw]
                                sums[row][dw] = t if old is None else old + t
                for row in range(2):
                    left = jnp.where(column == 0, 0.0, pltpu.roll(sums[row][0], 1, 0))
                    right = jnp.where(column == WW - 1, 0.0, pltpu.roll(sums[row][2], WW - 1, 0))
                    v = sums[row][1] + left + right + par[28:29, lanes]
                    half = 0.5 * v
                    t = jnp.tanh(v * (0.7978845608028654 + 0.035677408136300125 * (v * v)))
                    to = pl.ds(pl.multiple_of((r + row) * WW, WW), WW)
                    act[to, lanes] = (half + half * t).astype(BF16)

    conv(0)
    g0.p3()
    g1.p1y()
    g1.p1x()
    conv(1)
    g0.p4()
    g2.p1y()
    g2.p1x()
    conv(2)
    g1.p2y()
    g1.p2x()
    conv(3)
    g0.finish()

    units = D // UNIT
    chains = [
        (u, way, 4 if (u % 2 == 0) == (way == 1) else 3) for u in range(units) for way in (1, -1)
    ]
    slot, n = {}, 0
    for i, (u, way, length) in enumerate(chains):
        for st in range(length):
            slot[i, st] = n
            n += 1
    k_of = {}

    def multiply(u):
        @pl.loop(0, UNIT // 256)
        def _(i):
            at = pl.multiple_of(i * 256, 256)
            w = wout[u // 2, :, :, pl.ds(u % 2 * UNIT + at, 256)].reshape(CH, 256)
            part[u, :, pl.ds(at, 256)] = jnp.dot(act[...], w, preferred_element_type=F32)

    def pass_on(u, st):
        for i, (u_, way, length) in enumerate(chains):
            if u_ != u or st >= length:
                continue
            at = (z + way * (length - st) + NZ) % NZ
            rows = pl.ds(pl.multiple_of(at * OWN, OWN), OWN)
            value = part[u, rows, :]
            if st > 0:
                got = recvbuf.at[slot[i, st - 1]]
                s.arrived(got, k_of[i, st - 1])
                value = value + got[...].astype(F32)
            mine = slot[i, st]
            sendbuf[mine] = value.astype(BF16)
            to = dev(y, c, x, zp if way == 1 else zm)
            k_of[i, st] = s.send(sendbuf.at[mine], recvbuf.at[mine], to)

    back = []

    w = BLK // 3

    def collect(u):
        rows = pl.ds(pl.multiple_of(z * OWN, OWN), OWN)
        value = part[u, rows, :]
        for i in (2 * u, 2 * u + 1):
            mine = slot[i, chains[i][2] - 1]
            s.arrived(recvbuf.at[mine], k_of[i, chains[i][2] - 1])
            value = value + recvbuf[mine].astype(F32)
        for n_ in range(NY):
            lo = (n_ * 2 + u % 2) * BLK + u // 2 * w
            summed[u, :, n_ * w : (n_ + 1) * w] = (
                value[:, n_ * w : (n_ + 1) * w] + bout[lo : lo + w].reshape(1, w)
            ).astype(BF16)
        k = s.send(summed.at[u], moved.at[u], dev(y, fc, fx, z), when=moves)
        stay = pltpu.make_async_copy(summed.at[u], moved.at[u], rsem.at[k])
        pl.when(stays)(stay.start)
        back.append(stay)

    def put(u):
        back[u].wait()
        for n_ in range(NY):
            lo = (n_ * 2 + u % 2) * BLK + u // 2 * w
            done[:, lo : lo + w] = moved[u, :, n_ * w : (n_ + 1) * w]

    def hop(q, st):
        pass_on(2 * q, st)
        pass_on(2 * q + 1, st)

    own_bout.wait()
    multiply(0)
    pass_on(0, 0)
    multiply(1)
    pass_on(1, 0)
    g1.p3()
    g2.p2y()
    g2.p2x()
    g1.p4()
    hop(0, 1)
    g1.finish()
    multiply(2)
    pass_on(2, 0)
    multiply(3)
    pass_on(3, 0)
    g2.p3()
    hop(0, 2)
    g2.p4()
    hop(1, 1)
    g2.finish()
    multiply(4)
    pass_on(4, 0)
    multiply(5)
    pass_on(5, 0)
    hop(0, 3)
    hop(2, 1)
    hop(1, 2)
    collect(0)
    collect(1)
    hop(2, 2)
    hop(1, 3)
    put(0)
    put(1)
    hop(2, 3)
    collect(2)
    collect(3)
    collect(4)
    collect(5)
    put(2)
    put(3)
    put(4)
    put(5)
    stored = pltpu.make_async_copy(done, out, lsem.at[9])
    stored.start()
    stored.wait()
    s.drain()


def body(tokens, w_in, b_in, conv_taps, conv_bias, w_out, b_out):
    keys = 300
    hbm = pl.BlockSpec(memory_space=pl.ANY)
    return pl.pallas_call(
        block_kernel,
        out_shape=jax.ShapeDtypeStruct((OWN, D), BF16),
        in_specs=[hbm] * 7,
        out_specs=hbm,
        scratch_shapes=[
            pltpu.VMEM((GROUP, D), BF16),
            pltpu.VMEM((NY, 2, BLK, CH), BF16),
            pltpu.VMEM((3, NX, BLK, 2 * UNIT), BF16),
            pltpu.VMEM((3, ROWS + 2, WW, CH), BF16),
            pltpu.VMEM((GROUP, CH), BF16),
            pltpu.VMEM((6, GROUP, UNIT), F32),
            pltpu.VMEM((32, BLK), F32),
            pltpu.VMEM((32, CH), F32),
            pltpu.VMEM((27, BLK), F32),
            pltpu.VMEM((BLK,), F32),
            pltpu.VMEM((BLK,), F32),
            pltpu.VMEM((D,), F32),
            pltpu.VMEM((42, OWN, UNIT), BF16),
            pltpu.VMEM((42, OWN, UNIT), BF16),
            pltpu.VMEM((6, OWN, UNIT), BF16),
            pltpu.VMEM((6, OWN, UNIT), BF16),
            pltpu.VMEM((OWN, D), BF16),
            pltpu.VMEM((OWN, D), BF16),
            pltpu.SemaphoreType.DMA((10,)),
            pltpu.SemaphoreType.DMA((keys,)),
            pltpu.SemaphoreType.DMA((keys,)),
        ],
        compiler_params=pltpu.CompilerParams(
            collective_id=0, has_side_effects=True, vmem_limit_bytes=60 * 2**20
        ),
        name="mix_ffn",
    )(tokens, w_in, b_in, conv_taps, conv_bias, w_out, b_out)


def solution(mesh):
    placed = (
        P(("row", "col"), None),
        P("row", "col"),
        P("col"),
        P(None, "col"),
        P("col"),
        P("col", "row"),
        P(),
    )
    return jax.shard_map(
        body, mesh=mesh, in_specs=placed, out_specs=P(("row", "col"), None), check_vma=False
    )
```
